128 devices in a mesh: gx: 8 (over z, x_hi), gy: 8 (over y, core), gz: 2 (over x_lo).
Axes of the slice: x: 4 (x_hi: 2, x_lo: 2; x = x_hi * 2 + x_lo), y: 4, z: 4, core: 2. Of those that a mesh axis runs over, the one named last changes fastest.
Arguments:
- volume: bfloat16 [64, 128, 32, 128], P('gx', 'gy', 'gz'), may hold values from -6 to 6
- w_full: bfloat16 [3, 3, 3, 128, 128], replicated, may hold values from -0.15625 to 0.15625
- w_half: bfloat16 [3, 3, 3, 128, 256], replicated, may hold values from -0.15625 to 0.15625
- w_bottom_in: bfloat16 [3, 3, 3, 256, 512], P(None, None, None, None, 'gx'), may hold values from -0.109375 to 0.109375
- w_bottom_out: bfloat16 [3, 3, 3, 512, 512], P(None, None, None, None, 'gx'), may hold values from -0.078125 to 0.078125
- w_up: bfloat16 [3, 3, 3, 768, 256], replicated, may hold values from -0.0625 to 0.0625
Outputs:
- decoded: bfloat16 [32, 64, 16, 256], P('gx', 'gy', 'gz')
The draws below stay inside these ranges and needn't reach their ends.
All inputs are finite; a program needn't handle non-finite values.
Results may differ from the reference program's by a relative error of at most 0.009.
Values may be sent and summed in bfloat16 or wider, within the bound.
No kernel may reach another device: no remote copies, remote signals or barrier semaphores. Data moves between devices by JAX's collectives and lax.ppermute only.
A program may use at most 64 MiB of HBM per device.

```python
import jax
import jax.numpy as jnp
from jax import lax

C0 = 128
C1 = 256
C2 = 512
NX = 64
NY = 128
NZ = 32


def block_levels(own_key, shape, cuts, least, top_value):
    def one(dim, blocks):
        draws = jax.random.uniform(jax.random.fold_in(jax.random.fold_in(own_key, 6), dim), (blocks,), jnp.float32, least / len(cuts), top_value / len(cuts))
        return jnp.repeat(jnp.exp(draws), shape[dim] // blocks).reshape((-1,) + (1,) * (len(shape) - dim - 1))

    gain = one(*cuts[0])
    for cut in cuts[1:]:
        gain = gain * one(*cut)
    return gain


def normal_values(own_key, dims, scale, reach, cuts=(), held_as=jnp.bfloat16):
    array = scale * jax.random.normal(own_key, dims, jnp.float32)
    if cuts:
        array = array * block_levels(own_key, dims, cuts, -0.22, 0.18)
    return jnp.clip(array, -reach, reach).astype(held_as)


def setup_inputs(seed: int = 0) -> dict:
    keys = jax.random.split(jax.random.key(seed), 7)
    return {
        "volume": normal_values(keys[0], (NX, NY, NZ, C0), 1.0, 6.0, ((0, 8), (1, 8), (2, 2))),
        "w_full": normal_values(keys[1], (3, 3, 3, C0, C0), (27 * C0 // 2) ** -0.5, 0.15625),
        "w_half": normal_values(keys[2], (3, 3, 3, C0, C1), (27 * C0 // 2) ** -0.5, 0.15625),
        "w_bottom_in": normal_values(keys[3], (3, 3, 3, C1, C2), (27 * C1 // 2) ** -0.5, 0.109375, ((4, 8),)),
        "w_bottom_out": normal_values(keys[4], (3, 3, 3, C2, C2), (27 * C2 // 2) ** -0.5, 0.078125, ((4, 8),)),
        "w_up": normal_values(keys[5], (3, 3, 3, C2 + C1, C1), (27 * (C2 + C1) // 2) ** -0.5, 0.0625),
    }


def convolve(field, kernel):
    result = lax.conv_general_dilated(field[None], kernel, (1, 1, 1), "SAME", dimension_numbers=("NDHWC", "DHWIO", "NDHWC"), preferred_element_type=jnp.float32)
    return result[0]


def rectify(total):
    return jnp.maximum(total, 0.0).astype(jnp.bfloat16)


def shrink(field):
    size_x, size_y, size_z, channels = field.shape
    blocks = field.reshape(size_x // 2, 2, size_y // 2, 2, size_z // 2, 2, channels)
    return jnp.max(blocks, axis=(1, 3, 5))


def enlarge(field):
    size_x, size_y, size_z, channels = field.shape
    spread = jnp.broadcast_to(field[:, None, :, None, :, None, :], (size_x, 2, size_y, 2, size_z, 2, channels))
    return spread.reshape(2 * size_x, 2 * size_y, 2 * size_z, channels)


def reference(volume, w_full, w_half, w_bottom_in, w_bottom_out, w_up):
    full_level = rectify(convolve(volume, w_full))
    pooled = shrink(full_level)
    skip_level = rectify(convolve(pooled, w_half))
    coarse = shrink(skip_level)
    bottom_first = rectify(convolve(coarse, w_bottom_in))
    bottom_second = rectify(convolve(bottom_first, w_bottom_out))
    joined = jnp.concatenate([enlarge(bottom_second), skip_level], axis=3)
    return convolve(joined, w_up).astype(jnp.bfloat16)
```

```python
import jax
import jax.numpy as jnp
from jax import lax
from jax.sharding import PartitionSpec as P


def conv(field, kernel):
    result = lax.conv_general_dilated(
        field[None],
        kernel,
        (1, 1, 1),
        "VALID",
        dimension_numbers=("NDHWC", "DHWIO", "NDHWC"),
        preferred_element_type=jnp.float32,
    )
    return result[0]


def rectify(total):
    return jnp.maximum(total, 0.0).astype(jnp.bfloat16)


def shrink(field):
    size_x, size_y, size_z, channels = field.shape
    blocks = field.reshape(size_x // 2, 2, size_y // 2, 2, size_z // 2, 2, channels)
    return jnp.max(blocks, axis=(1, 3, 5))


def enlarge(field):
    size_x, size_y, size_z, channels = field.shape
    spread = jnp.broadcast_to(
        field[:, None, :, None, :, None, :], (size_x, 2, size_y, 2, size_z, 2, channels)
    )
    return spread.reshape(2 * size_x, 2 * size_y, 2 * size_z, channels)


def halo(field, axis, count, dim, width):
    place = lax.axis_index(axis)
    size = field.shape[dim]
    low = lax.slice_in_dim(field, 0, width, axis=dim)
    high = lax.slice_in_dim(field, size - width, size, axis=dim)
    zero = jnp.zeros_like(low)
    if count == 2:
        got = lax.ppermute(jnp.where(place == 0, high, low), axis, [(0, 1), (1, 0)])
        below = jnp.where(place == 1, got, zero)
        above = jnp.where(place == 0, got, zero)
        return below, above
    even = place % 2 == 0
    inner = [(i, i ^ 1) for i in range(count)]
    outer = [(i, (((i + 1) ^ 1) - 1) % count) for i in range(count)]
    got_in = lax.ppermute(jnp.where(even, high, low), axis, inner)
    got_out = lax.ppermute(jnp.where(even, low, high), axis, outer)
    below = jnp.where(place > 0, jnp.where(even, got_out, got_in), zero)
    above = jnp.where(place < count - 1, jnp.where(even, got_in, got_out), zero)
    return below, above


def extend(field, axis, count, dim, width):
    below, above = halo(field, axis, count, dim, width)
    return jnp.concatenate([below, field, above], axis=dim)


def clear_outside(field, axis, count, dim, width):
    place = lax.axis_index(axis)
    size = field.shape[dim]
    index = lax.broadcasted_iota(jnp.int32, field.shape, dim)
    inside = ((index >= width) | (place > 0)) & ((index < size - width) | (place < count - 1))
    return jnp.where(inside, field, jnp.zeros_like(field))


def solution(mesh):
    gx, gy, gz = mesh.shape["gx"], mesh.shape["gy"], mesh.shape["gz"]

    def local(volume, w_full, w_half, w_bottom_in, w_bottom_out, w_up):
        place_z = lax.axis_index("gz")
        field = extend(volume, "gx", gx, 0, 3)
        field = extend(field, "gy", gy, 1, 3)
        field = extend(field, "gz", gz, 2, 1)
        pooled = shrink(rectify(conv(field, w_full)))
        pooled = clear_outside(pooled, "gx", gx, 0, 1)
        pooled = clear_outside(pooled, "gy", gy, 1, 1)
        pooled = extend(pooled, "gz", gz, 2, 1)
        skip = rectify(conv(pooled, w_half))
        coarse = shrink(skip)
        own_x, own_y, own_z, ch1 = coarse.shape

        column = extend(coarse, "gy", gy, 1, 1)
        column = jnp.broadcast_to(column[None], (gx * gz,) + column.shape)
        column = lax.all_to_all(column, ("gx", "gz"), 0, 0)
        column = column.reshape(gx, gz, own_x, own_y + 2, own_z, ch1)
        column = column.transpose(0, 2, 3, 1, 4, 5).reshape(gx * own_x, own_y + 2, gz * own_z, ch1)
        first = rectify(conv(jnp.pad(column, ((1, 1), (0, 0), (1, 1), (0, 0))), w_bottom_in))

        part = first.shape[-1]
        first = jnp.broadcast_to(first[None], (gx,) + first.shape)
        first = lax.all_to_all(first, "gx", 0, 0)
        first = first.transpose(1, 2, 3, 0, 4).reshape(first.shape[1:4] + (gx * part,))
        first = extend(first, "gy", gy, 1, 2)
        first = jnp.pad(first, ((1, 1), (0, 0), (1, 1), (0, 0)))
        second = rectify(conv(first, w_bottom_out))
        second = clear_outside(second, "gy", gy, 1, 1)
        second = jnp.pad(second, ((1, 1), (0, 0), (1, 1), (0, 0)))
        second = lax.dynamic_slice_in_dim(second, place_z * own_z, own_z + 2, axis=2)
        second = jnp.stack([second[own_x * i : own_x * i + own_x + 2] for i in range(gx)])
        second = lax.all_to_all(second, "gx", 0, 0)
        second = second.transpose(1, 2, 3, 0, 4).reshape(second.shape[1:4] + (gx * part,))

        around = extend(skip, "gx", gx, 0, 1)
        around = extend(around, "gy", gy, 1, 1)
        around = extend(around, "gz", gz, 2, 1)
        spread = enlarge(second)[1:-1, 1:-1, 1:-1]
        joined = jnp.concatenate([spread, around], axis=3)
        return conv(joined, w_up).astype(jnp.bfloat16)

    space = P("gx", "gy", "gz", None)
    filters = P(None, None, None, None, "gx")
    return jax.shard_map(
        local,
        mesh=mesh,
        in_specs=(space, P(), P(), filters, filters, P()),
        out_specs=space,
        check_vma=False,
    )
```

```python
import jax
import jax.numpy as jnp
from jax import lax
from jax.experimental import pallas as pl
from jax.experimental.pallas import tpu as pltpu
from jax.sharding import PartitionSpec as P


def conv(field, kernel):
    result = lax.conv_general_dilated(
        field[None],
        kernel,
        (1, 1, 1),
        "VALID",
        dimension_numbers=("NDHWC", "DHWIO", "NDHWC"),
        preferred_element_type=jnp.float32,
    )
    return result[0]


def rectify(total):
    return jnp.maximum(total, 0.0).astype(jnp.bfloat16)


def shrink(field):
    size_x, size_y, size_z, channels = field.shape
    blocks = field.reshape(size_x // 2, 2, size_y // 2, 2, size_z // 2, 2, channels)
    return jnp.max(blocks, axis=(1, 3, 5))


def enlarge(field):
    size_x, size_y, size_z, channels = field.shape
    spread = jnp.broadcast_to(
        field[:, None, :, None, :, None, :], (size_x, 2, size_y, 2, size_z, 2, channels)
    )
    return spread.reshape(2 * size_x, 2 * size_y, 2 * size_z, channels)


def halo(field, axis, count, dim, width):
    place = lax.axis_index(axis)
    size = field.shape[dim]
    low = lax.slice_in_dim(field, 0, width, axis=dim)
    high = lax.slice_in_dim(field, size - width, size, axis=dim)
    zero = jnp.zeros_like(low)
    if count == 2:
        got = lax.ppermute(jnp.where(place == 0, high, low), axis, [(0, 1), (1, 0)])
        below = jnp.where(place == 1, got, zero)
        above = jnp.where(place == 0, got, zero)
        return below, above
    even = place % 2 == 0
    inner = [(i, i ^ 1) for i in range(count)]
    outer = [(i, (((i + 1) ^ 1) - 1) % count) for i in range(count)]
    got_in = lax.ppermute(jnp.where(even, high, low), axis, inner)
    got_out = lax.ppermute(jnp.where(even, low, high), axis, outer)
    below = jnp.where(place > 0, jnp.where(even, got_out, got_in), zero)
    above = jnp.where(place < count - 1, jnp.where(even, got_in, got_out), zero)
    return below, above


def extend(field, axis, count, dim, width):
    below, above = halo(field, axis, count, dim, width)
    return jnp.concatenate([below, field, above], axis=dim)


def clear_outside(field, axis, count, dim, width):
    place = lax.axis_index(axis)
    size = field.shape[dim]
    index = lax.broadcasted_iota(jnp.int32, field.shape, dim)
    inside = ((index >= width) | (place > 0)) & ((index < size - width) | (place < count - 1))
    return jnp.where(inside, field, jnp.zeros_like(field))


def roll_rows(block, shift):
    return pltpu.roll(block, shift % block.shape[1], 1)


def tile_conv(field, weights, name):
    size_a, size_b, size_s, channels = field.shape
    size_a, size_b = size_a - 2, size_b - 2
    steps, taps, _, width = weights.shape
    filters = width if taps == 3 else 64
    wide = width if taps == 3 else 128
    part = max(1, 256 // (size_b * size_s))

    def body(field_ref, weights_ref, out_ref):
        for first in range(0, size_a, part):
            rows = part * size_b * size_s
            groups = part * size_b
            blocks = []
            for step in range(steps):
                da, db = step // 3, step % 3
                block = field_ref[first + da : first + da + part, db : db + size_b]
                if size_s % 16:
                    block = block.astype(jnp.float32)
                blocks.append(block.reshape(rows, channels).astype(jnp.bfloat16))
            block = jnp.concatenate(blocks, axis=1)
            sums = []
            for tap in range(taps):
                kernel = weights_ref[:, tap].reshape(steps * channels, width)
                sums.append(jnp.dot(block, kernel, preferred_element_type=jnp.float32))
            if taps == 3:
                low, mid, high = [total.reshape(groups, size_s, width) for total in sums]
            else:
                low = sums[0][:, :128].reshape(groups, size_s, 128)
                mid = pltpu.roll(sums[0][:, :128], 64, 1).reshape(groups, size_s, 128)
                high = sums[0][:, 128:].reshape(groups, size_s, 128)
            if size_s == 8:
                total = roll_rows(low, 1) + mid + roll_rows(high, -1)
            else:
                index = lax.broadcasted_iota(jnp.int32, (groups, 8, wide), 1)
                down = jnp.where(index == 0, roll_rows(low[:, 8:], 1), roll_rows(low[:, :8], 1))
                up = jnp.where(index == 7, roll_rows(high[:, 8:], -1), roll_rows(high[:, :8], -1))
                total = down + mid[:, :8] + up
            total = jnp.maximum(total, 0.0).reshape(part, size_b, 8, wide)
            out_ref[first : first + part] = total[..., :filters].astype(out_ref.dtype)

    return pl.pallas_call(
        body,
        in_specs=[pl.BlockSpec(memory_space=pltpu.VMEM)] * 2,
        out_specs=pl.BlockSpec(memory_space=pltpu.VMEM),
        out_shape=jax.ShapeDtypeStruct((size_a, size_b, 8, filters), jnp.bfloat16),
        compiler_params=pltpu.CompilerParams(vmem_limit_bytes=40 << 20),
        name=name,
    )(field, weights)


def decode(place_z, field, edge, weights):
    size_x, size_y, size_z, channels = field.shape
    size_x, size_y = size_x - 2, size_y - 2
    filters = weights.shape[-1]
    rows, extra = size_x * size_y * size_z, size_x * size_y
    weights = weights.reshape(9, 3, channels, filters)

    def body(place_ref, field_ref, edge_ref, weights_hbm, out_ref, weights_ref, sums_ref, sems):
        copies = [pltpu.make_async_copy(weights_hbm.at[step], weights_ref.at[step], sems.at[step]) for step in range(9)]
        for copy in copies:
            copy.start()
        for dx in range(3):
            blocks = []
            for dy in range(3):
                main = field_ref[dx : dx + size_x, dy : dy + size_y].astype(jnp.float32).reshape(rows, channels)
                side = edge_ref[dy, dx : dx + size_x].astype(jnp.float32).reshape(extra, channels)
                blocks.append(jnp.concatenate([main, side], axis=0).astype(jnp.bfloat16))
                copies[3 * dx + dy].wait()
            block = jnp.concatenate(blocks, axis=1)
            for tap in range(3):
                kernel = weights_ref[3 * dx : 3 * dx + 3, tap].reshape(3 * channels, filters)
                product = jnp.dot(block, kernel, preferred_element_type=jnp.float32)
                if dx == 0:
                    sums_ref[tap] = product
                else:
                    sums_ref[tap] += product
        first = place_ref[0] == 0
        low, mid, high = [sums_ref[tap, :rows].reshape(extra, size_z, filters) for tap in range(3)]
        zero = jnp.zeros((extra, filters), jnp.float32)
        below = jnp.where(first, zero, sums_ref[0, rows:])
        above = jnp.where(first, sums_ref[2, rows:], zero)
        index = lax.broadcasted_iota(jnp.int32, (extra, size_z, filters), 1)
        down = jnp.where(index == 0, below[:, None, :], roll_rows(low, 1))
        up = jnp.where(index == size_z - 1, above[:, None, :], roll_rows(high, -1))
        out_ref[...] = (down + mid + up).reshape(size_x, size_y, size_z, filters).astype(out_ref.dtype)

    return pl.pallas_call(
        body,
        in_specs=[
            pl.BlockSpec(memory_space=pltpu.SMEM),
            pl.BlockSpec(memory_space=pltpu.VMEM),
            pl.BlockSpec(memory_space=pltpu.VMEM),
            pl.BlockSpec(memory_space=pl.ANY),
        ],
        out_specs=pl.BlockSpec(memory_space=pltpu.VMEM),
        out_shape=jax.ShapeDtypeStruct((size_x, size_y, size_z, filters), jnp.bfloat16),
        scratch_shapes=[
            pltpu.VMEM(weights.shape, weights.dtype),
            pltpu.VMEM((3, rows + extra, filters), jnp.float32),
            pltpu.SemaphoreType.DMA((9,)),
        ],
        compiler_params=pltpu.CompilerParams(vmem_limit_bytes=48 << 20),
        name="decode",
    )(place_z, field, edge, weights)


def beside(weights):
    channels, filters = weights.shape[3:]
    weights = weights.transpose(0, 2, 3, 1, 4).reshape(9, 1, channels, 3 * filters)
    return jnp.pad(weights, ((0, 0), (0, 0), (0, 0), (0, 256 - 3 * filters)))


def solution(mesh):
    gx, gy, gz = mesh.shape["gx"], mesh.shape["gy"], mesh.shape["gz"]

    def local(volume, w_full, w_half, w_bottom_in, w_bottom_out, w_up):
        place_z = lax.axis_index("gz")
        field = extend(volume, "gx", gx, 0, 3)
        field = extend(field, "gy", gy, 1, 3)
        field = extend(field, "gz", gz, 2, 1)
        pooled = shrink(rectify(conv(field, w_full)))
        pooled = clear_outside(pooled, "gx", gx, 0, 1)
        pooled = clear_outside(pooled, "gy", gy, 1, 1)
        below, above = halo(pooled, "gz", gz, 2, 1)
        pooled = jnp.concatenate([pooled, above, jnp.zeros_like(pooled)[:, :, :6], below], axis=2)
        skip = tile_conv(pooled, w_half.reshape(9, 3, w_half.shape[3], w_half.shape[4]), "half")
        coarse = shrink(skip)
        own_x, own_y, own_z, ch1 = coarse.shape

        column = extend(coarse, "gy", gy, 1, 1)
        column = jnp.broadcast_to(column[None], (gx * gz,) + column.shape)
        column = lax.all_to_all(column, ("gx", "gz"), 0, 0)
        column = column.reshape(gx, gz, own_x, own_y + 2, own_z, ch1)
        column = column.transpose(0, 2, 1, 4, 3, 5).reshape(gx * own_x, gz * own_z, own_y + 2, ch1)
        column = jnp.pad(column, ((1, 1), (1, 1), (0, 2), (0, 0)))
        first = tile_conv(column, beside(w_bottom_in), "bottom_in")[:, :, 1 : own_y + 1]

        part = first.shape[-1]
        first = jnp.broadcast_to(first[None], (gx,) + first.shape)
        first = lax.all_to_all(first, "gx", 0, 0)
        first = first.transpose(1, 2, 3, 0, 4).reshape(first.shape[1:4] + (gx * part,))
        first = extend(first, "gy", gy, 2, 2)
        first = jnp.pad(first, ((1, 1), (1, 1), (0, 0), (0, 0)))
        second = tile_conv(first, beside(w_bottom_out), "bottom_out")[:, :, 1 : own_y + 3]
        second = clear_outside(second, "gy", gy, 2, 1)
        second = jnp.pad(second, ((1, 1), (1, 1), (0, 0), (0, 0)))
        second = lax.dynamic_slice_in_dim(second, place_z * own_z, own_z + 2, axis=1)
        second = jnp.stack([second[own_x * i : own_x * i + own_x + 2] for i in range(gx)])
        second = lax.all_to_all(second, "gx", 0, 0)
        second = second.transpose(1, 3, 2, 0, 4).reshape(own_x + 2, own_y + 2, own_z + 2, gx * part)

        around = extend(skip, "gx", gx, 0, 1)
        around = extend(around, "gy", gy, 1, 1)
        got = lax.ppermute(jnp.where(place_z == 0, around[:, :, -1], around[:, :, 0]), "gz", [(0, 1), (1, 0)])
        spread = enlarge(second)[1:-1, 1:-1]
        side = jnp.where(place_z == 0, spread[:, :, -2], spread[:, :, 1])
        joined = jnp.concatenate([spread[:, :, 2:-2], around], axis=3)
        side = jnp.concatenate([side, got], axis=2)
        side = jnp.stack([side[:, dy : dy + skip.shape[1]] for dy in range(3)])
        return decode(place_z[None], joined, side, w_up)

    space = P("gx", "gy", "gz", None)
    filters = P(None, None, None, None, "gx")
    return jax.shard_map(
        local,
        mesh=mesh,
        in_specs=(space, P(), P(), filters, filters, P()),
        out_specs=space,
        check_vma=False,
    )
```

```python
import jax
import jax.numpy as jnp
from jax import lax
from jax.experimental import pallas as pl
from jax.experimental.pallas import tpu as pltpu
from jax.sharding import PartitionSpec as P


def shrink(field):
    size_x, size_y, size_z, channels = field.shape
    blocks = field.reshape(size_x // 2, 2, size_y // 2, 2, size_z // 2, 2, channels)
    return jnp.max(blocks, axis=(1, 3, 5))


def halo(field, axis, count, dim, width):
    place = lax.axis_index(axis)
    size = field.shape[dim]
    low = lax.slice_in_dim(field, 0, width, axis=dim)
    high = lax.slice_in_dim(field, size - width, size, axis=dim)
    zero = jnp.zeros_like(low)
    if count == 2:
        got = lax.ppermute(jnp.where(place == 0, high, low), axis, [(0, 1), (1, 0)])
        below = jnp.where(place == 1, got, zero)
        above = jnp.where(place == 0, got, zero)
        return below, above
    even = place % 2 == 0
    inner = [(i, i ^ 1) for i in range(count)]
    outer = [(i, (((i + 1) ^ 1) - 1) % count) for i in range(count)]
    got_in = lax.ppermute(jnp.where(even, high, low), axis, inner)
    got_out = lax.ppermute(jnp.where(even, low, high), axis, outer)
    below = jnp.where(place > 0, jnp.where(even, got_out, got_in), zero)
    above = jnp.where(place < count - 1, jnp.where(even, got_in, got_out), zero)
    return below, above


def extend(field, axis, count, dim, width):
    below, above = halo(field, axis, count, dim, width)
    return jnp.concatenate([below, field, above], axis=dim)


def roll_rows(block, shift):
    return pltpu.roll(block, shift % block.shape[1], 1)


def tile_conv(field, weights, name):
    size_a, size_b, size_s, channels = field.shape
    size_a, size_b = size_a - 2, size_b - 2
    steps, taps, _, width = weights.shape
    filters = width if taps == 3 else 64
    wide = width if taps == 3 else 128
    part = max(1, 256 // (size_b * size_s))

    def body(field_ref, weights_ref, out_ref):
        for first in range(0, size_a, part):
            rows = part * size_b * size_s
            groups = part * size_b
            blocks = []
            for step in range(steps):
                da, db = step // 3, step % 3
                block = field_ref[first + da : first + da + part, db : db + size_b]
                if size_s % 16:
                    block = block.astype(jnp.float32)
                blocks.append(block.reshape(rows, channels).astype(jnp.bfloat16))
            block = jnp.concatenate(blocks, axis=1)
            sums = []
            for tap in range(taps):
                kernel = weights_ref[:, tap].reshape(steps * channels, width)
                sums.append(jnp.dot(block, kernel, preferred_element_type=jnp.float32))
            if taps == 3:
                low, mid, high = [total.reshape(groups, size_s, width) for total in sums]
            else:
                low = sums[0][:, :128].reshape(groups, size_s, 128)
                mid = pltpu.roll(sums[0][:, :128], 64, 1).reshape(groups, size_s, 128)
                high = sums[0][:, 128:].reshape(groups, size_s, 128)
            if size_s == 8:
                total = roll_rows(low, 1) + mid + roll_rows(high, -1)
            else:
                index = lax.broadcasted_iota(jnp.int32, (groups, 8, wide), 1)
                down = jnp.where(index == 0, roll_rows(low[:, 8:], 1), roll_rows(low[:, :8], 1))
                up = jnp.where(index == 7, roll_rows(high[:, 8:], -1), roll_rows(high[:, :8], -1))
                total = down + mid[:, :8] + up
            total = jnp.maximum(total, 0.0).reshape(part, size_b, 8, wide)
            out_ref[first : first + part] = total[..., :filters].astype(out_ref.dtype)

    return pl.pallas_call(
        body,
        in_specs=[pl.BlockSpec(memory_space=pltpu.VMEM)] * 2,
        out_specs=pl.BlockSpec(memory_space=pltpu.VMEM),
        out_shape=jax.ShapeDtypeStruct((size_a, size_b, 8, filters), jnp.bfloat16),
        compiler_params=pltpu.CompilerParams(vmem_limit_bytes=40 << 20),
        name=name,
    )(field, weights)


def encode(place, field, edge, weights):
    size_x, size_y, size_z, channels = field.shape
    size_x, size_y = size_x - 2, size_y - 2
    filters = weights.shape[-1] // 2
    rows, extra = size_y * size_z, edge.shape[2]
    pool_y, pool_z = size_y // 2, size_z // 2

    def body(place_ref, field_ref, edge_ref, weights_ref, out_ref, rows_ref):
        index = lax.broadcasted_iota(jnp.int32, (size_y, size_z, 2 * filters), 1)
        first = place_ref[2] == 0
        line = lax.broadcasted_iota(jnp.int32, (pool_y, pool_z, filters), 0)
        inside_y = ((line > 0) | (place_ref[1] > 0)) & ((line < pool_y - 1) | (place_ref[1] < place_ref[4]))
        for pair in range(size_x // 2):
            blocks = []
            for plane in range(4):
                for dy in range(3):
                    main = field_ref[2 * pair + plane, dy : dy + size_y].reshape(rows, channels)
                    blocks.append(jnp.concatenate([main, edge_ref[dy, 2 * pair + plane]], axis=0))
            block = jnp.concatenate(blocks, axis=1)
            sums = []
            for tap in range(3):
                kernel = weights_ref[:, :, tap].reshape(12 * channels, 2 * filters)
                sums.append(jnp.dot(block, kernel, preferred_element_type=jnp.float32))
            low, mid, high = [total[:rows].reshape(size_y, size_z, 2 * filters) for total in sums]
            below = jnp.where(first, 0.0, sums[0][rows : rows + size_y])
            above = jnp.where(first, sums[2][rows : rows + size_y], 0.0)
            down = jnp.where(index == 0, below[:, None, :], pltpu.roll(low, 1, 1))
            up = jnp.where(index == size_z - 1, above[:, None, :], pltpu.roll(high, size_z - 1, 1))
            total = jnp.maximum(down + mid + up, 0.0)
            total = jnp.maximum(total[..., :filters], total[..., filters:])
            total = jnp.max(total.reshape(pool_y, 2, size_z, filters), axis=1)
            rows_ref[...] = total.reshape(pool_y * size_z, filters)
            total = jnp.maximum(
                rows_ref[pl.ds(0, pool_y * pool_z, stride=2), :], rows_ref[pl.ds(1, pool_y * pool_z, stride=2), :]
            ).reshape(pool_y, pool_z, filters)
            inside = inside_y
            if pair == 0:
                inside = inside & (place_ref[0] > 0)
            if pair == size_x // 2 - 1:
                inside = inside & (place_ref[0] < place_ref[3])
            out_ref[pair] = jnp.where(inside, total, 0.0).astype(out_ref.dtype)

    return pl.pallas_call(
        body,
        in_specs=[pl.BlockSpec(memory_space=pltpu.SMEM)] + [pl.BlockSpec(memory_space=pltpu.VMEM)] * 3,
        out_specs=pl.BlockSpec(memory_space=pltpu.VMEM),
        out_shape=jax.ShapeDtypeStruct((size_x // 2, pool_y, pool_z, filters), jnp.bfloat16),
        scratch_shapes=[pltpu.VMEM((pool_y * size_z, filters), jnp.float32)],
        compiler_params=pltpu.CompilerParams(vmem_limit_bytes=32 << 20),
        name="encode",
    )(place, field, edge, weights)


def paired(weights):
    grow = [(0, 0)] * 4
    return jnp.concatenate([jnp.pad(weights, [(0, 1)] + grow), jnp.pad(weights, [(1, 0)] + grow)], axis=4)


def halves(pair_low, pair_high):
    lane = lax.broadcasted_iota(jnp.int32, pair_low.shape, pair_low.ndim - 1)
    axis = pair_low.ndim - 1
    even = jnp.where(lane < 64, pair_low, pltpu.roll(pair_high, 64, axis))
    odd = jnp.where(lane < 64, pltpu.roll(pair_low, 64, axis), pair_high)
    return even, odd


def side_by_side(even, odd):
    lane = lax.broadcasted_iota(jnp.int32, even.shape, even.ndim - 1)
    return jnp.where(lane < 64, even, pltpu.roll(odd, 64, even.ndim - 1))


def column_product(pad_ref, weights_ref, first, start, planes, size_z):
    channels = pad_ref.shape[-1]
    rows = planes * size_z * 8
    blocks = []
    for dx in range(3):
        for dz in range(3):
            block = pad_ref[first + dx : first + dx + planes, pl.ds(start + dz, size_z)]
            blocks.append(block.reshape(rows, channels).astype(jnp.bfloat16))
    block = jnp.concatenate(blocks, axis=1)
    total = jnp.dot(block, weights_ref[...].reshape(9 * channels, 256), preferred_element_type=jnp.float32)
    low = total[:, :128].reshape(planes * size_z, 8, 128)
    mid = pltpu.roll(total[:, :128], 64, 1).reshape(planes * size_z, 8, 128)
    high = total[:, 128:].reshape(planes * size_z, 8, 128)
    total = pltpu.roll(low, 1, 1) + mid + pltpu.roll(high, 7, 1)
    return jnp.maximum(total, 0.0).reshape(planes, size_z, 8, 128)


def bottom_in(place, field, weights):
    count, own_x, own_z, _, channels = field.shape
    devices = count // 2
    size_x, all_z, size_z, size_y = devices * own_x, 2 * own_z, own_z + 2, own_z

    def body(place_ref, field_ref, weights_ref, out_ref, pad_ref):
        zero = jnp.zeros((all_z + 2, 8, channels), jnp.float32)
        pad_ref[0] = zero
        pad_ref[size_x + 1] = zero
        for x in range(size_x):
            pad_ref[x + 1, 0] = zero[0]
            pad_ref[x + 1, all_z + 1] = zero[0]
        for i in range(devices):
            for half in range(2):
                block = field_ref[2 * i + half].astype(jnp.float32)
                pad_ref[1 + own_x * i : 1 + own_x * i + own_x, 1 + own_z * half : 1 + own_z * half + own_z] = block
        start = 2 * place_ref[2]
        for first in range(0, size_x, 4):
            total = column_product(pad_ref, weights_ref, first, start, 4, size_z)
            for pair in range(2):
                both = side_by_side(total[2 * pair], total[2 * pair + 1])[:, 1 : size_y + 1].astype(out_ref.dtype)
                for i in range(devices):
                    out_ref[i, first // 2 + pair] = both

    return pl.pallas_call(
        body,
        in_specs=[pl.BlockSpec(memory_space=pltpu.SMEM)] + [pl.BlockSpec(memory_space=pltpu.VMEM)] * 2,
        out_specs=pl.BlockSpec(memory_space=pltpu.VMEM),
        out_shape=jax.ShapeDtypeStruct((devices, size_x // 2, size_z, size_y, 128), jnp.bfloat16),
        scratch_shapes=[pltpu.VMEM((size_x + 2, all_z + 2, 8, channels), jnp.float32)],
        compiler_params=pltpu.CompilerParams(vmem_limit_bytes=16 << 20),
        name="bottom_in",
    )(place, field, weights)


def bottom_out(place, field, weights):
    devices, pairs, size_z, _, _ = field.shape
    size_x, channels = 2 * pairs, 64 * devices
    own_x = size_x // devices

    def body(place_ref, field_ref, weights_ref, out_ref, pad_ref, total_ref):
        zero = jnp.zeros((size_z + 2, 8, channels), jnp.float32)
        for ref in (pad_ref, total_ref):
            wide = ref.shape[-1]
            ref[0] = zero[..., :wide]
            ref[size_x + 1] = zero[..., :wide]
            for x in range(size_x):
                ref[x + 1, 0] = zero[0, :, :wide]
                ref[x + 1, size_z + 1] = zero[0, :, :wide]
        for k in range(devices // 2):
            for pair in range(pairs):
                low, high = [field_ref[2 * k + i, pair].astype(jnp.float32) for i in range(2)]
                even, odd = halves(low, high)
                pad_ref[1 + 2 * pair, 1 : size_z + 1, :, 128 * k : 128 * k + 128] = even
                pad_ref[2 + 2 * pair, 1 : size_z + 1, :, 128 * k : 128 * k + 128] = odd
        for first in range(0, size_x, 4):
            total = column_product(pad_ref, weights_ref, first, 0, 4, size_z)
            total_ref[1 + first : 5 + first, 1 : size_z + 1] = total
        start = 2 * place_ref[2]
        for i in range(size_x // 2 + 1):
            low, high = [total_ref[2 * i + n, pl.ds(start, size_z)] for n in range(2)]
            both = side_by_side(low, high).astype(out_ref.dtype)
            if i < devices:
                out_ref[i, 0] = both
            if i > 0:
                out_ref[i - 1, 1] = both

    return pl.pallas_call(
        body,
        in_specs=[pl.BlockSpec(memory_space=pltpu.SMEM)] + [pl.BlockSpec(memory_space=pltpu.VMEM)] * 2,
        out_specs=pl.BlockSpec(memory_space=pltpu.VMEM),
        out_shape=jax.ShapeDtypeStruct((devices, own_x, size_z, 8, 128), jnp.bfloat16),
        scratch_shapes=[
            pltpu.VMEM((size_x + 2, size_z + 2, 8, channels), jnp.float32),
            pltpu.VMEM((size_x + 2, size_z + 2, 8, 128), jnp.float32),
        ],
        compiler_params=pltpu.CompilerParams(vmem_limit_bytes=24 << 20),
        name="bottom_out",
    )(place, field, weights)


def decode(place, bottom, skip, edge, weights):
    devices, pairs, coarse_z, _, _ = bottom.shape
    full_x, full_y, size_z, skip_channels = skip.shape
    size_x, size_y = full_x - 2, full_y - 2
    channels = 64 * devices + skip_channels
    filters = weights.shape[-1]
    rows, extra = size_x * size_y * size_z, size_x * size_y
    weights = weights.reshape(9, 3, channels, filters)

    def body(place_ref, bottom_ref, skip_ref, edge_ref, weights_hbm, out_ref, weights_ref, main_ref, side_ref, sums_ref, sems):
        copies = [pltpu.make_async_copy(weights_hbm.at[step], weights_ref.at[step], sems.at[step]) for step in range(9)]
        for copy in copies:
            copy.start()
        first = place_ref[2] == 0
        planes = [[] for _ in range(2 * pairs)]
        for k in range(devices // 2):
            for pair in range(pairs):
                low, high = [bottom_ref[2 * k + i, pair].astype(jnp.float32) for i in range(2)]
                even, odd = halves(low, high)
                planes[2 * pair].append(even.reshape(coarse_z * 8, 128))
                planes[2 * pair + 1].append(odd.reshape(coarse_z * 8, 128))

        def choice(y, z, source):
            line = (y + 1) // 2 + 1
            inside = ((line > 1) | (place_ref[1] > 0)) & ((line < coarse_z) | (place_ref[1] < place_ref[4]))
            return jnp.where((source == z * 8 + line) & inside, 1.0, 0.0).astype(jnp.bfloat16)

        shape = (full_y * size_z, coarse_z * 8)
        row = lax.broadcasted_iota(jnp.int32, shape, 0)
        spread = choice(row // size_z, row % size_z // 2 + 1, lax.broadcasted_iota(jnp.int32, shape, 1))
        shape = (16, coarse_z * 8)
        row = lax.broadcasted_iota(jnp.int32, shape, 0)
        other = jnp.where(first, coarse_z - 1, 0)
        spread_edge = choice(row, other, lax.broadcasted_iota(jnp.int32, shape, 1))
        for plane in range(2 * pairs):
            coarse = jnp.concatenate(planes[plane], axis=1).astype(jnp.bfloat16)
            fine = jnp.dot(spread, coarse, preferred_element_type=jnp.float32)
            fine_edge = jnp.dot(spread_edge, coarse, preferred_element_type=jnp.float32)
            for x in range(full_x):
                if (x + 1) // 2 != plane:
                    continue
                joined = jnp.concatenate([fine, skip_ref[x].astype(jnp.float32).reshape(full_y * size_z, skip_channels)], axis=1)
                joined_edge = jnp.concatenate([fine_edge, edge_ref[x].astype(jnp.float32)], axis=1)
                for dy in range(3):
                    main_ref[dy, x] = joined[8 * dy : 8 * dy + size_y * size_z].astype(jnp.bfloat16)
                    side_ref[dy, x] = joined_edge[dy : dy + size_y]
        for dx in range(3):
            blocks = []
            for dy in range(3):
                main = main_ref[dy, dx : dx + size_x].reshape(rows, channels)
                side = side_ref[dy, dx : dx + size_x].reshape(extra, channels).astype(jnp.bfloat16)
                blocks.append(jnp.concatenate([main, side], axis=0))
                copies[3 * dx + dy].wait()
            block = jnp.concatenate(blocks, axis=1)
            for tap in range(3):
                kernel = weights_ref[3 * dx : 3 * dx + 3, tap].reshape(3 * channels, filters)
                product = jnp.dot(block, kernel, preferred_element_type=jnp.float32)
                if dx == 0:
                    sums_ref[tap] = product
                else:
                    sums_ref[tap] += product
        low, mid, high = [sums_ref[tap, :rows].reshape(extra, size_z, filters) for tap in range(3)]
        below = jnp.where(first, 0.0, sums_ref[0, rows:])
        above = jnp.where(first, sums_ref[2, rows:], 0.0)
        index = lax.broadcasted_iota(jnp.int32, (extra, size_z, filters), 1)
        down = jnp.where(index == 0, below[:, None, :], roll_rows(low, 1))
        up = jnp.where(index == size_z - 1, above[:, None, :], roll_rows(high, -1))
        out_ref[...] = (down + mid + up).reshape(size_x, size_y, size_z, filters).astype(out_ref.dtype)

    return pl.pallas_call(
        body,
        in_specs=[pl.BlockSpec(memory_space=pltpu.SMEM)]
        + [pl.BlockSpec(memory_space=pltpu.VMEM)] * 3
        + [pl.BlockSpec(memory_space=pl.ANY)],
        out_specs=pl.BlockSpec(memory_space=pltpu.VMEM),
        out_shape=jax.ShapeDtypeStruct((size_x, size_y, size_z, filters), jnp.bfloat16),
        scratch_shapes=[
            pltpu.VMEM(weights.shape, weights.dtype),
            pltpu.VMEM((3, full_x, size_y * size_z, channels), jnp.bfloat16),
            pltpu.VMEM((3, full_x, size_y, channels), jnp.float32),
            pltpu.VMEM((3, rows + extra, filters), jnp.float32),
            pltpu.SemaphoreType.DMA((9,)),
        ],
        compiler_params=pltpu.CompilerParams(vmem_limit_bytes=32 << 20),
        name="decode",
    )(place, bottom, skip, edge, weights)


def beside(weights):
    channels, filters = weights.shape[3:]
    weights = weights.transpose(0, 2, 3, 1, 4).reshape(9, channels, 3 * filters)
    return jnp.pad(weights, ((0, 0), (0, 0), (0, 256 - 3 * filters)))


def solution(mesh):
    gx, gy, gz = mesh.shape["gx"], mesh.shape["gy"], mesh.shape["gz"]

    def local(volume, w_full, w_half, w_bottom_in, w_bottom_out, w_up):
        place_z = lax.axis_index("gz")
        place = jnp.stack([lax.axis_index("gx"), lax.axis_index("gy"), place_z, jnp.int32(gx - 1), jnp.int32(gy - 1)])
        swap = [(0, 1), (1, 0)]

        def edge_of(plane_low, plane_high):
            return lax.ppermute(jnp.where(place_z == 0, plane_high, plane_low), "gz", swap)

        below, above = halo(volume, "gx", gx, 0, 3)
        w_pair, w_in, w_out = paired(w_full), beside(w_bottom_in), beside(w_bottom_out)
        below, above, w_pair, w_in, w_out = lax.optimization_barrier((below, above, w_pair, w_in, w_out))
        field = jnp.concatenate([below, volume, above], axis=0)
        field = extend(field, "gy", gy, 1, 3)
        edge = edge_of(field[:, :, 0], field[:, :, -1])
        rows = field.shape[1] - 2
        edge = jnp.stack([jnp.pad(edge[:, dy : dy + rows], ((0, 0), (0, -rows % 16), (0, 0))) for dy in range(3)])
        pooled = encode(place, field, edge, w_pair)

        got = edge_of(pooled[:, :, 0], pooled[:, :, -1])[:, :, None]
        zero = jnp.zeros_like(got)
        above, below = jnp.where(place_z == 0, got, zero), jnp.where(place_z == 0, zero, got)
        pooled = jnp.concatenate([pooled, above, jnp.zeros_like(pooled)[:, :, :6], below], axis=2)
        skip = tile_conv(pooled, w_half.reshape(9, 3, w_half.shape[3], w_half.shape[4]), "half")
        coarse = shrink(skip).transpose(0, 2, 1, 3)
        own_y = coarse.shape[2]

        column = jnp.pad(extend(coarse, "gy", gy, 2, 1), ((0, 0), (0, 0), (0, 6 - own_y), (0, 0)))
        column = jnp.broadcast_to(column[None], (gx * gz,) + column.shape)
        column = lax.all_to_all(column, ("gx", "gz"), 0, 0)
        first = bottom_in(place, column, w_in)
        first = lax.all_to_all(first, "gx", 0, 0)
        first = extend(first, "gy", gy, 3, 2)
        second = bottom_out(place, first, w_out)
        second = lax.all_to_all(second, "gx", 0, 0)

        around = extend(skip, "gx", gx, 0, 1)
        around = extend(around, "gy", gy, 1, 1)
        side = edge_of(around[:, :, 0], around[:, :, -1])
        side = jnp.pad(side, ((0, 0), (0, -side.shape[1] % 16), (0, 0)))
        return decode(place, second, around, side, w_up)

    space = P("gx", "gy", "gz", None)
    filters = P(None, None, None, None, "gx")
    return jax.shard_map(
        local,
        mesh=mesh,
        in_specs=(space, P(), P(), filters, filters, P()),
        out_specs=space,
        check_vma=False,
    )
```

```python
import jax
import jax.numpy as jnp
from jax import lax
from jax.experimental import pallas as pl
from jax.experimental.pallas import tpu as pltpu
from jax.sharding import PartitionSpec as P


def swaps(low, high, axis, count):
    even = lax.axis_index(axis) % 2 == 0
    inner = [(i, i ^ 1) for i in range(count)]
    outer = [(i, (((i + 1) ^ 1) - 1) % count) for i in range(count)]
    got_in = lax.ppermute(jnp.where(even, high, low), axis, inner)
    got_out = lax.ppermute(jnp.where(even, low, high), axis, outer)
    return got_in, got_out


def ordered(got_in, got_out, axis):
    even = lax.axis_index(axis) % 2 == 0
    return jnp.where(even, got_out, got_in), jnp.where(even, got_in, got_out)


def halo(field, axis, count, dim, width):
    place = lax.axis_index(axis)
    size = field.shape[dim]
    low = lax.slice_in_dim(field, 0, width, axis=dim)
    high = lax.slice_in_dim(field, size - width, size, axis=dim)
    below, above = ordered(*swaps(low, high, axis, count), axis)
    zero = jnp.zeros_like(low)
    return jnp.where(place > 0, below, zero), jnp.where(place < count - 1, above, zero)


def extend(field, axis, count, dim, width):
    below, above = halo(field, axis, count, dim, width)
    return jnp.concatenate([below, field, above], axis=dim)


def half_level(place, field, edge, weights):
    full_x, full_y, size_z, channels = field.shape
    size_x, size_y = full_x - 2, full_y - 2
    filters = weights.shape[-1]
    rows, extra = size_x * size_y * size_z, size_x * size_y

    def body(place_ref, field_ref, edge_ref, weights_ref, out_ref, coarse_ref, rows_ref):
        first = place_ref[2] == 0
        edge_plane = edge_ref[...].astype(jnp.float32)
        blocks = []
        for dx in range(3):
            for dy in range(3):
                main = field_ref[dx : dx + size_x, dy : dy + size_y].astype(jnp.float32).reshape(rows, channels)
                side = edge_plane[dx : dx + size_x, dy : dy + size_y].reshape(extra, channels)
                blocks.append(jnp.concatenate([main, side], axis=0).astype(jnp.bfloat16))
        block = jnp.concatenate(blocks, axis=1)
        sums = []
        for tap in range(3):
            kernel = weights_ref[:, tap].reshape(9 * channels, filters)
            sums.append(jnp.dot(block, kernel, preferred_element_type=jnp.float32))
        total = jnp.maximum(join_taps(first, sums, extra, size_z), 0.0)
        out_ref[...] = total.reshape(size_x, size_y, size_z, filters).astype(out_ref.dtype)
        total = jnp.max(total.reshape(size_x // 2, 2, size_y // 2, 2, size_z, filters), axis=(1, 3))
        count = size_y // 2
        for part in range(filters // 128):
            rows_ref[...] = total[..., 128 * part : 128 * part + 128].reshape(rows // 4, 128)
            for x in range(size_x // 2):
                for z in range(size_z // 2):
                    start = x * count * size_z + 2 * z
                    pooled = jnp.maximum(
                        rows_ref[pl.ds(start, count, stride=size_z), :], rows_ref[pl.ds(start + 1, count, stride=size_z), :]
                    )
                    coarse_ref[x, z, :, 128 * part : 128 * part + 128] = pooled.astype(coarse_ref.dtype)

    return pl.pallas_call(
        body,
        in_specs=[pl.BlockSpec(memory_space=pltpu.SMEM)] + [pl.BlockSpec(memory_space=pltpu.VMEM)] * 3,
        out_specs=[pl.BlockSpec(memory_space=pltpu.VMEM)] * 2,
        out_shape=[
            jax.ShapeDtypeStruct((size_x, size_y, size_z, filters), jnp.bfloat16),
            jax.ShapeDtypeStruct((size_x // 2, size_z // 2, size_y // 2, filters), jnp.bfloat16),
        ],
        scratch_shapes=[pltpu.VMEM((rows // 4, 128), jnp.float32)],
        compiler_params=pltpu.CompilerParams(vmem_limit_bytes=12 << 20),
        name="half_level",
    )(place, field, edge, weights)


def join_taps(first, sums, groups, size_z):
    rows, filters = groups * size_z, sums[0].shape[-1]
    low, mid, high = [total[:rows].reshape(groups, size_z, filters) for total in sums]
    below = jnp.where(first, 0.0, sums[0][rows : rows + groups])
    above = jnp.where(first, sums[2][rows : rows + groups], 0.0)
    index = lax.broadcasted_iota(jnp.int32, (groups, size_z, filters), 1)
    down = jnp.where(index == 0, below[:, None, :], pltpu.roll(low, 1, 1))
    up = jnp.where(index == size_z - 1, above[:, None, :], pltpu.roll(high, size_z - 1, 1))
    return down + mid + up


def encode(place, own, x_in, x_out, y_in, y_out, edge, weights):
    own_x, own_y, size_z, channels = own.shape
    reach = x_in.shape[0]
    full_x, full_y = own_x + 2 * reach, own_y + 2 * reach
    size_x, size_y = full_x - 2, full_y - 2
    filters = weights.shape[-1] // 2
    rows, extra = size_y * size_z, size_y + (-size_y % 16)
    pool_y, pool_z = size_y // 2, size_z // 2

    def body(
        place_ref, own_ref, x_in_ref, x_out_ref, y_in_ref, y_out_ref, edge_ref, weights_ref, out_ref, field_ref, side_ref, rows_ref
    ):
        even_x, even_y = place_ref[0] % 2 == 0, place_ref[1] % 2 == 0
        low_x, high_x = place_ref[0] > 0, place_ref[0] < place_ref[3]
        low_y, high_y = place_ref[1] > 0, place_ref[1] < place_ref[4]
        nil = jnp.bfloat16(0)
        inner_y = slice(reach, reach + own_y)
        below, above = jnp.where(even_x, x_out_ref[...], x_in_ref[...]), jnp.where(even_x, x_in_ref[...], x_out_ref[...])
        field_ref[:reach, inner_y] = jnp.where(low_x, below, nil)
        field_ref[reach + own_x :, inner_y] = jnp.where(high_x, above, nil)
        field_ref[reach : reach + own_x, inner_y] = own_ref[...]
        for x in range(full_x):
            here_low, here_high = low_y, high_y
            if x < reach:
                here_low, here_high = low_y & low_x, high_y & low_x
            if x >= reach + own_x:
                here_low, here_high = low_y & high_x, high_y & high_x
            below, above = jnp.where(even_y, y_out_ref[x], y_in_ref[x]), jnp.where(even_y, y_in_ref[x], y_out_ref[x])
            field_ref[x, :reach] = jnp.where(here_low, below, nil)
            field_ref[x, reach + own_y :] = jnp.where(here_high, above, nil)
            line = lax.broadcasted_iota(jnp.int32, (full_y, channels), 0)
            inside = ((line >= reach) | low_y) & ((line < reach + own_y) | high_y)
            if x < reach:
                inside = inside & low_x
            if x >= reach + own_x:
                inside = inside & high_x
            plane = jnp.where(inside, edge_ref[x].astype(jnp.float32), 0.0)
            for dy in range(3):
                side_ref[dy, x, :size_y] = plane[dy : dy + size_y]
                side_ref[dy, x, size_y:] = jnp.zeros((extra - size_y, channels), jnp.float32)

        first = place_ref[2] == 0
        line = lax.broadcasted_iota(jnp.int32, (pool_y, pool_z, filters), 0)
        inside_y = ((line > 0) | low_y) & ((line < pool_y - 1) | high_y)
        for pair in range(size_x // 2):
            blocks = []
            for plane in range(4):
                for dy in range(3):
                    main = field_ref[2 * pair + plane, dy : dy + size_y].reshape(rows, channels)
                    side = side_ref[dy, 2 * pair + plane].astype(jnp.bfloat16)
                    blocks.append(jnp.concatenate([main, side], axis=0))
            block = jnp.concatenate(blocks, axis=1)
            sums = []
            for tap in range(3):
                kernel = weights_ref[:, :, tap].reshape(12 * channels, 2 * filters)
                sums.append(jnp.dot(block, kernel, preferred_element_type=jnp.float32))
            total = jnp.maximum(join_taps(first, sums, size_y, size_z), 0.0)
            total = jnp.maximum(total[..., :filters], total[..., filters:])
            total = jnp.max(total.reshape(pool_y, 2, size_z, filters), axis=1)
            rows_ref[...] = total.reshape(pool_y * size_z, filters)
            total = jnp.maximum(
                rows_ref[pl.ds(0, pool_y * pool_z, stride=2), :], rows_ref[pl.ds(1, pool_y * pool_z, stride=2), :]
            ).reshape(pool_y, pool_z, filters)
            inside = inside_y
            if pair == 0:
                inside = inside & low_x
            if pair == size_x // 2 - 1:
                inside = inside & high_x
            out_ref[pair] = jnp.where(inside, total, 0.0).astype(out_ref.dtype)

    return pl.pallas_call(
        body,
        in_specs=[pl.BlockSpec(memory_space=pltpu.SMEM)] + [pl.BlockSpec(memory_space=pltpu.VMEM)] * 7,
        out_specs=pl.BlockSpec(memory_space=pltpu.VMEM),
        out_shape=jax.ShapeDtypeStruct((size_x // 2, pool_y, pool_z, filters), jnp.bfloat16),
        scratch_shapes=[
            pltpu.VMEM((full_x, full_y, size_z, channels), jnp.bfloat16),
            pltpu.VMEM((3, full_x, extra, channels), jnp.float32),
            pltpu.VMEM((pool_y * size_z, filters), jnp.float32),
        ],
        compiler_params=pltpu.CompilerParams(vmem_limit_bytes=16 << 20),
        name="encode",
    )(place, own, x_in, x_out, y_in, y_out, edge, weights)


def paired(weights):
    grow = [(0, 0)] * 4
    return jnp.concatenate([jnp.pad(weights, [(0, 1)] + grow), jnp.pad(weights, [(1, 0)] + grow)], axis=4)


def halves(pair_low, pair_high):
    lane = lax.broadcasted_iota(jnp.int32, pair_low.shape, pair_low.ndim - 1)
    axis = pair_low.ndim - 1
    even = jnp.where(lane < 64, pair_low, pltpu.roll(pair_high, 64, axis))
    odd = jnp.where(lane < 64, pltpu.roll(pair_low, 64, axis), pair_high)
    return even, odd


def side_by_side(even, odd):
    lane = lax.broadcasted_iota(jnp.int32, even.shape, even.ndim - 1)
    return jnp.where(lane < 64, even, pltpu.roll(odd, 64, even.ndim - 1))


def column_product(pad_ref, weights_ref, first, start, planes, size_z):
    channels = pad_ref.shape[-1]
    rows = planes * size_z * 8
    blocks = []
    for dx in range(3):
        for dz in range(3):
            block = pad_ref[first + dx : first + dx + planes, pl.ds(start + dz, size_z)]
            blocks.append(block.reshape(rows, channels).astype(jnp.bfloat16))
    block = jnp.concatenate(blocks, axis=1)
    total = jnp.dot(block, weights_ref[...].reshape(9 * channels, 256), preferred_element_type=jnp.float32)
    low = total[:, :128].reshape(planes * size_z, 8, 128)
    mid = pltpu.roll(total[:, :128], 64, 1).reshape(planes * size_z, 8, 128)
    high = total[:, 128:].reshape(planes * size_z, 8, 128)
    total = pltpu.roll(low, 1, 1) + mid + pltpu.roll(high, 7, 1)
    return jnp.maximum(total, 0.0).reshape(planes, size_z, 8, 128)


def bottom_in(place, field, weights):
    count, own_x, own_z, _, channels = field.shape
    devices = count // 2
    size_x, all_z, size_z, size_y = devices * own_x, 2 * own_z, own_z + 2, own_z

    def body(place_ref, field_ref, weights_ref, out_ref, pad_ref):
        zero = jnp.zeros((all_z + 2, 8, channels), jnp.float32)
        pad_ref[0] = zero
        pad_ref[size_x + 1] = zero
        for x in range(size_x):
            pad_ref[x + 1, 0] = zero[0]
            pad_ref[x + 1, all_z + 1] = zero[0]
        for i in range(devices):
            for half in range(2):
                block = field_ref[2 * i + half].astype(jnp.float32)
                pad_ref[1 + own_x * i : 1 + own_x * i + own_x, 1 + own_z * half : 1 + own_z * half + own_z] = block
        start = 2 * place_ref[2]
        for first in range(0, size_x, 4):
            total = column_product(pad_ref, weights_ref, first, start, 4, size_z)
            for pair in range(2):
                both = side_by_side(total[2 * pair], total[2 * pair + 1])[:, 1 : size_y + 1].astype(out_ref.dtype)
                for i in range(devices):
                    out_ref[i, first // 2 + pair] = both

    return pl.pallas_call(
        body,
        in_specs=[pl.BlockSpec(memory_space=pltpu.SMEM)] + [pl.BlockSpec(memory_space=pltpu.VMEM)] * 2,
        out_specs=pl.BlockSpec(memory_space=pltpu.VMEM),
        out_shape=jax.ShapeDtypeStruct((devices, size_x // 2, size_z, size_y, 128), jnp.bfloat16),
        scratch_shapes=[pltpu.VMEM((size_x + 2, all_z + 2, 8, channels), jnp.float32)],
        compiler_params=pltpu.CompilerParams(vmem_limit_bytes=12 << 20),
        name="bottom_in",
    )(place, field, weights)


def bottom_out(place, field, weights):
    devices, pairs, size_z, _, _ = field.shape
    size_x, channels = 2 * pairs, 64 * devices
    own_x = size_x // devices

    def body(place_ref, field_ref, weights_ref, out_ref, pad_ref, total_ref):
        zero = jnp.zeros((size_z + 2, 8, channels), jnp.float32)
        for ref in (pad_ref, total_ref):
            wide = ref.shape[-1]
            ref[0] = zero[..., :wide]
            ref[size_x + 1] = zero[..., :wide]
            for x in range(size_x):
                ref[x + 1, 0] = zero[0, :, :wide]
                ref[x + 1, size_z + 1] = zero[0, :, :wide]
        for k in range(devices // 2):
            for pair in range(pairs):
                low, high = [field_ref[2 * k + i, pair].astype(jnp.float32) for i in range(2)]
                even, odd = halves(low, high)
                pad_ref[1 + 2 * pair, 1 : size_z + 1, :, 128 * k : 128 * k + 128] = even
                pad_ref[2 + 2 * pair, 1 : size_z + 1, :, 128 * k : 128 * k + 128] = odd
        for first in range(0, size_x, 4):
            total = column_product(pad_ref, weights_ref, first, 0, 4, size_z)
            total_ref[1 + first : 5 + first, 1 : size_z + 1] = total
        start = 2 * place_ref[2]
        for i in range(size_x // 2 + 1):
            low, high = [total_ref[2 * i + n, pl.ds(start, size_z)] for n in range(2)]
            both = side_by_side(low, high).astype(out_ref.dtype)
            if i < devices:
                out_ref[i, 0] = both
            if i > 0:
                out_ref[i - 1, 1] = both

    return pl.pallas_call(
        body,
        in_specs=[pl.BlockSpec(memory_space=pltpu.SMEM)] + [pl.BlockSpec(memory_space=pltpu.VMEM)] * 2,
        out_specs=pl.BlockSpec(memory_space=pltpu.VMEM),
        out_shape=jax.ShapeDtypeStruct((devices, own_x, size_z, 8, 128), jnp.bfloat16),
        scratch_shapes=[
            pltpu.VMEM((size_x + 2, size_z + 2, 8, channels), jnp.float32),
            pltpu.VMEM((size_x + 2, size_z + 2, 8, 128), jnp.float32),
        ],
        compiler_params=pltpu.CompilerParams(vmem_limit_bytes=16 << 20),
        name="bottom_out",
    )(place, field, weights)


def decode(place, bottom, skip, edge, weights):
    devices, pairs, coarse_z, _, _ = bottom.shape
    full_x, full_y, size_z, skip_channels = skip.shape
    size_x, size_y = full_x - 2, full_y - 2
    channels = 64 * devices + skip_channels
    filters = weights.shape[-1]
    rows, extra = size_x * size_y * size_z, size_x * size_y
    weights = weights.reshape(9, 3, channels, filters)

    def body(place_ref, bottom_ref, skip_ref, edge_ref, weights_ref, out_ref, main_ref, side_ref, sums_ref):
        first = place_ref[2] == 0
        planes = [[] for _ in range(2 * pairs)]
        for k in range(devices // 2):
            for pair in range(pairs):
                low, high = [bottom_ref[2 * k + i, pair].astype(jnp.float32) for i in range(2)]
                even, odd = halves(low, high)
                planes[2 * pair].append(even.reshape(coarse_z * 8, 128))
                planes[2 * pair + 1].append(odd.reshape(coarse_z * 8, 128))

        def choice(y, z, source):
            line = (y + 1) // 2 + 1
            inside = ((line > 1) | (place_ref[1] > 0)) & ((line < coarse_z) | (place_ref[1] < place_ref[4]))
            return jnp.where((source == z * 8 + line) & inside, 1.0, 0.0).astype(jnp.bfloat16)

        shape = (full_y * size_z, coarse_z * 8)
        row = lax.broadcasted_iota(jnp.int32, shape, 0)
        spread = choice(row // size_z, row % size_z // 2 + 1, lax.broadcasted_iota(jnp.int32, shape, 1))
        shape = (16, coarse_z * 8)
        row = lax.broadcasted_iota(jnp.int32, shape, 0)
        other = jnp.where(first, coarse_z - 1, 0)
        spread_edge = choice(row, other, lax.broadcasted_iota(jnp.int32, shape, 1))
        for plane in range(2 * pairs):
            coarse = jnp.concatenate(planes[plane], axis=1).astype(jnp.bfloat16)
            fine = jnp.dot(spread, coarse, preferred_element_type=jnp.float32)
            fine_edge = jnp.dot(spread_edge, coarse, preferred_element_type=jnp.float32)
            for x in range(full_x):
                if (x + 1) // 2 != plane:
                    continue
                joined = jnp.concatenate([fine, skip_ref[x].astype(jnp.float32).reshape(full_y * size_z, skip_channels)], axis=1)
                joined_edge = jnp.concatenate([fine_edge, edge_ref[x].astype(jnp.float32)], axis=1)
                for dy in range(3):
                    main_ref[dy, x] = joined[8 * dy : 8 * dy + size_y * size_z].astype(jnp.bfloat16)
                    side_ref[dy, x] = joined_edge[dy : dy + size_y]
        for dx in range(3):
            blocks = []
            for dy in range(3):
                main = main_ref[dy, dx : dx + size_x].reshape(rows, channels)
                side = side_ref[dy, dx : dx + size_x].reshape(extra, channels).astype(jnp.bfloat16)
                blocks.append(jnp.concatenate([main, side], axis=0))
            block = jnp.concatenate(blocks, axis=1)
            for tap in range(3):
                kernel = weights_ref[3 * dx : 3 * dx + 3, tap].reshape(3 * channels, filters)
                product = jnp.dot(block, kernel, preferred_element_type=jnp.float32)
                if dx == 0:
                    sums_ref[tap] = product
                else:
                    sums_ref[tap] += product
        total = join_taps(first, [sums_ref[tap] for tap in range(3)], extra, size_z)
        out_ref[...] = total.reshape(size_x, size_y, size_z, filters).astype(out_ref.dtype)

    return pl.pallas_call(
        body,
        in_specs=[pl.BlockSpec(memory_space=pltpu.SMEM)]
        + [pl.BlockSpec(memory_space=pltpu.VMEM)] * 4,
        out_specs=pl.BlockSpec(memory_space=pltpu.VMEM),
        out_shape=jax.ShapeDtypeStruct((size_x, size_y, size_z, filters), jnp.bfloat16),
        scratch_shapes=[
            pltpu.VMEM((3, full_x, size_y * size_z, channels), jnp.bfloat16),
            pltpu.VMEM((3, full_x, size_y, channels), jnp.float32),
            pltpu.VMEM((3, rows + extra, filters), jnp.float32),
        ],
        compiler_params=pltpu.CompilerParams(vmem_limit_bytes=16 << 20),
        name="decode",
    )(place, bottom, skip, edge, weights)


def beside(weights):
    channels, filters = weights.shape[3:]
    weights = weights.transpose(0, 2, 3, 1, 4).reshape(9, channels, 3 * filters)
    return jnp.pad(weights, ((0, 0), (0, 0), (0, 256 - 3 * filters)))


def solution(mesh):
    gx, gy, gz = mesh.shape["gx"], mesh.shape["gy"], mesh.shape["gz"]

    def local(volume, w_full, w_half, w_bottom_in, w_bottom_out, w_up):
        place_z = lax.axis_index("gz")
        place = jnp.stack([lax.axis_index("gx"), lax.axis_index("gy"), place_z, jnp.int32(gx - 1), jnp.int32(gy - 1)])
        swap = [(0, 1), (1, 0)]

        def edge_of(plane_low, plane_high):
            return lax.ppermute(jnp.where(place_z == 0, plane_high, plane_low), "gz", swap)

        x_in, x_out = swaps(volume[:3], volume[-3:], "gx", gx)
        w_pair, w_out = paired(w_full), beside(w_bottom_out)
        x_in, x_out, w_pair, w_out = lax.optimization_barrier((x_in, x_out, w_pair, w_out))
        below, above = ordered(x_in, x_out, "gx")
        y_low = jnp.concatenate([below[:, :3], volume[:, :3], above[:, :3]], axis=0)
        y_high = jnp.concatenate([below[:, -3:], volume[:, -3:], above[:, -3:]], axis=0)
        y_in, y_out = swaps(y_low, y_high, "gy", gy)
        low, high = ordered(y_in, y_out, "gy")

        def plane(z):
            middle = jnp.concatenate([below[:, :, z], volume[:, :, z], above[:, :, z]], axis=0)
            return jnp.concatenate([low[:, :, z], middle, high[:, :, z]], axis=1)

        edge = edge_of(plane(0), plane(-1))
        edge, w_in = lax.optimization_barrier((edge, beside(w_bottom_in)))
        pooled = encode(place, volume, x_in, x_out, y_in, y_out, edge, w_pair)

        edge = edge_of(pooled[:, :, 0], pooled[:, :, -1])
        skip, coarse = half_level(place, pooled, edge, w_half.reshape(9, 3, w_half.shape[3], w_half.shape[4]))
        own_y = coarse.shape[2]

        column = jnp.pad(extend(coarse, "gy", gy, 2, 1), ((0, 0), (0, 0), (0, 6 - own_y), (0, 0)))
        column = jnp.broadcast_to(column[None], (gx * gz,) + column.shape)
        column = lax.all_to_all(column, ("gx", "gz"), 0, 0)
        first = bottom_in(place, column, w_in)
        first = lax.all_to_all(first, "gx", 0, 0)
        first = extend(first, "gy", gy, 3, 2)
        second = bottom_out(place, first, w_out)
        second = lax.all_to_all(second, "gx", 0, 0)

        around = extend(skip, "gx", gx, 0, 1)
        around = extend(around, "gy", gy, 1, 1)
        side = edge_of(around[:, :, 0], around[:, :, -1])
        side = jnp.pad(side, ((0, 0), (0, -side.shape[1] % 16), (0, 0)))
        return decode(place, second, around, side, w_up)

    space = P("gx", "gy", "gz", None)
    filters = P(None, None, None, None, "gx")
    return jax.shard_map(
        local,
        mesh=mesh,
        in_specs=(space, P(), P(), filters, filters, P()),
        out_specs=space,
        check_vma=False,
    )
```

```python
import jax
import jax.numpy as jnp
from jax import lax
from jax.experimental import pallas as pl
from jax.experimental.pallas import tpu as pltpu
from jax.sharding import PartitionSpec as P


def swaps(low, high, axis, count):
    both = isinstance(axis, tuple)
    even = lax.axis_index(axis[0] if both else axis) % 2 == 0
    inner = [(i, i ^ 1) for i in range(count)]
    outer = [(i, (((i + 1) ^ 1) - 1) % count) for i in range(count)]
    if both:
        inner, outer = [[(2 * i + n, 2 * j + 1 - n) for i, j in pairs for n in range(2)] for pairs in (inner, outer)]
    got_in = lax.ppermute(jnp.where(even, high, low), axis, inner)
    got_out = lax.ppermute(jnp.where(even, low, high), axis, outer)
    return got_in, got_out


def ordered(got_in, got_out, axis):
    even = lax.axis_index(axis) % 2 == 0
    return jnp.where(even, got_out, got_in), jnp.where(even, got_in, got_out)


def halo(field, axis, count, dim, width):
    place = lax.axis_index(axis)
    size = field.shape[dim]
    low = lax.slice_in_dim(field, 0, width, axis=dim)
    high = lax.slice_in_dim(field, size - width, size, axis=dim)
    below, above = ordered(*swaps(low, high, axis, count), axis)
    zero = jnp.zeros_like(low)
    return jnp.where(place > 0, below, zero), jnp.where(place < count - 1, above, zero)


def extend(field, axis, count, dim, width):
    below, above = halo(field, axis, count, dim, width)
    return jnp.concatenate([below, field, above], axis=dim)


def half_level(place, field, edge, weights):
    full_x, full_y, size_z, channels = field.shape
    size_x, size_y = full_x - 2, full_y - 2
    filters = weights.shape[-1]
    rows, extra = size_x * size_y * size_z, size_x * size_y

    def body(place_ref, field_ref, edge_ref, weights_ref, out_ref, coarse_ref, rows_ref, coarse_rows_ref):
        first = place_ref[2] == 0
        edge_plane = edge_ref[...].astype(jnp.float32)
        blocks = []
        for dx in range(3):
            for dy in range(3):
                main = field_ref[dx : dx + size_x, dy : dy + size_y].astype(jnp.float32).reshape(rows, channels)
                side = edge_plane[dx : dx + size_x, dy : dy + size_y].reshape(extra, channels)
                blocks.append(jnp.concatenate([main, side], axis=0).astype(jnp.bfloat16))
        block = jnp.concatenate(blocks, axis=1)
        sums = []
        for tap in range(3):
            kernel = weights_ref[:, tap].reshape(9 * channels, filters)
            sums.append(jnp.dot(block, kernel, preferred_element_type=jnp.float32))
        total = jnp.maximum(join_taps(first, sums, extra, size_z), 0.0)
        out_ref[...] = total.reshape(size_x, size_y, size_z, filters).astype(out_ref.dtype)
        total = jnp.max(total.reshape(size_x // 2, 2, size_y // 2, 2, size_z, filters), axis=(1, 3))
        count = size_y // 2
        for part in range(filters // 128):
            rows_ref[...] = total[..., 128 * part : 128 * part + 128].reshape(rows // 4, 128)
            for x in range(size_x // 2):
                for z in range(size_z // 2):
                    start = x * count * size_z + 2 * z
                    pooled = jnp.maximum(
                        rows_ref[pl.ds(start, count, stride=size_z), :], rows_ref[pl.ds(start + 1, count, stride=size_z), :]
                    )
                    coarse_rows_ref[x, count * z : count * z + count, 128 * part : 128 * part + 128] = pooled
        coarse_ref[...] = coarse_rows_ref[...].astype(coarse_ref.dtype)

    return pl.pallas_call(
        body,
        in_specs=[pl.BlockSpec(memory_space=pltpu.SMEM)] + [pl.BlockSpec(memory_space=pltpu.VMEM)] * 3,
        out_specs=[pl.BlockSpec(memory_space=pltpu.VMEM)] * 2,
        out_shape=[
            jax.ShapeDtypeStruct((size_x, size_y, size_z, filters), jnp.bfloat16),
            jax.ShapeDtypeStruct((size_x // 2, size_z * size_y // 4, filters), jnp.bfloat16),
        ],
        scratch_shapes=[
            pltpu.VMEM((rows // 4, 128), jnp.float32),
            pltpu.VMEM((size_x // 2, size_z * size_y // 4, filters), jnp.float32),
        ],
        compiler_params=pltpu.CompilerParams(vmem_limit_bytes=12 << 20),
        name="half_level",
    )(place, field, edge, weights)


def join_taps(first, sums, groups, size_z):
    rows, filters = groups * size_z, sums[0].shape[-1]
    low, mid, high = [total[:rows].reshape(groups, size_z, filters) for total in sums]
    below = jnp.where(first, 0.0, sums[0][rows : rows + groups])
    above = jnp.where(first, sums[2][rows : rows + groups], 0.0)
    index = lax.broadcasted_iota(jnp.int32, (groups, size_z, filters), 1)
    down = jnp.where(index == 0, below[:, None, :], pltpu.roll(low, 1, 1))
    up = jnp.where(index == size_z - 1, above[:, None, :], pltpu.roll(high, size_z - 1, 1))
    return down + mid + up


def encode(place, own, x_in, x_out, y_in, y_out, edge, weights):
    own_x, own_y, size_z, channels = own.shape
    reach = x_in.shape[0]
    full_x, full_y = own_x + 2 * reach, own_y + 2 * reach
    size_x, size_y = full_x - 2, full_y - 2
    filters = weights.shape[-1] // 2
    rows, extra = size_y * size_z, size_y + (-size_y % 16)
    pool_y, pool_z = size_y // 2, size_z // 2

    def body(
        place_ref, own_ref, x_in_ref, x_out_ref, y_in_ref, y_out_ref, edge_ref, weights_ref, out_ref, field_ref, side_ref, rows_ref
    ):
        even_x, even_y = place_ref[0] % 2 == 0, place_ref[1] % 2 == 0
        low_x, high_x = place_ref[0] > 0, place_ref[0] < place_ref[3]
        low_y, high_y = place_ref[1] > 0, place_ref[1] < place_ref[4]
        nil = jnp.bfloat16(0)
        inner_y = slice(reach, reach + own_y)
        below, above = jnp.where(even_x, x_out_ref[...], x_in_ref[...]), jnp.where(even_x, x_in_ref[...], x_out_ref[...])
        field_ref[:reach, inner_y] = jnp.where(low_x, below, nil)
        field_ref[reach + own_x :, inner_y] = jnp.where(high_x, above, nil)
        field_ref[reach : reach + own_x, inner_y] = own_ref[...]
        for x in range(full_x):
            here_low, here_high = low_y, high_y
            if x < reach:
                here_low, here_high = low_y & low_x, high_y & low_x
            if x >= reach + own_x:
                here_low, here_high = low_y & high_x, high_y & high_x
            below, above = jnp.where(even_y, y_out_ref[x], y_in_ref[x]), jnp.where(even_y, y_in_ref[x], y_out_ref[x])
            field_ref[x, :reach] = jnp.where(here_low, below, nil)
            field_ref[x, reach + own_y :] = jnp.where(here_high, above, nil)
            line = lax.broadcasted_iota(jnp.int32, (full_y, channels), 0)
            inside = ((line >= reach) | low_y) & ((line < reach + own_y) | high_y)
            if x < reach:
                inside = inside & low_x
            if x >= reach + own_x:
                inside = inside & high_x
            plane = jnp.where(inside, edge_ref[x].astype(jnp.float32), 0.0)
            for dy in range(3):
                side_ref[dy, x, :size_y] = plane[dy : dy + size_y]
                side_ref[dy, x, size_y:] = jnp.zeros((extra - size_y, channels), jnp.float32)

        first = place_ref[2] == 0
        line = lax.broadcasted_iota(jnp.int32, (pool_y, pool_z, filters), 0)
        inside_y = ((line > 0) | low_y) & ((line < pool_y - 1) | high_y)
        for pair in range(size_x // 2):
            blocks = []
            for plane in range(4):
                for dy in range(3):
                    main = field_ref[2 * pair + plane, dy : dy + size_y].reshape(rows, channels)
                    side = side_ref[dy, 2 * pair + plane].astype(jnp.bfloat16)
                    blocks.append(jnp.concatenate([main, side], axis=0))
            block = jnp.concatenate(blocks, axis=1)
            sums = []
            for tap in range(3):
                kernel = weights_ref[:, :, tap].reshape(12 * channels, 2 * filters)
                sums.append(jnp.dot(block, kernel, preferred_element_type=jnp.float32))
            total = jnp.maximum(join_taps(first, sums, size_y, size_z), 0.0)
            total = jnp.maximum(total[..., :filters], total[..., filters:])
            total = jnp.max(total.reshape(pool_y, 2, size_z, filters), axis=1)
            rows_ref[...] = total.reshape(pool_y * size_z, filters)
            total = jnp.maximum(
                rows_ref[pl.ds(0, pool_y * pool_z, stride=2), :], rows_ref[pl.ds(1, pool_y * pool_z, stride=2), :]
            ).reshape(pool_y, pool_z, filters)
            inside = inside_y
            if pair == 0:
                inside = inside & low_x
            if pair == size_x // 2 - 1:
                inside = inside & high_x
            out_ref[pair] = jnp.where(inside, total, 0.0).astype(out_ref.dtype)

    return pl.pallas_call(
        body,
        in_specs=[pl.BlockSpec(memory_space=pltpu.SMEM)] + [pl.BlockSpec(memory_space=pltpu.VMEM)] * 7,
        out_specs=pl.BlockSpec(memory_space=pltpu.VMEM),
        out_shape=jax.ShapeDtypeStruct((size_x // 2, pool_y, pool_z, filters), jnp.bfloat16),
        scratch_shapes=[
            pltpu.VMEM((full_x, full_y, size_z, channels), jnp.bfloat16),
            pltpu.VMEM((3, full_x, extra, channels), jnp.float32),
            pltpu.VMEM((pool_y * size_z, filters), jnp.float32),
        ],
        compiler_params=pltpu.CompilerParams(vmem_limit_bytes=16 << 20),
        name="encode",
    )(place, own, x_in, x_out, y_in, y_out, edge, weights)


def paired(weights):
    grow = [(0, 0)] * 4
    return jnp.concatenate([jnp.pad(weights, [(0, 1)] + grow), jnp.pad(weights, [(1, 0)] + grow)], axis=4)


def halves(pair_low, pair_high):
    lane = lax.broadcasted_iota(jnp.int32, pair_low.shape, pair_low.ndim - 1)
    axis = pair_low.ndim - 1
    even = jnp.where(lane < 64, pair_low, pltpu.roll(pair_high, 64, axis))
    odd = jnp.where(lane < 64, pltpu.roll(pair_low, 64, axis), pair_high)
    return even, odd


def side_by_side(even, odd):
    lane = lax.broadcasted_iota(jnp.int32, even.shape, even.ndim - 1)
    return jnp.where(lane < 64, even, pltpu.roll(odd, 64, even.ndim - 1))


def column_product(pad_ref, weights_ref, first, start, planes, size_z):
    channels = pad_ref.shape[-1]
    rows = planes * size_z * 8
    blocks = []
    for dx in range(3):
        for dz in range(3):
            block = pad_ref[first + dx : first + dx + planes, pl.ds(start + dz, size_z)]
            blocks.append(block.reshape(rows, channels).astype(jnp.bfloat16))
    block = jnp.concatenate(blocks, axis=1)
    total = jnp.dot(block, weights_ref[...].reshape(9 * channels, 256), preferred_element_type=jnp.float32)
    low = total[:, :128].reshape(planes * size_z, 8, 128)
    mid = pltpu.roll(total[:, :128], 64, 1).reshape(planes * size_z, 8, 128)
    high = total[:, 128:].reshape(planes * size_z, 8, 128)
    total = pltpu.roll(low, 1, 1) + mid + pltpu.roll(high, 7, 1)
    return jnp.maximum(total, 0.0).reshape(planes, size_z, 8, 128)


def bottom_in(place, field, weights):
    count, own_x, lines, channels = field.shape
    devices = count // 2
    own_z = size_y = 4
    size_x, all_z, size_z = devices * own_x, 2 * own_z, own_z + 2

    def body(place_ref, field_ref, weights_ref, out_ref, pad_ref):
        zero = jnp.zeros((all_z + 2, 8, channels), jnp.float32)
        pad_ref[0] = zero
        pad_ref[size_x + 1] = zero
        for x in range(size_x):
            pad_ref[x + 1, 0] = zero[0]
            pad_ref[x + 1, all_z + 1] = zero[0]
        for i in range(devices):
            for half in range(2):
                for x in range(own_x):
                    block = field_ref[2 * i + half, x].astype(jnp.float32)
                    for z in range(own_z):
                        to = (1 + own_x * i + x, 1 + own_z * half + z)
                        pad_ref[*to, 0:1] = block[own_z * size_y + z : own_z * size_y + z + 1]
                        pad_ref[*to, 1 : size_y + 1] = block[size_y * z : size_y * z + size_y]
                        line = own_z * (size_y + 1) + z
                        pad_ref[*to, size_y + 1 : size_y + 2] = block[line : line + 1]
                        pad_ref[*to, size_y + 2 :] = zero[0, size_y + 2 :]
        start = 2 * place_ref[2]
        for first in range(0, size_x, 4):
            total = column_product(pad_ref, weights_ref, first, start, 4, size_z)
            for pair in range(2):
                both = side_by_side(total[2 * pair], total[2 * pair + 1])[:, 1 : size_y + 1].astype(out_ref.dtype)
                for i in range(devices):
                    out_ref[i, first // 2 + pair] = both

    return pl.pallas_call(
        body,
        in_specs=[pl.BlockSpec(memory_space=pltpu.SMEM)] + [pl.BlockSpec(memory_space=pltpu.VMEM)] * 2,
        out_specs=pl.BlockSpec(memory_space=pltpu.VMEM),
        out_shape=jax.ShapeDtypeStruct((devices, size_x // 2, size_z, size_y, 128), jnp.bfloat16),
        scratch_shapes=[pltpu.VMEM((size_x + 2, all_z + 2, 8, channels), jnp.float32)],
        compiler_params=pltpu.CompilerParams(vmem_limit_bytes=12 << 20),
        name="bottom_in",
    )(place, field, weights)


def bottom_out(place, field, weights):
    devices, pairs, size_z, _, _ = field.shape
    size_x, channels = 2 * pairs, 64 * devices
    own_x = size_x // devices

    def body(place_ref, field_ref, weights_ref, out_ref, pad_ref, total_ref):
        zero = jnp.zeros((size_z + 2, 8, channels), jnp.float32)
        for ref in (pad_ref, total_ref):
            wide = ref.shape[-1]
            ref[0] = zero[..., :wide]
            ref[size_x + 1] = zero[..., :wide]
            for x in range(size_x):
                ref[x + 1, 0] = zero[0, :, :wide]
                ref[x + 1, size_z + 1] = zero[0, :, :wide]
        for k in range(devices // 2):
            for pair in range(pairs):
                low, high = [field_ref[2 * k + i, pair].astype(jnp.float32) for i in range(2)]
                even, odd = halves(low, high)
                pad_ref[1 + 2 * pair, 1 : size_z + 1, :, 128 * k : 128 * k + 128] = even
                pad_ref[2 + 2 * pair, 1 : size_z + 1, :, 128 * k : 128 * k + 128] = odd
        for first in range(0, size_x, 4):
            total = column_product(pad_ref, weights_ref, first, 0, 4, size_z)
            total_ref[1 + first : 5 + first, 1 : size_z + 1] = total
        start = 2 * place_ref[2]
        for i in range(size_x // 2 + 1):
            low, high = [total_ref[2 * i + n, pl.ds(start, size_z)] for n in range(2)]
            both = side_by_side(low, high).astype(out_ref.dtype)
            if i < devices:
                out_ref[i, 0] = both
            if i > 0:
                out_ref[i - 1, 1] = both

    return pl.pallas_call(
        body,
        in_specs=[pl.BlockSpec(memory_space=pltpu.SMEM)] + [pl.BlockSpec(memory_space=pltpu.VMEM)] * 2,
        out_specs=pl.BlockSpec(memory_space=pltpu.VMEM),
        out_shape=jax.ShapeDtypeStruct((devices, own_x, size_z, 8, 128), jnp.bfloat16),
        scratch_shapes=[
            pltpu.VMEM((size_x + 2, size_z + 2, 8, channels), jnp.float32),
            pltpu.VMEM((size_x + 2, size_z + 2, 8, 128), jnp.float32),
        ],
        compiler_params=pltpu.CompilerParams(vmem_limit_bytes=16 << 20),
        name="bottom_out",
    )(place, field, weights)


def decode(place, bottom, skip, edge, weights):
    devices, pairs, coarse_z, _, _ = bottom.shape
    full_x, full_y, size_z, skip_channels = skip.shape
    size_x, size_y = full_x - 2, full_y - 2
    channels = 64 * devices + skip_channels
    filters = weights.shape[-1]
    rows, extra = size_x * size_y * size_z, size_x * size_y
    weights = weights.reshape(9, 3, channels, filters)

    def body(place_ref, bottom_ref, skip_ref, edge_ref, weights_ref, out_ref, main_ref, side_ref, sums_ref):
        first = place_ref[2] == 0
        planes = [[] for _ in range(2 * pairs)]
        for k in range(devices // 2):
            for pair in range(pairs):
                low, high = [bottom_ref[2 * k + i, pair].astype(jnp.float32) for i in range(2)]
                even, odd = halves(low, high)
                planes[2 * pair].append(even.reshape(coarse_z * 8, 128))
                planes[2 * pair + 1].append(odd.reshape(coarse_z * 8, 128))

        def choice(y, z, source):
            line = (y + 1) // 2 + 1
            inside = ((line > 1) | (place_ref[1] > 0)) & ((line < coarse_z) | (place_ref[1] < place_ref[4]))
            return jnp.where((source == z * 8 + line) & inside, 1.0, 0.0).astype(jnp.bfloat16)

        shape = (full_y * size_z, coarse_z * 8)
        row = lax.broadcasted_iota(jnp.int32, shape, 0)
        spread = choice(row // size_z, row % size_z // 2 + 1, lax.broadcasted_iota(jnp.int32, shape, 1))
        shape = (16, coarse_z * 8)
        row = lax.broadcasted_iota(jnp.int32, shape, 0)
        other = jnp.where(first, coarse_z - 1, 0)
        spread_edge = choice(row, other, lax.broadcasted_iota(jnp.int32, shape, 1))
        for plane in range(2 * pairs):
            coarse = jnp.concatenate(planes[plane], axis=1).astype(jnp.bfloat16)
            fine = jnp.dot(spread, coarse, preferred_element_type=jnp.float32)
            fine_edge = jnp.dot(spread_edge, coarse, preferred_element_type=jnp.float32)
            for x in range(full_x):
                if (x + 1) // 2 != plane:
                    continue
                joined = jnp.concatenate([fine, skip_ref[x].astype(jnp.float32).reshape(full_y * size_z, skip_channels)], axis=1)
                joined_edge = jnp.concatenate([fine_edge, edge_ref[x].astype(jnp.float32)], axis=1)
                for dy in range(3):
                    main_ref[dy, x] = joined[8 * dy : 8 * dy + size_y * size_z].astype(jnp.bfloat16)
                    side_ref[dy, x] = joined_edge[dy : dy + size_y]
        for dx in range(3):
            blocks = []
            for dy in range(3):
                main = main_ref[dy, dx : dx + size_x].reshape(rows, channels)
                side = side_ref[dy, dx : dx + size_x].reshape(extra, channels).astype(jnp.bfloat16)
                blocks.append(jnp.concatenate([main, side], axis=0))
            block = jnp.concatenate(blocks, axis=1)
            for tap in range(3):
                kernel = weights_ref[3 * dx : 3 * dx + 3, tap].reshape(3 * channels, filters)
                product = jnp.dot(block, kernel, preferred_element_type=jnp.float32)
                if dx == 0:
                    sums_ref[tap] = product
                else:
                    sums_ref[tap] += product
        total = join_taps(first, [sums_ref[tap] for tap in range(3)], extra, size_z)
        out_ref[...] = total.reshape(size_x, size_y, size_z, filters).astype(out_ref.dtype)

    return pl.pallas_call(
        body,
        in_specs=[pl.BlockSpec(memory_space=pltpu.SMEM)]
        + [pl.BlockSpec(memory_space=pltpu.VMEM)] * 4,
        out_specs=pl.BlockSpec(memory_space=pltpu.VMEM),
        out_shape=jax.ShapeDtypeStruct((size_x, size_y, size_z, filters), jnp.bfloat16),
        scratch_shapes=[
            pltpu.VMEM((3, full_x, size_y * size_z, channels), jnp.bfloat16),
            pltpu.VMEM((3, full_x, size_y, channels), jnp.float32),
            pltpu.VMEM((3, rows + extra, filters), jnp.float32),
        ],
        compiler_params=pltpu.CompilerParams(vmem_limit_bytes=16 << 20),
        name="decode",
    )(place, bottom, skip, edge, weights)


def beside(weights):
    channels, filters = weights.shape[3:]
    weights = weights.transpose(0, 2, 3, 1, 4).reshape(9, channels, 3 * filters)
    return jnp.pad(weights, ((0, 0), (0, 0), (0, 256 - 3 * filters)))


def solution(mesh):
    gx, gy, gz = mesh.shape["gx"], mesh.shape["gy"], mesh.shape["gz"]

    def local(volume, w_full, w_half, w_bottom_in, w_bottom_out, w_up):
        place_z = lax.axis_index("gz")
        place = jnp.stack([lax.axis_index("gx"), lax.axis_index("gy"), place_z, jnp.int32(gx - 1), jnp.int32(gy - 1)])
        swap = [(0, 1), (1, 0)]

        def edge_of(plane_low, plane_high):
            return lax.ppermute(jnp.where(place_z == 0, plane_high, plane_low), "gz", swap)

        x_in, x_out = swaps(volume[:3], volume[-3:], "gx", gx)
        w_pair, w_out = paired(w_full), beside(w_bottom_out)
        x_in, x_out, w_pair, w_out, w_bottom_in = lax.optimization_barrier((x_in, x_out, w_pair, w_out, w_bottom_in))
        below, above = ordered(x_in, x_out, "gx")
        y_low = jnp.concatenate([below[:, :3], volume[:, :3], above[:, :3]], axis=0)
        y_high = jnp.concatenate([below[:, -3:], volume[:, -3:], above[:, -3:]], axis=0)
        y_in, y_out = swaps(y_low, y_high, "gy", gy)

        def outer_plane(block):
            return jnp.where(place_z == 0, block[:, :, -1], block[:, :, 0])

        edge = jnp.concatenate([outer_plane(below), outer_plane(volume), outer_plane(above)], axis=0)
        edge_in, edge_out = swaps(edge[:, :3], edge[:, -3:], ("gy", "gz"), gy)
        edge = lax.ppermute(edge, "gz", swap)
        edge_low, edge_high = ordered(edge_in, edge_out, "gy")
        edge = jnp.concatenate([edge_low, edge, edge_high], axis=1)
        edge, w_in = lax.optimization_barrier((edge, beside(w_bottom_in)))
        pooled = encode(place, volume, x_in, x_out, y_in, y_out, edge, w_pair)

        edge = edge_of(pooled[:, :, 0], pooled[:, :, -1])
        skip, coarse = half_level(place, pooled, edge, w_half.reshape(9, 3, w_half.shape[3], w_half.shape[4]))
        lines = coarse.reshape(coarse.shape[0], 4, 4, coarse.shape[2])
        below, above = halo(lines, "gy", gy, 2, 1)
        column = jnp.concatenate([coarse, below[:, :, 0], above[:, :, 0]], axis=1)
        column = jnp.broadcast_to(column[None], (gx * gz,) + column.shape)
        column = lax.all_to_all(column, ("gx", "gz"), 0, 0)
        first = bottom_in(place, column, w_in)
        first = lax.all_to_all(first, "gx", 0, 0)
        first = extend(first, "gy", gy, 3, 2)
        second = bottom_out(place, first, w_out)
        second = lax.all_to_all(second, "gx", 0, 0)

        around = extend(skip, "gx", gx, 0, 1)
        around = extend(around, "gy", gy, 1, 1)
        side = edge_of(around[:, :, 0], around[:, :, -1])
        side = jnp.pad(side, ((0, 0), (0, -side.shape[1] % 16), (0, 0)))
        return decode(place, second, around, side, w_up)

    space = P("gx", "gy", "gz", None)
    filters = P(None, None, None, None, "gx")
    return jax.shard_map(
        local,
        mesh=mesh,
        in_specs=(space, P(), P(), filters, filters, P()),
        out_specs=space,
        check_vma=False,
    )
```

```python
import jax
import jax.numpy as jnp
from jax import lax
from jax.experimental import pallas as pl
from jax.experimental.pallas import tpu as pltpu
from jax.sharding import PartitionSpec as P


def send(inner_block, outer_block, axis, count):
    inner = [(i, i ^ 1) for i in range(count)]
    outer = [(i, (((i + 1) ^ 1) - 1) % count) for i in range(count)]
    return lax.ppermute(inner_block, axis, inner), lax.ppermute(outer_block, axis, outer)


def swaps(low, high, axis, count):
    even = lax.axis_index(axis) % 2 == 0
    return send(jnp.where(even, high, low), jnp.where(even, low, high), axis, count)


def ordered(got_in, got_out, axis):
    even = lax.axis_index(axis) % 2 == 0
    return jnp.where(even, got_out, got_in), jnp.where(even, got_in, got_out)


def halo(field, axis, count, dim, width):
    place = lax.axis_index(axis)
    size = field.shape[dim]
    low = lax.slice_in_dim(field, 0, width, axis=dim)
    high = lax.slice_in_dim(field, size - width, size, axis=dim)
    below, above = ordered(*swaps(low, high, axis, count), axis)
    zero = jnp.zeros_like(low)
    return jnp.where(place > 0, below, zero), jnp.where(place < count - 1, above, zero)


def extend(field, axis, count, dim, width):
    below, above = halo(field, axis, count, dim, width)
    return jnp.concatenate([below, field, above], axis=dim)


def half_level(place, field, edge, weights):
    full_x, full_y, size_z, channels = field.shape
    size_x, size_y = full_x - 2, full_y - 2
    filters = weights.shape[-1]
    rows, extra = size_x * size_y * size_z, size_x * size_y

    def body(place_ref, field_ref, edge_ref, weights_ref, out_ref, coarse_ref, rows_ref, coarse_rows_ref):
        first = place_ref[2] == 0
        edge_plane = edge_ref[...].astype(jnp.float32)
        blocks = []
        for dx in range(3):
            for dy in range(3):
                main = field_ref[dx : dx + size_x, dy : dy + size_y].astype(jnp.float32).reshape(rows, channels)
                side = edge_plane[dx : dx + size_x, dy : dy + size_y].reshape(extra, channels)
                blocks.append(jnp.concatenate([main, side], axis=0).astype(jnp.bfloat16))
        block = jnp.concatenate(blocks, axis=1)
        sums = []
        for tap in range(3):
            kernel = weights_ref[:, tap].reshape(9 * channels, filters)
            sums.append(jnp.dot(block, kernel, preferred_element_type=jnp.float32))
        total = jnp.maximum(join_taps(first, sums, extra, size_z), 0.0)
        out_ref[...] = total.reshape(size_x, size_y, size_z, filters).astype(out_ref.dtype)
        total = jnp.max(total.reshape(size_x // 2, 2, size_y // 2, 2, size_z, filters), axis=(1, 3))
        count = size_y // 2
        for part in range(filters // 128):
            rows_ref[...] = total[..., 128 * part : 128 * part + 128].reshape(rows // 4, 128)
            for x in range(size_x // 2):
                for z in range(size_z // 2):
                    start = x * count * size_z + 2 * z
                    pooled = jnp.maximum(
                        rows_ref[pl.ds(start, count, stride=size_z), :], rows_ref[pl.ds(start + 1, count, stride=size_z), :]
                    )
                    coarse_rows_ref[x, count * z : count * z + count, 128 * part : 128 * part + 128] = pooled
        coarse_ref[...] = coarse_rows_ref[...].astype(coarse_ref.dtype)

    return pl.pallas_call(
        body,
        in_specs=[pl.BlockSpec(memory_space=pltpu.SMEM)] + [pl.BlockSpec(memory_space=pltpu.VMEM)] * 3,
        out_specs=[pl.BlockSpec(memory_space=pltpu.VMEM)] * 2,
        out_shape=[
            jax.ShapeDtypeStruct((size_x, size_y, size_z, filters), jnp.bfloat16),
            jax.ShapeDtypeStruct((size_x // 2, size_z * size_y // 4, filters), jnp.bfloat16),
        ],
        scratch_shapes=[
            pltpu.VMEM((rows // 4, 128), jnp.float32),
            pltpu.VMEM((size_x // 2, size_z * size_y // 4, filters), jnp.float32),
        ],
        compiler_params=pltpu.CompilerParams(vmem_limit_bytes=12 << 20),
        name="half_level",
    )(place, field, edge, weights)


def join_taps(first, sums, groups, size_z):
    rows, filters = groups * size_z, sums[0].shape[-1]
    low, mid, high = [total[:rows].reshape(groups, size_z, filters) for total in sums]
    below = jnp.where(first, 0.0, sums[0][rows : rows + groups])
    above = jnp.where(first, sums[2][rows : rows + groups], 0.0)
    index = lax.broadcasted_iota(jnp.int32, (groups, size_z, filters), 1)
    down = jnp.where(index == 0, below[:, None, :], pltpu.roll(low, 1, 1))
    up = jnp.where(index == size_z - 1, above[:, None, :], pltpu.roll(high, size_z - 1, 1))
    return down + mid + up


def encode(place, own, x_in, x_out, y_in, y_out, edge, weights):
    own_x, own_y, size_z, channels = own.shape
    reach = x_in.shape[0]
    full_x, full_y = own_x + 2 * reach, own_y + 2 * reach
    size_x, size_y = full_x - 2, full_y - 2
    filters = weights.shape[-1] // 2
    rows, extra = size_y * size_z, size_y + (-size_y % 16)
    pool_y, pool_z = size_y // 2, size_z // 2

    def body(
        place_ref, own_ref, x_in_ref, x_out_ref, y_in_ref, y_out_ref, edge_ref, weights_ref, out_ref, field_ref, side_ref, rows_ref
    ):
        even_x, even_y = place_ref[0] % 2 == 0, place_ref[1] % 2 == 0
        low_x, high_x = place_ref[0] > 0, place_ref[0] < place_ref[3]
        low_y, high_y = place_ref[1] > 0, place_ref[1] < place_ref[4]
        nil = jnp.bfloat16(0)
        inner_y = slice(reach, reach + own_y)
        below, above = jnp.where(even_x, x_out_ref[...], x_in_ref[...]), jnp.where(even_x, x_in_ref[...], x_out_ref[...])
        field_ref[:reach, inner_y] = jnp.where(low_x, below, nil)
        field_ref[reach + own_x :, inner_y] = jnp.where(high_x, above, nil)
        field_ref[reach : reach + own_x, inner_y] = own_ref[...]
        for x in range(full_x):
            here_low, here_high = low_y, high_y
            if x < reach:
                here_low, here_high = low_y & low_x, high_y & low_x
            if x >= reach + own_x:
                here_low, here_high = low_y & high_x, high_y & high_x
            below, above = jnp.where(even_y, y_out_ref[x], y_in_ref[x]), jnp.where(even_y, y_in_ref[x], y_out_ref[x])
            field_ref[x, :reach] = jnp.where(here_low, below, nil)
            field_ref[x, reach + own_y :] = jnp.where(here_high, above, nil)
            line = lax.broadcasted_iota(jnp.int32, (full_y, channels), 0)
            inside = ((line >= reach) | low_y) & ((line < reach + own_y) | high_y)
            if x < reach:
                inside = inside & low_x
            if x >= reach + own_x:
                inside = inside & high_x
            plane = jnp.where(inside, edge_ref[x].astype(jnp.float32), 0.0)
            for dy in range(3):
                side_ref[dy, x, :size_y] = plane[dy : dy + size_y]
                side_ref[dy, x, size_y:] = jnp.zeros((extra - size_y, channels), jnp.float32)

        first = place_ref[2] == 0
        line = lax.broadcasted_iota(jnp.int32, (pool_y, pool_z, filters), 0)
        inside_y = ((line > 0) | low_y) & ((line < pool_y - 1) | high_y)
        for pair in range(size_x // 2):
            blocks = []
            for plane in range(4):
                for dy in range(3):
                    main = field_ref[2 * pair + plane, dy : dy + size_y].reshape(rows, channels)
                    side = side_ref[dy, 2 * pair + plane].astype(jnp.bfloat16)
                    blocks.append(jnp.concatenate([main, side], axis=0))
            block = jnp.concatenate(blocks, axis=1)
            sums = []
            for tap in range(3):
                kernel = weights_ref[:, :, tap].reshape(12 * channels, 2 * filters)
                sums.append(jnp.dot(block, kernel, preferred_element_type=jnp.float32))
            total = jnp.maximum(join_taps(first, sums, size_y, size_z), 0.0)
            total = jnp.maximum(total[..., :filters], total[..., filters:])
            total = jnp.max(total.reshape(pool_y, 2, size_z, filters), axis=1)
            rows_ref[...] = total.reshape(pool_y * size_z, filters)
            total = jnp.maximum(
                rows_ref[pl.ds(0, pool_y * pool_z, stride=2), :], rows_ref[pl.ds(1, pool_y * pool_z, stride=2), :]
            ).reshape(pool_y, pool_z, filters)
            inside = inside_y
            if pair == 0:
                inside = inside & low_x
            if pair == size_x // 2 - 1:
                inside = inside & high_x
            out_ref[pair] = jnp.where(inside, total, 0.0).astype(out_ref.dtype)

    return pl.pallas_call(
        body,
        in_specs=[pl.BlockSpec(memory_space=pltpu.SMEM)] + [pl.BlockSpec(memory_space=pltpu.VMEM)] * 7,
        out_specs=pl.BlockSpec(memory_space=pltpu.VMEM),
        out_shape=jax.ShapeDtypeStruct((size_x // 2, pool_y, pool_z, filters), jnp.bfloat16),
        scratch_shapes=[
            pltpu.VMEM((full_x, full_y, size_z, channels), jnp.bfloat16),
            pltpu.VMEM((3, full_x, extra, channels), jnp.float32),
            pltpu.VMEM((pool_y * size_z, filters), jnp.float32),
        ],
        compiler_params=pltpu.CompilerParams(vmem_limit_bytes=16 << 20),
        name="encode",
    )(place, own, x_in, x_out, y_in, y_out, edge, weights)


def prepare(w_full, w_bottom_in, w_bottom_out):
    channels, filters = w_full.shape[3:]

    def body(full_ref, in_ref, out_ref, pair_ref, beside_in_ref, beside_out_ref):
        zero = jnp.zeros((3, 3, channels, filters), jnp.bfloat16)
        for plane in range(4):
            pair_ref[plane, :, :, :, :filters] = full_ref[plane] if plane < 3 else zero
            pair_ref[plane, :, :, :, filters:] = full_ref[plane - 1] if plane > 0 else zero
        for ref, to in ((in_ref, beside_in_ref), (out_ref, beside_out_ref)):
            depth = ref.shape[3]
            gap = jnp.zeros((depth, 64), jnp.float32)
            for dx in range(3):
                for dz in range(3):
                    first, second, third = [ref[dx, dy, dz].astype(jnp.float32) for dy in range(3)]
                    to[3 * dx + dz, :, :128] = jnp.concatenate([first, second], axis=1).astype(jnp.bfloat16)
                    to[3 * dx + dz, :, 128:] = jnp.concatenate([third, gap], axis=1).astype(jnp.bfloat16)

    return pl.pallas_call(
        body,
        in_specs=[pl.BlockSpec(memory_space=pltpu.VMEM)] * 3,
        out_specs=[pl.BlockSpec(memory_space=pltpu.VMEM)] * 3,
        out_shape=[jax.ShapeDtypeStruct((4, 3, 3, channels, 2 * filters), jnp.bfloat16)]
        + [jax.ShapeDtypeStruct((9, w.shape[3], 256), jnp.bfloat16) for w in (w_bottom_in, w_bottom_out)],
        compiler_params=pltpu.CompilerParams(vmem_limit_bytes=8 << 20),
        name="prepare",
    )(w_full, w_bottom_in, w_bottom_out)


def pack_y(place, own, x_in, x_out):
    own_x, own_y, size_z, channels = own.shape
    reach = x_in.shape[0]
    full_x = own_x + 2 * reach

    def body(place_ref, own_ref, x_in_ref, x_out_ref, inner_ref, outer_ref, plane_ref, rows_ref):
        even_x, even_y, first = place_ref[0] % 2 == 0, place_ref[1] % 2 == 0, place_ref[2] == 0
        below = jnp.where(even_x, x_out_ref[...], x_in_ref[...])
        above = jnp.where(even_x, x_in_ref[...], x_out_ref[...])
        for start, block in ((0, below), (reach, own_ref[...]), (reach + own_x, above)):
            size = block.shape[0]
            low, high = block[:, :reach], block[:, own_y - reach :]
            inner_ref[start : start + size] = jnp.where(even_y, high, low)
            outer_ref[start : start + size] = jnp.where(even_y, low, high)
            block = block.astype(jnp.float32)
            edge = jnp.where(first, block[:, :, size_z - 1 :], block[:, :, :1])
            for x in range(size):
                for y in range(own_y):
                    rows_ref[start + x, y : y + 1] = edge[x, y]
        plane_ref[...] = rows_ref[...].astype(plane_ref.dtype)

    return pl.pallas_call(
        body,
        in_specs=[pl.BlockSpec(memory_space=pltpu.SMEM)] + [pl.BlockSpec(memory_space=pltpu.VMEM)] * 3,
        out_specs=[pl.BlockSpec(memory_space=pltpu.VMEM)] * 3,
        out_shape=[jax.ShapeDtypeStruct((full_x, reach, size_z, channels), jnp.bfloat16)] * 2
        + [jax.ShapeDtypeStruct((full_x, own_y, channels), jnp.bfloat16)],
        scratch_shapes=[pltpu.VMEM((full_x, own_y, channels), jnp.float32)],
        compiler_params=pltpu.CompilerParams(vmem_limit_bytes=8 << 20),
        name="pack_y",
    )(place, own, x_in, x_out)


def pack_z(place, plane, y_in, y_out):
    full_x, own_y, channels = plane.shape
    reach, size_z = y_in.shape[1:3]
    full_y = own_y + 2 * reach

    def body(place_ref, plane_ref, y_in_ref, y_out_ref, out_ref, rows_ref):
        even_y, first = place_ref[1] % 2 == 0, place_ref[2] == 0
        rows_ref[:, reach : reach + own_y] = plane_ref[...].astype(jnp.float32)
        edges = []
        for ref in (y_in_ref, y_out_ref):
            block = ref[...].astype(jnp.float32)
            edges.append(jnp.where(first, block[:, :, size_z - 1 :], block[:, :, :1]))
        below, above = jnp.where(even_y, edges[1], edges[0]), jnp.where(even_y, edges[0], edges[1])
        for x in range(full_x):
            for y in range(reach):
                rows_ref[x, y : y + 1] = below[x, y]
                rows_ref[x, reach + own_y + y : reach + own_y + y + 1] = above[x, y]
        out_ref[...] = rows_ref[...].astype(out_ref.dtype)

    return pl.pallas_call(
        body,
        in_specs=[pl.BlockSpec(memory_space=pltpu.SMEM)] + [pl.BlockSpec(memory_space=pltpu.VMEM)] * 3,
        out_specs=pl.BlockSpec(memory_space=pltpu.VMEM),
        out_shape=jax.ShapeDtypeStruct((full_x, full_y, channels), jnp.bfloat16),
        scratch_shapes=[pltpu.VMEM((full_x, full_y, channels), jnp.float32)],
        compiler_params=pltpu.CompilerParams(vmem_limit_bytes=8 << 20),
        name="pack_z",
    )(place, plane, y_in, y_out)


def fetch(weights, after):
    def body(weights_ref, after_ref, out_ref, sems):
        copies = [pltpu.make_async_copy(weights_ref.at[i], out_ref.at[i], sems.at[i]) for i in range(9)]
        for copy in copies:
            copy.start()
        for copy in copies:
            copy.wait()

    return pl.pallas_call(
        body,
        in_specs=[pl.BlockSpec(memory_space=pltpu.HBM)] * 2,
        out_specs=pl.BlockSpec(memory_space=pltpu.VMEM),
        out_shape=jax.ShapeDtypeStruct(weights.shape, weights.dtype),
        scratch_shapes=[pltpu.SemaphoreType.DMA((9,))],
        compiler_params=pltpu.CompilerParams(vmem_limit_bytes=12 << 20),
        name="fetch",
    )(weights, after)


def halves(pair_low, pair_high):
    lane = lax.broadcasted_iota(jnp.int32, pair_low.shape, pair_low.ndim - 1)
    axis = pair_low.ndim - 1
    even = jnp.where(lane < 64, pair_low, pltpu.roll(pair_high, 64, axis))
    odd = jnp.where(lane < 64, pltpu.roll(pair_low, 64, axis), pair_high)
    return even, odd


def side_by_side(even, odd):
    lane = lax.broadcasted_iota(jnp.int32, even.shape, even.ndim - 1)
    return jnp.where(lane < 64, even, pltpu.roll(odd, 64, even.ndim - 1))


def column_product(pad_ref, weights_ref, first, start, planes, size_z):
    channels = pad_ref.shape[-1]
    rows = planes * size_z * 8
    blocks = []
    for dx in range(3):
        for dz in range(3):
            block = pad_ref[first + dx : first + dx + planes, pl.ds(start + dz, size_z)]
            blocks.append(block.reshape(rows, channels).astype(jnp.bfloat16))
    block = jnp.concatenate(blocks, axis=1)
    total = jnp.dot(block, weights_ref[...].reshape(9 * channels, 256), preferred_element_type=jnp.float32)
    low = total[:, :128].reshape(planes * size_z, 8, 128)
    mid = pltpu.roll(total[:, :128], 64, 1).reshape(planes * size_z, 8, 128)
    high = total[:, 128:].reshape(planes * size_z, 8, 128)
    total = pltpu.roll(low, 1, 1) + mid + pltpu.roll(high, 7, 1)
    return jnp.maximum(total, 0.0).reshape(planes, size_z, 8, 128)


def bottom_in(place, field, weights):
    count, own_x, lines, channels = field.shape
    devices = count // 2
    own_z = size_y = 4
    size_x, all_z, size_z = devices * own_x, 2 * own_z, own_z + 2

    def body(place_ref, field_ref, weights_ref, out_ref, pad_ref):
        zero = jnp.zeros((all_z + 2, 8, channels), jnp.float32)
        pad_ref[0] = zero
        pad_ref[size_x + 1] = zero
        for x in range(size_x):
            pad_ref[x + 1, 0] = zero[0]
            pad_ref[x + 1, all_z + 1] = zero[0]
        for i in range(devices):
            for half in range(2):
                for x in range(own_x):
                    block = field_ref[2 * i + half, x].astype(jnp.float32)
                    for z in range(own_z):
                        to = (1 + own_x * i + x, 1 + own_z * half + z)
                        pad_ref[*to, 0:1] = block[own_z * size_y + z : own_z * size_y + z + 1]
                        pad_ref[*to, 1 : size_y + 1] = block[size_y * z : size_y * z + size_y]
                        line = own_z * (size_y + 1) + z
                        pad_ref[*to, size_y + 1 : size_y + 2] = block[line : line + 1]
                        pad_ref[*to, size_y + 2 :] = zero[0, size_y + 2 :]
        start = 2 * place_ref[2]
        for first in range(0, size_x, 4):
            total = column_product(pad_ref, weights_ref, first, start, 4, size_z)
            for pair in range(2):
                both = side_by_side(total[2 * pair], total[2 * pair + 1])[:, 1 : size_y + 1].astype(out_ref.dtype)
                for i in range(devices):
                    out_ref[i, first // 2 + pair] = both

    return pl.pallas_call(
        body,
        in_specs=[pl.BlockSpec(memory_space=pltpu.SMEM)] + [pl.BlockSpec(memory_space=pltpu.VMEM)] * 2,
        out_specs=pl.BlockSpec(memory_space=pltpu.VMEM),
        out_shape=jax.ShapeDtypeStruct((devices, size_x // 2, size_z, size_y, 128), jnp.bfloat16),
        scratch_shapes=[pltpu.VMEM((size_x + 2, all_z + 2, 8, channels), jnp.float32)],
        compiler_params=pltpu.CompilerParams(vmem_limit_bytes=12 << 20),
        name="bottom_in",
    )(place, field, weights)


def bottom_out(place, field, y_in, y_out, weights):
    devices, pairs, size_z, _, _ = field.shape
    size_x, channels = 2 * pairs, 64 * devices
    own_x = size_x // devices

    def body(place_ref, field_ref, y_in_ref, y_out_ref, weights_ref, out_ref, pad_ref, total_ref):
        even_y = place_ref[1] % 2 == 0
        low_y, high_y = place_ref[1] > 0, place_ref[1] < place_ref[4]
        zero = jnp.zeros((size_z + 2, 8, channels), jnp.float32)
        for ref in (pad_ref, total_ref):
            wide = ref.shape[-1]
            ref[0] = zero[..., :wide]
            ref[size_x + 1] = zero[..., :wide]
            for x in range(size_x):
                ref[x + 1, 0] = zero[0, :, :wide]
                ref[x + 1, size_z + 1] = zero[0, :, :wide]
        for k in range(devices // 2):
            for pair in range(pairs):
                y_first, y_last = [], []
                for i in range(2):
                    one = y_in_ref[2 * k + i, pair].astype(jnp.float32)
                    other = y_out_ref[2 * k + i, pair].astype(jnp.float32)
                    y_first.append(jnp.where(low_y, jnp.where(even_y, other, one), 0.0))
                    y_last.append(jnp.where(high_y, jnp.where(even_y, one, other), 0.0))
                own = [field_ref[2 * k + i, pair].astype(jnp.float32) for i in range(2)]
                for line, blocks in ((0, y_first), (2, own), (6, y_last)):
                    even, odd = halves(*blocks)
                    lines = slice(line, line + even.shape[1])
                    pad_ref[1 + 2 * pair, 1 : size_z + 1, lines, 128 * k : 128 * k + 128] = even
                    pad_ref[2 + 2 * pair, 1 : size_z + 1, lines, 128 * k : 128 * k + 128] = odd
        for first in range(0, size_x, 4):
            total = column_product(pad_ref, weights_ref, first, 0, 4, size_z)
            total_ref[1 + first : 5 + first, 1 : size_z + 1] = total
        start = 2 * place_ref[2]
        for i in range(size_x // 2 + 1):
            low, high = [total_ref[2 * i + n, pl.ds(start, size_z)] for n in range(2)]
            both = side_by_side(low, high).astype(out_ref.dtype)
            if i < devices:
                out_ref[i, 0] = both
            if i > 0:
                out_ref[i - 1, 1] = both

    return pl.pallas_call(
        body,
        in_specs=[pl.BlockSpec(memory_space=pltpu.SMEM)] + [pl.BlockSpec(memory_space=pltpu.VMEM)] * 4,
        out_specs=pl.BlockSpec(memory_space=pltpu.VMEM),
        out_shape=jax.ShapeDtypeStruct((devices, own_x, size_z, 8, 128), jnp.bfloat16),
        scratch_shapes=[
            pltpu.VMEM((size_x + 2, size_z + 2, 8, channels), jnp.float32),
            pltpu.VMEM((size_x + 2, size_z + 2, 8, 128), jnp.float32),
        ],
        compiler_params=pltpu.CompilerParams(vmem_limit_bytes=16 << 20),
        name="bottom_out",
    )(place, field, y_in, y_out, weights)


def decode(place, bottom, skip, edge, weights):
    devices, pairs, coarse_z, _, _ = bottom.shape
    full_x, full_y, size_z, skip_channels = skip.shape
    size_x, size_y = full_x - 2, full_y - 2
    channels = 64 * devices + skip_channels
    filters = weights.shape[-1]
    rows, extra = size_x * size_y * size_z, size_x * size_y

    def body(place_ref, bottom_ref, skip_ref, edge_ref, weights_ref, out_ref, main_ref, side_ref, sums_ref):
        first = place_ref[2] == 0
        planes = [[] for _ in range(2 * pairs)]
        for k in range(devices // 2):
            for pair in range(pairs):
                low, high = [bottom_ref[2 * k + i, pair].astype(jnp.float32) for i in range(2)]
                even, odd = halves(low, high)
                planes[2 * pair].append(even.reshape(coarse_z * 8, 128))
                planes[2 * pair + 1].append(odd.reshape(coarse_z * 8, 128))

        def choice(y, z, source):
            line = (y + 1) // 2 + 1
            inside = ((line > 1) | (place_ref[1] > 0)) & ((line < coarse_z) | (place_ref[1] < place_ref[4]))
            return jnp.where((source == z * 8 + line) & inside, 1.0, 0.0).astype(jnp.bfloat16)

        shape = (full_y * size_z, coarse_z * 8)
        row = lax.broadcasted_iota(jnp.int32, shape, 0)
        spread = choice(row // size_z, row % size_z // 2 + 1, lax.broadcasted_iota(jnp.int32, shape, 1))
        shape = (16, coarse_z * 8)
        row = lax.broadcasted_iota(jnp.int32, shape, 0)
        other = jnp.where(first, coarse_z - 1, 0)
        spread_edge = choice(row, other, lax.broadcasted_iota(jnp.int32, shape, 1))
        for plane in range(2 * pairs):
            coarse = jnp.concatenate(planes[plane], axis=1).astype(jnp.bfloat16)
            fine = jnp.dot(spread, coarse, preferred_element_type=jnp.float32)
            fine_edge = jnp.dot(spread_edge, coarse, preferred_element_type=jnp.float32)
            for x in range(full_x):
                if (x + 1) // 2 != plane:
                    continue
                joined = jnp.concatenate([fine, skip_ref[x].astype(jnp.float32).reshape(full_y * size_z, skip_channels)], axis=1)
                joined_edge = jnp.concatenate([fine_edge, edge_ref[x].astype(jnp.float32)], axis=1)
                for dy in range(3):
                    main_ref[dy, x] = joined[8 * dy : 8 * dy + size_y * size_z].astype(jnp.bfloat16)
                    side_ref[dy, x] = joined_edge[dy : dy + size_y]
        for dx in range(3):
            blocks = []
            for dy in range(3):
                main = main_ref[dy, dx : dx + size_x].reshape(rows, channels)
                side = side_ref[dy, dx : dx + size_x].reshape(extra, channels).astype(jnp.bfloat16)
                blocks.append(jnp.concatenate([main, side], axis=0))
            block = jnp.concatenate(blocks, axis=1)
            for tap in range(3):
                kernel = weights_ref[3 * dx : 3 * dx + 3, tap].reshape(3 * channels, filters)
                product = jnp.dot(block, kernel, preferred_element_type=jnp.float32)
                if dx == 0:
                    sums_ref[tap] = product
                else:
                    sums_ref[tap] += product
        total = join_taps(first, [sums_ref[tap] for tap in range(3)], extra, size_z)
        out_ref[...] = total.reshape(size_x, size_y, size_z, filters).astype(out_ref.dtype)

    return pl.pallas_call(
        body,
        in_specs=[pl.BlockSpec(memory_space=pltpu.SMEM)]
        + [pl.BlockSpec(memory_space=pltpu.VMEM)] * 4,
        out_specs=pl.BlockSpec(memory_space=pltpu.VMEM),
        out_shape=jax.ShapeDtypeStruct((size_x, size_y, size_z, filters), jnp.bfloat16),
        scratch_shapes=[
            pltpu.VMEM((3, full_x, size_y * size_z, channels), jnp.bfloat16),
            pltpu.VMEM((3, full_x, size_y, channels), jnp.float32),
            pltpu.VMEM((3, rows + extra, filters), jnp.float32),
        ],
        compiler_params=pltpu.CompilerParams(vmem_limit_bytes=16 << 20),
        name="decode",
    )(place, bottom, skip, edge, weights)


def solution(mesh):
    gx, gy, gz = mesh.shape["gx"], mesh.shape["gy"], mesh.shape["gz"]

    def local(volume, w_full, w_half, w_bottom_in, w_bottom_out, w_up):
        place_z = lax.axis_index("gz")
        place = jnp.stack([lax.axis_index("gx"), lax.axis_index("gy"), place_z, jnp.int32(gx - 1), jnp.int32(gy - 1)])
        swap = [(0, 1), (1, 0)]

        def edge_of(plane_low, plane_high):
            return lax.ppermute(jnp.where(place_z == 0, plane_high, plane_low), "gz", swap)

        x_in, x_out = swaps(volume[:3], volume[-3:], "gx", gx)
        weights = prepare(w_full, w_bottom_in, w_bottom_out)
        (w_pair, w_in, w_out), x_in, x_out = lax.optimization_barrier((weights, x_in, x_out))
        y_inner, y_outer, plane = pack_y(place, volume, x_in, x_out)
        y_in, y_out = send(y_inner, y_outer, "gy", gy)
        edge = lax.ppermute(pack_z(place, plane, y_in, y_out), "gz", swap)
        pooled = encode(place, volume, x_in, x_out, y_in, y_out, edge, w_pair)

        edge = edge_of(pooled[:, :, 0], pooled[:, :, -1])
        skip, coarse = half_level(place, pooled, edge, w_half.reshape(9, 3, w_half.shape[3], w_half.shape[4]))
        lines = coarse.reshape(coarse.shape[0], 4, 4, coarse.shape[2])
        below, above = halo(lines, "gy", gy, 2, 1)
        column = jnp.concatenate([coarse, below[:, :, 0], above[:, :, 0]], axis=1)
        column = jnp.broadcast_to(column[None], (gx * gz,) + column.shape)
        column = lax.all_to_all(column, ("gx", "gz"), 0, 0)
        first = bottom_in(place, column, w_in)
        first = lax.all_to_all(first, "gx", 0, 0)
        y_in, y_out = swaps(first[:, :, :, :2], first[:, :, :, -2:], "gy", gy)
        second = bottom_out(place, first, y_in, y_out, w_out)
        w_up = fetch(w_up.reshape(9, 3, w_up.shape[3], w_up.shape[4]), second)
        second = lax.all_to_all(second, "gx", 0, 0)

        around = extend(skip, "gx", gx, 0, 1)
        around = extend(around, "gy", gy, 1, 1)
        side = edge_of(around[:, :, 0], around[:, :, -1])
        side = jnp.pad(side, ((0, 0), (0, -side.shape[1] % 16), (0, 0)))
        return decode(place, second, around, side, w_up)

    space = P("gx", "gy", "gz", None)
    filters = P(None, None, None, None, "gx")
    return jax.shard_map(
        local,
        mesh=mesh,
        in_specs=(space, P(), P(), filters, filters, P()),
        out_specs=space,
        check_vma=False,
    )
```

```python
import jax
import jax.numpy as jnp
from jax import lax
from jax.experimental import pallas as pl
from jax.experimental.pallas import tpu as pltpu
from jax.sharding import PartitionSpec as P


def send(inner_block, outer_block, axis, count):
    inner = [(i, i ^ 1) for i in range(count)]
    outer = [(i, (((i + 1) ^ 1) - 1) % count) for i in range(count)]
    return lax.ppermute(inner_block, axis, inner), lax.ppermute(outer_block, axis, outer)


def swaps(low, high, axis, count):
    even = lax.axis_index(axis) % 2 == 0
    return send(jnp.where(even, high, low), jnp.where(even, low, high), axis, count)


def ordered(got_in, got_out, axis):
    even = lax.axis_index(axis) % 2 == 0
    return jnp.where(even, got_out, got_in), jnp.where(even, got_in, got_out)


def halo(field, axis, count, dim, width):
    place = lax.axis_index(axis)
    size = field.shape[dim]
    low = lax.slice_in_dim(field, 0, width, axis=dim)
    high = lax.slice_in_dim(field, size - width, size, axis=dim)
    below, above = ordered(*swaps(low, high, axis, count), axis)
    zero = jnp.zeros_like(low)
    return jnp.where(place > 0, below, zero), jnp.where(place < count - 1, above, zero)


def extend(field, axis, count, dim, width):
    below, above = halo(field, axis, count, dim, width)
    return jnp.concatenate([below, field, above], axis=dim)


def half_level(place, field, edge, weights):
    full_x, full_y, size_z, channels = field.shape
    size_x, size_y = full_x - 2, full_y - 2
    filters = weights.shape[-1]
    rows, extra = size_x * size_y * size_z, size_x * size_y

    def body(place_ref, field_ref, edge_ref, weights_ref, out_ref, coarse_ref, rows_ref, coarse_rows_ref):
        first = place_ref[2] == 0
        edge_plane = edge_ref[...].astype(jnp.float32)
        blocks = []
        for dx in range(3):
            for dy in range(3):
                main = field_ref[dx : dx + size_x, dy : dy + size_y].astype(jnp.float32).reshape(rows, channels)
                side = edge_plane[dx : dx + size_x, dy : dy + size_y].reshape(extra, channels)
                blocks.append(jnp.concatenate([main, side], axis=0).astype(jnp.bfloat16))
        block = jnp.concatenate(blocks, axis=1)
        sums = []
        for tap in range(3):
            kernel = weights_ref[:, tap].reshape(9 * channels, filters)
            sums.append(jnp.dot(block, kernel, preferred_element_type=jnp.float32))
        total = jnp.maximum(join_taps(first, sums, extra, size_z), 0.0)
        out_ref[...] = total.reshape(size_x, size_y, size_z, filters).astype(out_ref.dtype)
        total = jnp.max(total.reshape(size_x // 2, 2, size_y // 2, 2, size_z, filters), axis=(1, 3))
        count = size_y // 2
        for part in range(filters // 128):
            rows_ref[...] = total[..., 128 * part : 128 * part + 128].reshape(rows // 4, 128)
            for x in range(size_x // 2):
                for z in range(size_z // 2):
                    start = x * count * size_z + 2 * z
                    pooled = jnp.maximum(
                        rows_ref[pl.ds(start, count, stride=size_z), :], rows_ref[pl.ds(start + 1, count, stride=size_z), :]
                    )
                    coarse_rows_ref[x, count * z : count * z + count, 128 * part : 128 * part + 128] = pooled
        coarse_ref[...] = coarse_rows_ref[...].astype(coarse_ref.dtype)

    return pl.pallas_call(
        body,
        in_specs=[pl.BlockSpec(memory_space=pltpu.SMEM)] + [pl.BlockSpec(memory_space=pltpu.VMEM)] * 3,
        out_specs=[pl.BlockSpec(memory_space=pltpu.VMEM)] * 2,
        out_shape=[
            jax.ShapeDtypeStruct((size_x, size_y, size_z, filters), jnp.bfloat16),
            jax.ShapeDtypeStruct((size_x // 2, size_z * size_y // 4, filters), jnp.bfloat16),
        ],
        scratch_shapes=[
            pltpu.VMEM((rows // 4, 128), jnp.float32),
            pltpu.VMEM((size_x // 2, size_z * size_y // 4, filters), jnp.float32),
        ],
        compiler_params=pltpu.CompilerParams(vmem_limit_bytes=12 << 20),
        name="half_level",
    )(place, field, edge, weights)


def join_taps(first, sums, groups, size_z):
    rows, filters = groups * size_z, sums[0].shape[-1]
    low, mid, high = [total[:rows].reshape(groups, size_z, filters) for total in sums]
    below = jnp.where(first, 0.0, sums[0][rows : rows + groups])
    above = jnp.where(first, sums[2][rows : rows + groups], 0.0)
    index = lax.broadcasted_iota(jnp.int32, (groups, size_z, filters), 1)
    down = jnp.where(index == 0, below[:, None, :], pltpu.roll(low, 1, 1))
    up = jnp.where(index == size_z - 1, above[:, None, :], pltpu.roll(high, size_z - 1, 1))
    return down + mid + up


def encode(place, own, x_in, x_out, y_in, y_out, edge, weights):
    own_x, own_y, size_z, channels = own.shape
    reach = x_in.shape[0]
    full_x, full_y = own_x + 2 * reach, own_y + 2 * reach
    size_x, size_y = full_x - 2, full_y - 2
    filters = weights.shape[-1] // 2
    rows, extra = size_y * size_z, size_y + (-size_y % 16)
    pool_y, pool_z = size_y // 2, size_z // 2

    def body(
        place_ref,
        own_hbm,
        x_in_ref,
        x_out_ref,
        y_in_ref,
        y_out_ref,
        edge_ref,
        weights_hbm,
        out_ref,
        field_ref,
        side_ref,
        rows_ref,
        weights_ref,
        sems,
    ):
        inner = field_ref.at[reach : reach + own_x, reach : reach + own_y]
        copies = [pltpu.make_async_copy(own_hbm, inner, sems.at[0]), pltpu.make_async_copy(weights_hbm, weights_ref, sems.at[1])]
        for copy in copies:
            copy.start()
        even_x, even_y = place_ref[0] % 2 == 0, place_ref[1] % 2 == 0
        low_x, high_x = place_ref[0] > 0, place_ref[0] < place_ref[3]
        low_y, high_y = place_ref[1] > 0, place_ref[1] < place_ref[4]
        nil = jnp.bfloat16(0)
        inner_y = slice(reach, reach + own_y)
        below, above = jnp.where(even_x, x_out_ref[...], x_in_ref[...]), jnp.where(even_x, x_in_ref[...], x_out_ref[...])
        field_ref[:reach, inner_y] = jnp.where(low_x, below, nil)
        field_ref[reach + own_x :, inner_y] = jnp.where(high_x, above, nil)
        for x in range(full_x):
            here_low, here_high = low_y, high_y
            if x < reach:
                here_low, here_high = low_y & low_x, high_y & low_x
            if x >= reach + own_x:
                here_low, here_high = low_y & high_x, high_y & high_x
            below, above = jnp.where(even_y, y_out_ref[x], y_in_ref[x]), jnp.where(even_y, y_in_ref[x], y_out_ref[x])
            field_ref[x, :reach] = jnp.where(here_low, below, nil)
            field_ref[x, reach + own_y :] = jnp.where(here_high, above, nil)
            line = lax.broadcasted_iota(jnp.int32, (full_y, channels), 0)
            inside = ((line >= reach) | low_y) & ((line < reach + own_y) | high_y)
            if x < reach:
                inside = inside & low_x
            if x >= reach + own_x:
                inside = inside & high_x
            plane = jnp.where(inside, edge_ref[x].astype(jnp.float32), 0.0)
            for dy in range(3):
                side_ref[dy, x, :size_y] = plane[dy : dy + size_y]
                side_ref[dy, x, size_y:] = jnp.zeros((extra - size_y, channels), jnp.float32)

        first = place_ref[2] == 0
        for copy in copies:
            copy.wait()
        line = lax.broadcasted_iota(jnp.int32, (pool_y, pool_z, filters), 0)
        inside_y = ((line > 0) | low_y) & ((line < pool_y - 1) | high_y)
        for pair in range(size_x // 2):
            blocks = []
            for plane in range(4):
                for dy in range(3):
                    main = field_ref[2 * pair + plane, dy : dy + size_y].reshape(rows, channels)
                    side = side_ref[dy, 2 * pair + plane].astype(jnp.bfloat16)
                    blocks.append(jnp.concatenate([main, side], axis=0))
            block = jnp.concatenate(blocks, axis=1)
            sums = []
            for tap in range(3):
                kernel = weights_ref[:, :, tap].reshape(12 * channels, 2 * filters)
                sums.append(jnp.dot(block, kernel, preferred_element_type=jnp.float32))
            total = jnp.maximum(join_taps(first, sums, size_y, size_z), 0.0)
            total = jnp.maximum(total[..., :filters], total[..., filters:])
            total = jnp.max(total.reshape(pool_y, 2, size_z, filters), axis=1)
            rows_ref[...] = total.reshape(pool_y * size_z, filters)
            total = jnp.maximum(
                rows_ref[pl.ds(0, pool_y * pool_z, stride=2), :], rows_ref[pl.ds(1, pool_y * pool_z, stride=2), :]
            ).reshape(pool_y, pool_z, filters)
            inside = inside_y
            if pair == 0:
                inside = inside & low_x
            if pair == size_x // 2 - 1:
                inside = inside & high_x
            out_ref[pair] = jnp.where(inside, total, 0.0).astype(out_ref.dtype)

    return pl.pallas_call(
        body,
        in_specs=[pl.BlockSpec(memory_space=pltpu.SMEM), pl.BlockSpec(memory_space=pltpu.HBM)]
        + [pl.BlockSpec(memory_space=pltpu.VMEM)] * 5
        + [pl.BlockSpec(memory_space=pltpu.HBM)],
        out_specs=pl.BlockSpec(memory_space=pltpu.VMEM),
        out_shape=jax.ShapeDtypeStruct((size_x // 2, pool_y, pool_z, filters), jnp.bfloat16),
        scratch_shapes=[
            pltpu.VMEM((full_x, full_y, size_z, channels), jnp.bfloat16),
            pltpu.VMEM((3, full_x, extra, channels), jnp.float32),
            pltpu.VMEM((pool_y * size_z, filters), jnp.float32),
            pltpu.VMEM(weights.shape, weights.dtype),
            pltpu.SemaphoreType.DMA((2,)),
        ],
        compiler_params=pltpu.CompilerParams(vmem_limit_bytes=20 << 20),
        name="encode",
    )(place, far(own), x_in, x_out, y_in, y_out, edge, far(weights))


def paired(weights):
    grow = [(0, 0)] * 4
    return jnp.concatenate([jnp.pad(weights, [(0, 1)] + grow), jnp.pad(weights, [(1, 0)] + grow)], axis=4)


def far(array):
    return pltpu.with_memory_space_constraint(array, pltpu.HBM)


def pack_y(place, own, x_in, x_out):
    own_x, own_y, size_z, channels = own.shape
    reach = x_in.shape[0]
    full_x = own_x + 2 * reach

    def body(place_ref, own_ref, x_in_ref, x_out_ref, inner_ref, outer_ref, plane_ref, rows_ref):
        even_x, even_y, first = place_ref[0] % 2 == 0, place_ref[1] % 2 == 0, place_ref[2] == 0
        below = jnp.where(even_x, x_out_ref[...], x_in_ref[...])
        above = jnp.where(even_x, x_in_ref[...], x_out_ref[...])
        for start, block in ((0, below), (reach, own_ref[...]), (reach + own_x, above)):
            size = block.shape[0]
            low, high = block[:, :reach], block[:, own_y - reach :]
            inner_ref[start : start + size] = jnp.where(even_y, high, low)
            outer_ref[start : start + size] = jnp.where(even_y, low, high)
            block = block.astype(jnp.float32)
            edge = jnp.where(first, block[:, :, size_z - 1 :], block[:, :, :1])
            for x in range(size):
                for y in range(own_y):
                    rows_ref[start + x, y : y + 1] = edge[x, y]
        plane_ref[...] = rows_ref[...].astype(plane_ref.dtype)

    return pl.pallas_call(
        body,
        in_specs=[pl.BlockSpec(memory_space=pltpu.SMEM)] + [pl.BlockSpec(memory_space=pltpu.VMEM)] * 3,
        out_specs=[pl.BlockSpec(memory_space=pltpu.VMEM)] * 3,
        out_shape=[jax.ShapeDtypeStruct((full_x, reach, size_z, channels), jnp.bfloat16)] * 2
        + [jax.ShapeDtypeStruct((full_x, own_y, channels), jnp.bfloat16)],
        scratch_shapes=[pltpu.VMEM((full_x, own_y, channels), jnp.float32)],
        compiler_params=pltpu.CompilerParams(vmem_limit_bytes=8 << 20),
        name="pack_y",
    )(place, own, x_in, x_out)


def pack_z(place, plane, y_in, y_out):
    full_x, own_y, channels = plane.shape
    reach, size_z = y_in.shape[1:3]
    full_y = own_y + 2 * reach

    def body(place_ref, plane_ref, y_in_ref, y_out_ref, out_ref, rows_ref):
        even_y, first = place_ref[1] % 2 == 0, place_ref[2] == 0
        rows_ref[:, reach : reach + own_y] = plane_ref[...].astype(jnp.float32)
        edges = []
        for ref in (y_in_ref, y_out_ref):
            block = ref[...].astype(jnp.float32)
            edges.append(jnp.where(first, block[:, :, size_z - 1 :], block[:, :, :1]))
        below, above = jnp.where(even_y, edges[1], edges[0]), jnp.where(even_y, edges[0], edges[1])
        for x in range(full_x):
            for y in range(reach):
                rows_ref[x, y : y + 1] = below[x, y]
                rows_ref[x, reach + own_y + y : reach + own_y + y + 1] = above[x, y]
        out_ref[...] = rows_ref[...].astype(out_ref.dtype)

    return pl.pallas_call(
        body,
        in_specs=[pl.BlockSpec(memory_space=pltpu.SMEM)] + [pl.BlockSpec(memory_space=pltpu.VMEM)] * 3,
        out_specs=pl.BlockSpec(memory_space=pltpu.VMEM),
        out_shape=jax.ShapeDtypeStruct((full_x, full_y, channels), jnp.bfloat16),
        scratch_shapes=[pltpu.VMEM((full_x, full_y, channels), jnp.float32)],
        compiler_params=pltpu.CompilerParams(vmem_limit_bytes=8 << 20),
        name="pack_z",
    )(place, plane, y_in, y_out)


def halves(pair_low, pair_high):
    lane = lax.broadcasted_iota(jnp.int32, pair_low.shape, pair_low.ndim - 1)
    axis = pair_low.ndim - 1
    even = jnp.where(lane < 64, pair_low, pltpu.roll(pair_high, 64, axis))
    odd = jnp.where(lane < 64, pltpu.roll(pair_low, 64, axis), pair_high)
    return even, odd


def side_by_side(even, odd):
    lane = lax.broadcasted_iota(jnp.int32, even.shape, even.ndim - 1)
    return jnp.where(lane < 64, even, pltpu.roll(odd, 64, even.ndim - 1))


def column_weights(weights_hbm, weights_ref, sems):
    filters, channels = weights_hbm.shape[3:]
    weights_ref[3 * filters :] = jnp.zeros((weights_ref.shape[0] - 3 * filters, 9 * channels), weights_ref.dtype)
    copies = []
    for dx in range(3):
        for dy in range(3):
            for dz in range(3):
                lanes = pl.ds((3 * dx + dz) * channels, channels)
                to = weights_ref.at[pl.ds(filters * dy, filters), lanes]
                copies.append(pltpu.make_async_copy(weights_hbm.at[dx, dy, dz], to, sems.at[9 * dx + 3 * dy + dz]))
                copies[-1].start()
    return copies


def column_product(pad_ref, weights_ref, first, start, planes, size_z):
    channels = pad_ref.shape[-1]
    rows = planes * size_z * 8
    blocks = []
    for dx in range(3):
        for dz in range(3):
            block = pad_ref[first + dx : first + dx + planes, pl.ds(start + dz, size_z)]
            blocks.append(block.reshape(rows, channels).astype(jnp.bfloat16))
    block = jnp.concatenate(blocks, axis=1)
    total = lax.dot_general(block, weights_ref[...], (((1,), (1,)), ((), ())), preferred_element_type=jnp.float32)
    low = total[:, :128].reshape(planes * size_z, 8, 128)
    mid = pltpu.roll(total[:, :128], 64, 1).reshape(planes * size_z, 8, 128)
    high = total[:, 128:].reshape(planes * size_z, 8, 128)
    total = pltpu.roll(low, 1, 1) + mid + pltpu.roll(high, 7, 1)
    return jnp.maximum(total, 0.0).reshape(planes, size_z, 8, 128)


def bottom_in(place, field, weights):
    count, own_x, lines, channels = field.shape
    devices = count // 2
    own_z = size_y = 4
    size_x, all_z, size_z = devices * own_x, 2 * own_z, own_z + 2

    def body(place_ref, field_ref, weights_hbm, out_ref, pad_ref, weights_ref, sems):
        copies = column_weights(weights_hbm, weights_ref, sems)
        zero = jnp.zeros((all_z + 2, 8, channels), jnp.float32)
        pad_ref[0] = zero
        pad_ref[size_x + 1] = zero
        for x in range(size_x):
            pad_ref[x + 1, 0] = zero[0]
            pad_ref[x + 1, all_z + 1] = zero[0]
        for i in range(devices):
            for half in range(2):
                for x in range(own_x):
                    block = field_ref[2 * i + half, x].astype(jnp.float32)
                    for z in range(own_z):
                        to = (1 + own_x * i + x, 1 + own_z * half + z)
                        pad_ref[*to, 0:1] = block[own_z * size_y + z : own_z * size_y + z + 1]
                        pad_ref[*to, 1 : size_y + 1] = block[size_y * z : size_y * z + size_y]
                        line = own_z * (size_y + 1) + z
                        pad_ref[*to, size_y + 1 : size_y + 2] = block[line : line + 1]
                        pad_ref[*to, size_y + 2 :] = zero[0, size_y + 2 :]
        start = 2 * place_ref[2]
        for copy in copies:
            copy.wait()
        for first in range(0, size_x, 4):
            total = column_product(pad_ref, weights_ref, first, start, 4, size_z)
            for pair in range(2):
                both = side_by_side(total[2 * pair], total[2 * pair + 1])[:, 1 : size_y + 1].astype(out_ref.dtype)
                for i in range(devices):
                    out_ref[i, first // 2 + pair] = both

    return pl.pallas_call(
        body,
        in_specs=[pl.BlockSpec(memory_space=space) for space in (pltpu.SMEM, pltpu.VMEM, pltpu.HBM)],
        out_specs=pl.BlockSpec(memory_space=pltpu.VMEM),
        out_shape=jax.ShapeDtypeStruct((devices, size_x // 2, size_z, size_y, 128), jnp.bfloat16),
        scratch_shapes=[
            pltpu.VMEM((size_x + 2, all_z + 2, 8, channels), jnp.float32),
            pltpu.VMEM((256, 9 * channels), jnp.bfloat16),
            pltpu.SemaphoreType.DMA((27,)),
        ],
        compiler_params=pltpu.CompilerParams(vmem_limit_bytes=12 << 20),
        name="bottom_in",
    )(place, field, far(weights))


def bottom_out(place, field, y_in, y_out, weights):
    devices, pairs, size_z, _, _ = field.shape
    size_x, channels = 2 * pairs, 64 * devices
    own_x = size_x // devices

    def body(place_ref, field_ref, y_in_ref, y_out_ref, weights_hbm, out_ref, pad_ref, total_ref, weights_ref, sems):
        copies = column_weights(weights_hbm, weights_ref, sems)
        even_y = place_ref[1] % 2 == 0
        low_y, high_y = place_ref[1] > 0, place_ref[1] < place_ref[4]
        zero = jnp.zeros((size_z + 2, 8, channels), jnp.float32)
        for ref in (pad_ref, total_ref):
            wide = ref.shape[-1]
            ref[0] = zero[..., :wide]
            ref[size_x + 1] = zero[..., :wide]
            for x in range(size_x):
                ref[x + 1, 0] = zero[0, :, :wide]
                ref[x + 1, size_z + 1] = zero[0, :, :wide]
        for k in range(devices // 2):
            for pair in range(pairs):
                y_first, y_last = [], []
                for i in range(2):
                    one = y_in_ref[2 * k + i, pair].astype(jnp.float32)
                    other = y_out_ref[2 * k + i, pair].astype(jnp.float32)
                    y_first.append(jnp.where(low_y, jnp.where(even_y, other, one), 0.0))
                    y_last.append(jnp.where(high_y, jnp.where(even_y, one, other), 0.0))
                own = [field_ref[2 * k + i, pair].astype(jnp.float32) for i in range(2)]
                for line, blocks in ((0, y_first), (2, own), (6, y_last)):
                    even, odd = halves(*blocks)
                    lines = slice(line, line + even.shape[1])
                    pad_ref[1 + 2 * pair, 1 : size_z + 1, lines, 128 * k : 128 * k + 128] = even
                    pad_ref[2 + 2 * pair, 1 : size_z + 1, lines, 128 * k : 128 * k + 128] = odd
        for copy in copies:
            copy.wait()
        for first in range(0, size_x, 4):
            total = column_product(pad_ref, weights_ref, first, 0, 4, size_z)
            total_ref[1 + first : 5 + first, 1 : size_z + 1] = total
        start = 2 * place_ref[2]
        for i in range(size_x // 2 + 1):
            low, high = [total_ref[2 * i + n, pl.ds(start, size_z)] for n in range(2)]
            both = side_by_side(low, high).astype(out_ref.dtype)
            if i < devices:
                out_ref[i, 0] = both
            if i > 0:
                out_ref[i - 1, 1] = both

    return pl.pallas_call(
        body,
        in_specs=[pl.BlockSpec(memory_space=pltpu.SMEM)]
        + [pl.BlockSpec(memory_space=pltpu.VMEM)] * 3
        + [pl.BlockSpec(memory_space=pltpu.HBM)],
        out_specs=pl.BlockSpec(memory_space=pltpu.VMEM),
        out_shape=jax.ShapeDtypeStruct((devices, own_x, size_z, 8, 128), jnp.bfloat16),
        scratch_shapes=[
            pltpu.VMEM((size_x + 2, size_z + 2, 8, channels), jnp.float32),
            pltpu.VMEM((size_x + 2, size_z + 2, 8, 128), jnp.float32),
            pltpu.VMEM((256, 9 * channels), jnp.bfloat16),
            pltpu.SemaphoreType.DMA((27,)),
        ],
        compiler_params=pltpu.CompilerParams(vmem_limit_bytes=20 << 20),
        name="bottom_out",
    )(place, field, y_in, y_out, far(weights))


def decode(place, bottom, skip, edge, weights):
    devices, pairs, coarse_z, _, _ = bottom.shape
    full_x, full_y, size_z, skip_channels = skip.shape
    size_x, size_y = full_x - 2, full_y - 2
    channels = 64 * devices + skip_channels
    filters = weights.shape[-1]
    rows, extra = size_x * size_y * size_z, size_x * size_y

    def body(place_ref, bottom_ref, skip_ref, edge_ref, weights_hbm, out_ref, main_ref, side_ref, sums_ref, weights_ref, sems):
        copies = [pltpu.make_async_copy(weights_hbm.at[step], weights_ref.at[step], sems.at[step]) for step in range(9)]
        for copy in copies:
            copy.start()
        first = place_ref[2] == 0
        planes = [[] for _ in range(2 * pairs)]
        for k in range(devices // 2):
            for pair in range(pairs):
                low, high = [bottom_ref[2 * k + i, pair].astype(jnp.float32) for i in range(2)]
                even, odd = halves(low, high)
                planes[2 * pair].append(even.reshape(coarse_z * 8, 128))
                planes[2 * pair + 1].append(odd.reshape(coarse_z * 8, 128))

        def choice(y, z, source):
            line = (y + 1) // 2 + 1
            inside = ((line > 1) | (place_ref[1] > 0)) & ((line < coarse_z) | (place_ref[1] < place_ref[4]))
            return jnp.where((source == z * 8 + line) & inside, 1.0, 0.0).astype(jnp.bfloat16)

        shape = (full_y * size_z, coarse_z * 8)
        row = lax.broadcasted_iota(jnp.int32, shape, 0)
        spread = choice(row // size_z, row % size_z // 2 + 1, lax.broadcasted_iota(jnp.int32, shape, 1))
        shape = (16, coarse_z * 8)
        row = lax.broadcasted_iota(jnp.int32, shape, 0)
        other = jnp.where(first, coarse_z - 1, 0)
        spread_edge = choice(row, other, lax.broadcasted_iota(jnp.int32, shape, 1))
        for plane in range(2 * pairs):
            coarse = jnp.concatenate(planes[plane], axis=1).astype(jnp.bfloat16)
            fine = jnp.dot(spread, coarse, preferred_element_type=jnp.float32)
            fine_edge = jnp.dot(spread_edge, coarse, preferred_element_type=jnp.float32)
            for x in range(full_x):
                if (x + 1) // 2 != plane:
                    continue
                joined = jnp.concatenate([fine, skip_ref[x].astype(jnp.float32).reshape(full_y * size_z, skip_channels)], axis=1)
                joined_edge = jnp.concatenate([fine_edge, edge_ref[x].astype(jnp.float32)], axis=1)
                for dy in range(3):
                    main_ref[dy, x] = joined[8 * dy : 8 * dy + size_y * size_z].astype(jnp.bfloat16)
                    side_ref[dy, x] = joined_edge[dy : dy + size_y]
        for dx in range(3):
            blocks = []
            for dy in range(3):
                main = main_ref[dy, dx : dx + size_x].reshape(rows, channels)
                side = side_ref[dy, dx : dx + size_x].reshape(extra, channels).astype(jnp.bfloat16)
                blocks.append(jnp.concatenate([main, side], axis=0))
                copies[3 * dx + dy].wait()
            block = jnp.concatenate(blocks, axis=1)
            for tap in range(3):
                kernel = weights_ref[3 * dx : 3 * dx + 3, tap].reshape(3 * channels, filters)
                product = jnp.dot(block, kernel, preferred_element_type=jnp.float32)
                if dx == 0:
                    sums_ref[tap] = product
                else:
                    sums_ref[tap] += product
        total = join_taps(first, [sums_ref[tap] for tap in range(3)], extra, size_z)
        out_ref[...] = total.reshape(size_x, size_y, size_z, filters).astype(out_ref.dtype)

    return pl.pallas_call(
        body,
        in_specs=[pl.BlockSpec(memory_space=pltpu.SMEM)]
        + [pl.BlockSpec(memory_space=pltpu.VMEM)] * 3
        + [pl.BlockSpec(memory_space=pltpu.HBM)],
        out_specs=pl.BlockSpec(memory_space=pltpu.VMEM),
        out_shape=jax.ShapeDtypeStruct((size_x, size_y, size_z, filters), jnp.bfloat16),
        scratch_shapes=[
            pltpu.VMEM((3, full_x, size_y * size_z, channels), jnp.bfloat16),
            pltpu.VMEM((3, full_x, size_y, channels), jnp.float32),
            pltpu.VMEM((3, rows + extra, filters), jnp.float32),
            pltpu.VMEM(weights.shape, weights.dtype),
            pltpu.SemaphoreType.DMA((9,)),
        ],
        compiler_params=pltpu.CompilerParams(vmem_limit_bytes=26 << 20),
        name="decode",
    )(place, bottom, skip, edge, far(weights))


def solution(mesh):
    gx, gy, gz = mesh.shape["gx"], mesh.shape["gy"], mesh.shape["gz"]

    def local(volume, w_full, w_half, w_bottom_in, w_bottom_out, w_up):
        place_z = lax.axis_index("gz")
        place = jnp.stack([lax.axis_index("gx"), lax.axis_index("gy"), place_z, jnp.int32(gx - 1), jnp.int32(gy - 1)])
        swap = [(0, 1), (1, 0)]

        def edge_of(plane_low, plane_high):
            return lax.ppermute(jnp.where(place_z == 0, plane_high, plane_low), "gz", swap)

        x_in, x_out = swaps(volume[:3], volume[-3:], "gx", gx)
        w_pair, x_in, x_out = lax.optimization_barrier((paired(w_full), x_in, x_out))
        y_inner, y_outer, plane = pack_y(place, volume, x_in, x_out)
        y_in, y_out = send(y_inner, y_outer, "gy", gy)
        edge = lax.ppermute(pack_z(place, plane, y_in, y_out), "gz", swap)
        pooled = encode(place, volume, x_in, x_out, y_in, y_out, edge, w_pair)

        edge = edge_of(pooled[:, :, 0], pooled[:, :, -1])
        skip, coarse = half_level(place, pooled, edge, w_half.reshape(9, 3, w_half.shape[3], w_half.shape[4]))
        lines = coarse.reshape(coarse.shape[0], 4, 4, coarse.shape[2])
        below, above = halo(lines, "gy", gy, 2, 1)
        column = jnp.concatenate([coarse, below[:, :, 0], above[:, :, 0]], axis=1)
        column = jnp.broadcast_to(column[None], (gx * gz,) + column.shape)
        column = lax.all_to_all(column, ("gx", "gz"), 0, 0)
        first = bottom_in(place, column, w_bottom_in.transpose(0, 1, 2, 4, 3))
        first = lax.all_to_all(first, "gx", 0, 0)
        y_in, y_out = swaps(first[:, :, :, :2], first[:, :, :, -2:], "gy", gy)
        second = bottom_out(place, first, y_in, y_out, w_bottom_out.transpose(0, 1, 2, 4, 3))
        second = lax.all_to_all(second, "gx", 0, 0)

        around = extend(skip, "gx", gx, 0, 1)
        around = extend(around, "gy", gy, 1, 1)
        side = edge_of(around[:, :, 0], around[:, :, -1])
        side = jnp.pad(side, ((0, 0), (0, -side.shape[1] % 16), (0, 0)))
        return decode(place, second, around, side, w_up.reshape(9, 3, w_up.shape[3], w_up.shape[4]))

    space = P("gx", "gy", "gz", None)
    filters = P(None, None, None, None, "gx")
    return jax.shard_map(
        local,
        mesh=mesh,
        in_specs=(space, P(), P(), filters, filters, P()),
        out_specs=space,
        check_vma=False,
    )
```

```python
import jax
import jax.numpy as jnp
from jax import lax
from jax.experimental import pallas as pl
from jax.experimental.pallas import tpu as pltpu
from jax.sharding import PartitionSpec as P


def send(inner_block, outer_block, axis, count):
    inner = [(i, i ^ 1) for i in range(count)]
    outer = [(i, (((i + 1) ^ 1) - 1) % count) for i in range(count)]
    return lax.ppermute(inner_block, axis, inner), lax.ppermute(outer_block, axis, outer)


def swaps(low, high, axis, count):
    even = lax.axis_index(axis) % 2 == 0
    return send(jnp.where(even, high, low), jnp.where(even, low, high), axis, count)


def ordered(got_in, got_out, axis):
    even = lax.axis_index(axis) % 2 == 0
    return jnp.where(even, got_out, got_in), jnp.where(even, got_in, got_out)


def halo(field, axis, count, dim, width):
    place = lax.axis_index(axis)
    size = field.shape[dim]
    low = lax.slice_in_dim(field, 0, width, axis=dim)
    high = lax.slice_in_dim(field, size - width, size, axis=dim)
    below, above = ordered(*swaps(low, high, axis, count), axis)
    zero = jnp.zeros_like(low)
    return jnp.where(place > 0, below, zero), jnp.where(place < count - 1, above, zero)


def extend(field, axis, count, dim, width):
    below, above = halo(field, axis, count, dim, width)
    return jnp.concatenate([below, field, above], axis=dim)


def half_level(place, field, edge, weights):
    full_x, full_y, size_z, channels = field.shape
    size_x, size_y = full_x - 2, full_y - 2
    filters = weights.shape[-1]
    rows, extra = size_x * size_y * size_z, size_x * size_y

    def body(place_ref, field_ref, edge_ref, weights_ref, out_ref, coarse_ref, rows_ref, coarse_rows_ref):
        first = place_ref[2] == 0
        edge_plane = edge_ref[...].astype(jnp.float32)
        blocks = []
        for dx in range(3):
            for dy in range(3):
                main = field_ref[dx : dx + size_x, dy : dy + size_y].astype(jnp.float32).reshape(rows, channels)
                side = edge_plane[dx : dx + size_x, dy : dy + size_y].reshape(extra, channels)
                blocks.append(jnp.concatenate([main, side], axis=0).astype(jnp.bfloat16))
        block = jnp.concatenate(blocks, axis=1)
        sums = []
        for tap in range(3):
            kernel = weights_ref[:, tap].reshape(9 * channels, filters)
            sums.append(jnp.dot(block, kernel, preferred_element_type=jnp.float32))
        total = jnp.maximum(join_taps(first, sums, extra, size_z), 0.0)
        out_ref[...] = total.reshape(size_x, size_y, size_z, filters).astype(out_ref.dtype)
        total = jnp.max(total.reshape(size_x // 2, 2, size_y // 2, 2, size_z, filters), axis=(1, 3))
        count = size_y // 2
        for part in range(filters // 128):
            rows_ref[...] = total[..., 128 * part : 128 * part + 128].reshape(rows // 4, 128)
            for x in range(size_x // 2):
                for z in range(size_z // 2):
                    start = x * count * size_z + 2 * z
                    pooled = jnp.maximum(
                        rows_ref[pl.ds(start, count, stride=size_z), :], rows_ref[pl.ds(start + 1, count, stride=size_z), :]
                    )
                    coarse_rows_ref[x, count * z : count * z + count, 128 * part : 128 * part + 128] = pooled
        coarse_ref[...] = coarse_rows_ref[...].astype(coarse_ref.dtype)

    return pl.pallas_call(
        body,
        in_specs=[pl.BlockSpec(memory_space=pltpu.SMEM)] + [pl.BlockSpec(memory_space=pltpu.VMEM)] * 3,
        out_specs=[pl.BlockSpec(memory_space=pltpu.VMEM)] * 2,
        out_shape=[
            jax.ShapeDtypeStruct((size_x, size_y, size_z, filters), jnp.bfloat16),
            jax.ShapeDtypeStruct((size_x // 2, size_z * size_y // 4, filters), jnp.bfloat16),
        ],
        scratch_shapes=[
            pltpu.VMEM((rows // 4, 128), jnp.float32),
            pltpu.VMEM((size_x // 2, size_z * size_y // 4, filters), jnp.float32),
        ],
        compiler_params=pltpu.CompilerParams(vmem_limit_bytes=12 << 20),
        name="half_level",
    )(place, field, edge, weights)


def join_taps(first, sums, groups, size_z):
    rows, filters = groups * size_z, sums[0].shape[-1]
    low, mid, high = [total[:rows].reshape(groups, size_z, filters) for total in sums]
    below = jnp.where(first, 0.0, sums[0][rows : rows + groups])
    above = jnp.where(first, sums[2][rows : rows + groups], 0.0)
    index = lax.broadcasted_iota(jnp.int32, (groups, size_z, filters), 1)
    down = jnp.where(index == 0, below[:, None, :], pltpu.roll(low, 1, 1))
    up = jnp.where(index == size_z - 1, above[:, None, :], pltpu.roll(high, size_z - 1, 1))
    return down + mid + up


def encode(place, own, x_in, x_out, y_in, y_out, edge, weights):
    own_x, own_y, size_z, channels = own.shape
    reach = x_in.shape[0]
    full_x, full_y = own_x + 2 * reach, own_y + 2 * reach
    size_x, size_y = full_x - 2, full_y - 2
    filters = weights.shape[-1] // 2
    rows, extra = size_y * size_z, size_y + (-size_y % 16)
    pool_y, pool_z = size_y // 2, size_z // 2

    def body(
        place_ref,
        own_hbm,
        x_in_ref,
        x_out_ref,
        y_in_ref,
        y_out_ref,
        edge_ref,
        weights_hbm,
        out_ref,
        field_ref,
        side_ref,
        rows_ref,
        weights_ref,
        sems,
    ):
        inner = field_ref.at[reach : reach + own_x, reach : reach + own_y]
        copies = [pltpu.make_async_copy(own_hbm, inner, sems.at[0])]
        for tap in range(3):
            copies.append(pltpu.make_async_copy(weights_hbm.at[:, :, tap], weights_ref.at[tap], sems.at[1 + tap]))
        for copy in copies:
            copy.start()
        even_x, even_y = place_ref[0] % 2 == 0, place_ref[1] % 2 == 0
        low_x, high_x = place_ref[0] > 0, place_ref[0] < place_ref[3]
        low_y, high_y = place_ref[1] > 0, place_ref[1] < place_ref[4]
        nil = jnp.bfloat16(0)
        inner_y = slice(reach, reach + own_y)
        below, above = jnp.where(even_x, x_out_ref[...], x_in_ref[...]), jnp.where(even_x, x_in_ref[...], x_out_ref[...])
        field_ref[:reach, inner_y] = jnp.where(low_x, below, nil)
        field_ref[reach + own_x :, inner_y] = jnp.where(high_x, above, nil)
        for x in range(full_x):
            here_low, here_high = low_y, high_y
            if x < reach:
                here_low, here_high = low_y & low_x, high_y & low_x
            if x >= reach + own_x:
                here_low, here_high = low_y & high_x, high_y & high_x
            below, above = jnp.where(even_y, y_out_ref[x], y_in_ref[x]), jnp.where(even_y, y_in_ref[x], y_out_ref[x])
            field_ref[x, :reach] = jnp.where(here_low, below, nil)
            field_ref[x, reach + own_y :] = jnp.where(here_high, above, nil)
            line = lax.broadcasted_iota(jnp.int32, (full_y, channels), 0)
            inside = ((line >= reach) | low_y) & ((line < reach + own_y) | high_y)
            if x < reach:
                inside = inside & low_x
            if x >= reach + own_x:
                inside = inside & high_x
            plane = jnp.where(inside, edge_ref[x].astype(jnp.float32), 0.0)
            for dy in range(3):
                side_ref[dy, x, :size_y] = plane[dy : dy + size_y]
                side_ref[dy, x, size_y:] = jnp.zeros((extra - size_y, channels), jnp.float32)

        first = place_ref[2] == 0
        copies[0].wait()
        line = lax.broadcasted_iota(jnp.int32, (pool_y, pool_z, filters), 0)
        inside_y = ((line > 0) | low_y) & ((line < pool_y - 1) | high_y)
        for pair in range(size_x // 2):
            blocks = []
            for plane in range(4):
                for dy in range(3):
                    main = field_ref[2 * pair + plane, dy : dy + size_y].reshape(rows, channels)
                    side = side_ref[dy, 2 * pair + plane].astype(jnp.bfloat16)
                    blocks.append(jnp.concatenate([main, side], axis=0))
            block = jnp.concatenate(blocks, axis=1)
            sums = []
            for tap in range(3):
                if pair == 0:
                    copies[1 + tap].wait()
                kernel = weights_ref[tap].reshape(12 * channels, 2 * filters)
                sums.append(jnp.dot(block, kernel, preferred_element_type=jnp.float32))
            total = jnp.maximum(join_taps(first, sums, size_y, size_z), 0.0)
            total = jnp.maximum(total[..., :filters], total[..., filters:])
            total = jnp.max(total.reshape(pool_y, 2, size_z, filters), axis=1)
            rows_ref[...] = total.reshape(pool_y * size_z, filters)
            total = jnp.maximum(
                rows_ref[pl.ds(0, pool_y * pool_z, stride=2), :], rows_ref[pl.ds(1, pool_y * pool_z, stride=2), :]
            ).reshape(pool_y, pool_z, filters)
            inside = inside_y
            if pair == 0:
                inside = inside & low_x
            if pair == size_x // 2 - 1:
                inside = inside & high_x
            out_ref[pair] = jnp.where(inside, total, 0.0).astype(out_ref.dtype)

    return pl.pallas_call(
        body,
        in_specs=[pl.BlockSpec(memory_space=pltpu.SMEM), pl.BlockSpec(memory_space=pltpu.HBM)]
        + [pl.BlockSpec(memory_space=pltpu.VMEM)] * 5
        + [pl.BlockSpec(memory_space=pltpu.HBM)],
        out_specs=pl.BlockSpec(memory_space=pltpu.VMEM),
        out_shape=jax.ShapeDtypeStruct((size_x // 2, pool_y, pool_z, filters), jnp.bfloat16),
        scratch_shapes=[
            pltpu.VMEM((full_x, full_y, size_z, channels), jnp.bfloat16),
            pltpu.VMEM((3, full_x, extra, channels), jnp.float32),
            pltpu.VMEM((pool_y * size_z, filters), jnp.float32),
            pltpu.VMEM((3, 4, 3, channels, 2 * filters), weights.dtype),
            pltpu.SemaphoreType.DMA((4,)),
        ],
        compiler_params=pltpu.CompilerParams(vmem_limit_bytes=20 << 20),
        name="encode",
    )(place, far(own), x_in, x_out, y_in, y_out, edge, far(weights))


def far(array):
    return pltpu.with_memory_space_constraint(array, pltpu.HBM)


def prepare(w_full, w_in, w_out):
    channels, filters = w_full.shape[3:]
    depths = [w.shape[4] for w in (w_in, w_out)]

    def body(
        full_hbm, in_hbm, out_hbm, pair_hbm, to_in_hbm, to_out_hbm, full_ref, pair_ref, in_ref, out_ref, to_in_ref, to_out_ref, sems
    ):
        first = pltpu.make_async_copy(full_hbm, full_ref, sems.at[0])
        first.start()
        jobs = []
        for order, (hbm, ref) in enumerate(((in_hbm, in_ref), (out_hbm, out_ref))):
            copies = []
            for step in range(9):
                for dy in range(3):
                    to = ref.at[step, pl.ds(64 * dy, 64)]
                    sem = sems.at[1 + 27 * order + 3 * step + dy]
                    copies.append(pltpu.make_async_copy(hbm.at[step // 3, dy, step % 3], to, sem))
                    copies[-1].start()
            jobs.append(copies)
        first.wait()
        zero = jnp.zeros((3, 3, channels, filters), jnp.bfloat16)
        results = []
        for plane in range(4):
            pair_ref[plane, :, :, :, :filters] = full_ref[plane] if plane < 3 else zero
            pair_ref[plane, :, :, :, filters:] = full_ref[plane - 1] if plane > 0 else zero
            results.append(pltpu.make_async_copy(pair_ref.at[plane], pair_hbm.at[plane], sems.at[55 + plane]))
            results[-1].start()
        for order, (ref, to_ref, to_hbm) in enumerate(((in_ref, to_in_ref, to_in_hbm), (out_ref, to_out_ref, to_out_hbm))):
            for step in range(9):
                ref[step, 192:] = jnp.zeros((64, depths[order]), jnp.bfloat16)
                for copy in jobs[order][3 * step : 3 * step + 3]:
                    copy.wait()
                to_ref[step] = ref[step].T
                results.append(pltpu.make_async_copy(to_ref.at[step], to_hbm.at[step], sems.at[59 + 9 * order + step]))
                results[-1].start()
        for copy in results:
            copy.wait()

    shapes = [(4, 3, 3, channels, 2 * filters)] + [(9, depth, 256) for depth in depths]
    return pl.pallas_call(
        body,
        in_specs=[pl.BlockSpec(memory_space=pltpu.HBM)] * 3,
        out_specs=[pl.BlockSpec(memory_space=pltpu.HBM)] * 3,
        out_shape=[pltpu.HBM(shape, jnp.bfloat16) for shape in shapes],
        scratch_shapes=[pltpu.VMEM(w_full.shape, jnp.bfloat16), pltpu.VMEM(shapes[0], jnp.bfloat16)]
        + [pltpu.VMEM((9, 256, depth), jnp.bfloat16) for depth in depths]
        + [pltpu.VMEM((9, depth, 256), jnp.bfloat16) for depth in depths]
        + [pltpu.SemaphoreType.DMA((77,))],
        compiler_params=pltpu.CompilerParams(vmem_limit_bytes=20 << 20),
        name="prepare",
    )(far(w_full), far(w_in), far(w_out))


def pack_y(place, own, x_in, x_out):
    own_x, own_y, size_z, channels = own.shape
    reach = x_in.shape[0]
    full_x = own_x + 2 * reach

    def body(place_ref, own_ref, x_in_ref, x_out_ref, inner_ref, outer_ref, plane_ref, rows_ref):
        even_x, even_y, first = place_ref[0] % 2 == 0, place_ref[1] % 2 == 0, place_ref[2] == 0
        below = jnp.where(even_x, x_out_ref[...], x_in_ref[...])
        above = jnp.where(even_x, x_in_ref[...], x_out_ref[...])
        for start, block in ((0, below), (reach, own_ref[...]), (reach + own_x, above)):
            size = block.shape[0]
            low, high = block[:, :reach], block[:, own_y - reach :]
            inner_ref[start : start + size] = jnp.where(even_y, high, low)
            outer_ref[start : start + size] = jnp.where(even_y, low, high)
            block = block.astype(jnp.float32)
            edge = jnp.where(first, block[:, :, size_z - 1 :], block[:, :, :1])
            for x in range(size):
                for y in range(own_y):
                    rows_ref[start + x, y : y + 1] = edge[x, y]
        plane_ref[...] = rows_ref[...].astype(plane_ref.dtype)

    return pl.pallas_call(
        body,
        in_specs=[pl.BlockSpec(memory_space=pltpu.SMEM)] + [pl.BlockSpec(memory_space=pltpu.VMEM)] * 3,
        out_specs=[pl.BlockSpec(memory_space=pltpu.VMEM)] * 3,
        out_shape=[jax.ShapeDtypeStruct((full_x, reach, size_z, channels), jnp.bfloat16)] * 2
        + [jax.ShapeDtypeStruct((full_x, own_y, channels), jnp.bfloat16)],
        scratch_shapes=[pltpu.VMEM((full_x, own_y, channels), jnp.float32)],
        compiler_params=pltpu.CompilerParams(vmem_limit_bytes=8 << 20),
        name="pack_y",
    )(place, own, x_in, x_out)


def pack_z(place, plane, y_in, y_out):
    full_x, own_y, channels = plane.shape
    reach, size_z = y_in.shape[1:3]
    full_y = own_y + 2 * reach

    def body(place_ref, plane_ref, y_in_ref, y_out_ref, out_ref, rows_ref):
        even_y, first = place_ref[1] % 2 == 0, place_ref[2] == 0
        rows_ref[:, reach : reach + own_y] = plane_ref[...].astype(jnp.float32)
        edges = []
        for ref in (y_in_ref, y_out_ref):
            block = ref[...].astype(jnp.float32)
            edges.append(jnp.where(first, block[:, :, size_z - 1 :], block[:, :, :1]))
        below, above = jnp.where(even_y, edges[1], edges[0]), jnp.where(even_y, edges[0], edges[1])
        for x in range(full_x):
            for y in range(reach):
                rows_ref[x, y : y + 1] = below[x, y]
                rows_ref[x, reach + own_y + y : reach + own_y + y + 1] = above[x, y]
        out_ref[...] = rows_ref[...].astype(out_ref.dtype)

    return pl.pallas_call(
        body,
        in_specs=[pl.BlockSpec(memory_space=pltpu.SMEM)] + [pl.BlockSpec(memory_space=pltpu.VMEM)] * 3,
        out_specs=pl.BlockSpec(memory_space=pltpu.VMEM),
        out_shape=jax.ShapeDtypeStruct((full_x, full_y, channels), jnp.bfloat16),
        scratch_shapes=[pltpu.VMEM((full_x, full_y, channels), jnp.float32)],
        compiler_params=pltpu.CompilerParams(vmem_limit_bytes=8 << 20),
        name="pack_z",
    )(place, plane, y_in, y_out)


def halves(pair_low, pair_high):
    lane = lax.broadcasted_iota(jnp.int32, pair_low.shape, pair_low.ndim - 1)
    axis = pair_low.ndim - 1
    even = jnp.where(lane < 64, pair_low, pltpu.roll(pair_high, 64, axis))
    odd = jnp.where(lane < 64, pltpu.roll(pair_low, 64, axis), pair_high)
    return even, odd


def side_by_side(even, odd):
    lane = lax.broadcasted_iota(jnp.int32, even.shape, even.ndim - 1)
    return jnp.where(lane < 64, even, pltpu.roll(odd, 64, even.ndim - 1))


def column_product(pad_ref, weights_ref, first, start, planes, size_z):
    channels = pad_ref.shape[-1]
    rows = planes * size_z * 8
    blocks = []
    for dx in range(3):
        for dz in range(3):
            block = pad_ref[first + dx : first + dx + planes, pl.ds(start + dz, size_z)]
            blocks.append(block.reshape(rows, channels).astype(jnp.bfloat16))
    block = jnp.concatenate(blocks, axis=1)
    total = jnp.dot(block, weights_ref[...].reshape(9 * channels, 256), preferred_element_type=jnp.float32)
    low = total[:, :128].reshape(planes * size_z, 8, 128)
    mid = pltpu.roll(total[:, :128], 64, 1).reshape(planes * size_z, 8, 128)
    high = total[:, 128:].reshape(planes * size_z, 8, 128)
    total = pltpu.roll(low, 1, 1) + mid + pltpu.roll(high, 7, 1)
    return jnp.maximum(total, 0.0).reshape(planes, size_z, 8, 128)


def bottom_in(place, field, weights):
    count, own_x, lines, channels = field.shape
    devices = count // 2
    own_z = size_y = 4
    size_x, all_z, size_z = devices * own_x, 2 * own_z, own_z + 2

    def body(place_ref, field_ref, weights_hbm, out_ref, pad_ref, weights_ref, sem):
        copy = pltpu.make_async_copy(weights_hbm, weights_ref, sem)
        copy.start()
        zero = jnp.zeros((all_z + 2, 8, channels), jnp.float32)
        pad_ref[0] = zero
        pad_ref[size_x + 1] = zero
        for x in range(size_x):
            pad_ref[x + 1, 0] = zero[0]
            pad_ref[x + 1, all_z + 1] = zero[0]
        for i in range(devices):
            for half in range(2):
                for x in range(own_x):
                    block = field_ref[2 * i + half, x].astype(jnp.float32)
                    for z in range(own_z):
                        to = (1 + own_x * i + x, 1 + own_z * half + z)
                        pad_ref[*to, 0:1] = block[own_z * size_y + z : own_z * size_y + z + 1]
                        pad_ref[*to, 1 : size_y + 1] = block[size_y * z : size_y * z + size_y]
                        line = own_z * (size_y + 1) + z
                        pad_ref[*to, size_y + 1 : size_y + 2] = block[line : line + 1]
                        pad_ref[*to, size_y + 2 :] = zero[0, size_y + 2 :]
        start = 2 * place_ref[2]
        copy.wait()
        for first in range(0, size_x, 4):
            total = column_product(pad_ref, weights_ref, first, start, 4, size_z)
            for pair in range(2):
                both = side_by_side(total[2 * pair], total[2 * pair + 1])[:, 1 : size_y + 1].astype(out_ref.dtype)
                for i in range(devices):
                    out_ref[i, first // 2 + pair] = both

    return pl.pallas_call(
        body,
        in_specs=[pl.BlockSpec(memory_space=space) for space in (pltpu.SMEM, pltpu.VMEM, pltpu.HBM)],
        out_specs=pl.BlockSpec(memory_space=pltpu.VMEM),
        out_shape=jax.ShapeDtypeStruct((devices, size_x // 2, size_z, size_y, 128), jnp.bfloat16),
        scratch_shapes=[
            pltpu.VMEM((size_x + 2, all_z + 2, 8, channels), jnp.float32),
            pltpu.VMEM(weights.shape, weights.dtype),
            pltpu.SemaphoreType.DMA(()),
        ],
        compiler_params=pltpu.CompilerParams(vmem_limit_bytes=12 << 20),
        name="bottom_in",
    )(place, field, far(weights))


def bottom_out(place, field, y_in, y_out, weights):
    devices, pairs, size_z, _, _ = field.shape
    size_x, channels = 2 * pairs, 64 * devices
    own_x = size_x // devices

    def body(place_ref, field_ref, y_in_ref, y_out_ref, weights_hbm, out_ref, pad_ref, total_ref, weights_ref, sem):
        copy = pltpu.make_async_copy(weights_hbm, weights_ref, sem)
        copy.start()
        even_y = place_ref[1] % 2 == 0
        low_y, high_y = place_ref[1] > 0, place_ref[1] < place_ref[4]
        zero = jnp.zeros((size_z + 2, 8, channels), jnp.float32)
        for ref in (pad_ref, total_ref):
            wide = ref.shape[-1]
            ref[0] = zero[..., :wide]
            ref[size_x + 1] = zero[..., :wide]
            for x in range(size_x):
                ref[x + 1, 0] = zero[0, :, :wide]
                ref[x + 1, size_z + 1] = zero[0, :, :wide]
        for k in range(devices // 2):
            for pair in range(pairs):
                y_first, y_last = [], []
                for i in range(2):
                    one = y_in_ref[2 * k + i, pair].astype(jnp.float32)
                    other = y_out_ref[2 * k + i, pair].astype(jnp.float32)
                    y_first.append(jnp.where(low_y, jnp.where(even_y, other, one), 0.0))
                    y_last.append(jnp.where(high_y, jnp.where(even_y, one, other), 0.0))
                own = [field_ref[2 * k + i, pair].astype(jnp.float32) for i in range(2)]
                for line, blocks in ((0, y_first), (2, own), (6, y_last)):
                    even, odd = halves(*blocks)
                    lines = slice(line, line + even.shape[1])
                    pad_ref[1 + 2 * pair, 1 : size_z + 1, lines, 128 * k : 128 * k + 128] = even
                    pad_ref[2 + 2 * pair, 1 : size_z + 1, lines, 128 * k : 128 * k + 128] = odd
        copy.wait()
        for first in range(0, size_x, 4):
            total = column_product(pad_ref, weights_ref, first, 0, 4, size_z)
            total_ref[1 + first : 5 + first, 1 : size_z + 1] = total
        start = 2 * place_ref[2]
        for i in range(size_x // 2 + 1):
            low, high = [total_ref[2 * i + n, pl.ds(start, size_z)] for n in range(2)]
            both = side_by_side(low, high).astype(out_ref.dtype)
            if i < devices:
                out_ref[i, 0] = both
            if i > 0:
                out_ref[i - 1, 1] = both

    return pl.pallas_call(
        body,
        in_specs=[pl.BlockSpec(memory_space=pltpu.SMEM)]
        + [pl.BlockSpec(memory_space=pltpu.VMEM)] * 3
        + [pl.BlockSpec(memory_space=pltpu.HBM)],
        out_specs=pl.BlockSpec(memory_space=pltpu.VMEM),
        out_shape=jax.ShapeDtypeStruct((devices, own_x, size_z, 8, 128), jnp.bfloat16),
        scratch_shapes=[
            pltpu.VMEM((size_x + 2, size_z + 2, 8, channels), jnp.float32),
            pltpu.VMEM((size_x + 2, size_z + 2, 8, 128), jnp.float32),
            pltpu.VMEM(weights.shape, weights.dtype),
            pltpu.SemaphoreType.DMA(()),
        ],
        compiler_params=pltpu.CompilerParams(vmem_limit_bytes=20 << 20),
        name="bottom_out",
    )(place, field, y_in, y_out, far(weights))


def decode_skip(place, skip, edge, weights):
    full_x, full_y, size_z, channels = skip.shape
    size_x, size_y = full_x - 2, full_y - 2
    filters = weights.shape[-1]
    deep = weights.shape[2] - channels
    rows, extra = size_x * size_y * size_z, size_x * size_y

    def body(skip_ref, edge_ref, weights_hbm, out_ref, *refs):
        rest_refs, (weights_ref, sems) = refs[:3], refs[3:]
        copies = [
            pltpu.make_async_copy(weights_hbm.at[step, :, pl.ds(deep, channels)], weights_ref.at[step], sems.at[step])
            for step in range(9)
        ]
        rest = [
            pltpu.make_async_copy(weights_hbm.at[step, :, pl.ds(0, deep)], rest_refs[step], sems.at[9 + step])
            for step in range(3)
        ]
        for copy in copies + rest:
            copy.start()
        edge_plane = edge_ref[...].astype(jnp.float32)
        blocks = []
        for dx in range(3):
            for dy in range(3):
                main = skip_ref[dx : dx + size_x, dy : dy + size_y].astype(jnp.float32).reshape(rows, channels)
                side = edge_plane[dx : dx + size_x, dy : dy + size_y].reshape(extra, channels)
                blocks.append(jnp.concatenate([main, side], axis=0).astype(jnp.bfloat16))
        for copy in copies:
            copy.wait()
        block = jnp.concatenate(blocks, axis=1)
        for tap in range(3):
            kernel = weights_ref[:, tap].reshape(9 * channels, filters)
            out_ref[tap] = jnp.dot(block, kernel, preferred_element_type=jnp.float32)
        for copy in rest:
            copy.wait()

    return pl.pallas_call(
        body,
        in_specs=[pl.BlockSpec(memory_space=pltpu.VMEM)] * 2 + [pl.BlockSpec(memory_space=pltpu.HBM)],
        out_specs=[pl.BlockSpec(memory_space=pltpu.VMEM)] * 4,
        out_shape=[
            pltpu.VMEM((3, rows + extra, filters), jnp.float32),
        ]
        + [pltpu.VMEM((3, deep, filters), jnp.bfloat16)] * 3,
        scratch_shapes=[pltpu.VMEM((9, 3, channels, filters), jnp.bfloat16), pltpu.SemaphoreType.DMA((12,))],
        compiler_params=pltpu.CompilerParams(vmem_limit_bytes=14 << 20),
        name="decode_skip",
    )(skip, edge, far(weights))


def near(array):
    return pltpu.with_memory_space_constraint(array, pltpu.VMEM)


def decode(place, bottom, skip_sums, first_weights, weights, shape):
    devices, pairs, coarse_z, _, _ = bottom.shape
    size_x, size_y, size_z = shape
    full_x, full_y = size_x + 2, size_y + 2
    channels = 64 * devices
    filters = weights.shape[-1]
    rows, extra = size_x * size_y * size_z, size_x * size_y

    def body(place_ref, bottom_ref, skip_ref, *refs):
        near_refs, (weights_hbm, out_ref, main_ref, side_ref, sums_ref, weights_ref, sems) = refs[:3], refs[3:]
        copies = [
            pltpu.make_async_copy(weights_hbm.at[3 + step, :, pl.ds(0, channels)], weights_ref.at[step], sems.at[step])
            for step in range(6)
        ]
        for copy in copies:
            copy.start()
        first = place_ref[2] == 0
        planes = [[] for _ in range(2 * pairs)]
        for k in range(devices // 2):
            for pair in range(pairs):
                low, high = [bottom_ref[2 * k + i, pair].astype(jnp.float32) for i in range(2)]
                even, odd = halves(low, high)
                planes[2 * pair].append(even.reshape(coarse_z * 8, 128))
                planes[2 * pair + 1].append(odd.reshape(coarse_z * 8, 128))

        def choice(y, z, source):
            line = (y + 1) // 2 + 1
            inside = ((line > 1) | (place_ref[1] > 0)) & ((line < coarse_z) | (place_ref[1] < place_ref[4]))
            return jnp.where((source == z * 8 + line) & inside, 1.0, 0.0).astype(jnp.bfloat16)

        shape = (full_y * size_z, coarse_z * 8)
        row = lax.broadcasted_iota(jnp.int32, shape, 0)
        spread = choice(row // size_z, row % size_z // 2 + 1, lax.broadcasted_iota(jnp.int32, shape, 1))
        shape = (16, coarse_z * 8)
        row = lax.broadcasted_iota(jnp.int32, shape, 0)
        other = jnp.where(first, coarse_z - 1, 0)
        spread_edge = choice(row, other, lax.broadcasted_iota(jnp.int32, shape, 1))
        for plane in range(2 * pairs):
            coarse = jnp.concatenate(planes[plane], axis=1).astype(jnp.bfloat16)
            fine = jnp.dot(spread, coarse, preferred_element_type=jnp.float32)
            fine_edge = jnp.dot(spread_edge, coarse, preferred_element_type=jnp.float32)
            for x in range(full_x):
                if (x + 1) // 2 != plane:
                    continue
                for dy in range(3):
                    main_ref[dy, x] = fine[8 * dy : 8 * dy + size_y * size_z].astype(jnp.bfloat16)
                    side_ref[dy, x] = fine_edge[dy : dy + size_y]
        for dx in range(3):
            blocks = []
            for dy in range(3):
                main = main_ref[dy, dx : dx + size_x].reshape(rows, channels)
                side = side_ref[dy, dx : dx + size_x].reshape(extra, channels).astype(jnp.bfloat16)
                blocks.append(jnp.concatenate([main, side], axis=0))
                if dx:
                    copies[3 * dx + dy - 3].wait()
            block = jnp.concatenate(blocks, axis=1)
            for tap in range(3):
                if dx == 0:
                    kernel = jnp.concatenate([ref[tap] for ref in near_refs], axis=0)
                    sums_ref[tap] = skip_ref[tap] + jnp.dot(block, kernel, preferred_element_type=jnp.float32)
                else:
                    kernel = weights_ref[3 * dx - 3 : 3 * dx, tap].reshape(3 * channels, filters)
                    sums_ref[tap] += jnp.dot(block, kernel, preferred_element_type=jnp.float32)
        total = join_taps(first, [sums_ref[tap] for tap in range(3)], extra, size_z)
        out_ref[...] = total.reshape(size_x, size_y, size_z, filters).astype(out_ref.dtype)

    return pl.pallas_call(
        body,
        in_specs=[pl.BlockSpec(memory_space=pltpu.SMEM)]
        + [pl.BlockSpec(memory_space=pltpu.VMEM)] * 5
        + [pl.BlockSpec(memory_space=pltpu.HBM)],
        out_specs=pl.BlockSpec(memory_space=pltpu.VMEM),
        out_shape=jax.ShapeDtypeStruct((size_x, size_y, size_z, filters), jnp.bfloat16),
        scratch_shapes=[
            pltpu.VMEM((3, full_x, size_y * size_z, channels), jnp.bfloat16),
            pltpu.VMEM((3, full_x, size_y, channels), jnp.float32),
            pltpu.VMEM((3, rows + extra, filters), jnp.float32),
            pltpu.VMEM((6, 3, channels, filters), jnp.bfloat16),
            pltpu.SemaphoreType.DMA((6,)),
        ],
        compiler_params=pltpu.CompilerParams(vmem_limit_bytes=20 << 20),
        name="decode",
    )(place, bottom, near(skip_sums), *map(near, first_weights), far(weights))


def solution(mesh):
    gx, gy, gz = mesh.shape["gx"], mesh.shape["gy"], mesh.shape["gz"]

    def local(volume, w_full, w_half, w_bottom_in, w_bottom_out, w_up):
        place_z = lax.axis_index("gz")
        place = jnp.stack([lax.axis_index("gx"), lax.axis_index("gy"), place_z, jnp.int32(gx - 1), jnp.int32(gy - 1)])
        swap = [(0, 1), (1, 0)]

        def edge_of(plane_low, plane_high):
            return lax.ppermute(jnp.where(place_z == 0, plane_high, plane_low), "gz", swap)

        x_in, x_out = swaps(volume[:3], volume[-3:], "gx", gx)
        turned = [w.transpose(0, 1, 2, 4, 3) for w in (w_bottom_in, w_bottom_out)]
        (w_pair, w_in, w_out), x_in, x_out = lax.optimization_barrier((prepare(w_full, *turned), x_in, x_out))
        y_inner, y_outer, plane = pack_y(place, volume, x_in, x_out)
        y_in, y_out = send(y_inner, y_outer, "gy", gy)
        edge = lax.ppermute(pack_z(place, plane, y_in, y_out), "gz", swap)
        pooled = encode(place, volume, x_in, x_out, y_in, y_out, edge, w_pair)

        edge = edge_of(pooled[:, :, 0], pooled[:, :, -1])
        skip, coarse = half_level(place, pooled, edge, w_half.reshape(9, 3, w_half.shape[3], w_half.shape[4]))
        lines = coarse.reshape(coarse.shape[0], 4, 4, coarse.shape[2])
        below, above = halo(lines, "gy", gy, 2, 1)
        column = jnp.concatenate([coarse, below[:, :, 0], above[:, :, 0]], axis=1)
        column = jnp.broadcast_to(column[None], (gx * gz,) + column.shape)
        column = lax.all_to_all(column, ("gx", "gz"), 0, 0)
        first = bottom_in(place, column, w_in)
        first = lax.all_to_all(first, "gx", 0, 0)
        y_in, y_out = swaps(first[:, :, :, :2], first[:, :, :, -2:], "gy", gy)
        around = extend(skip, "gx", gx, 0, 1)
        around = extend(around, "gy", gy, 1, 1)
        side = edge_of(around[:, :, 0], around[:, :, -1])
        y_in, y_out, around, side = lax.optimization_barrier((y_in, y_out, around, side))
        second = bottom_out(place, first, y_in, y_out, w_out)
        second = lax.all_to_all(second, "gx", 0, 0)
        w_up = w_up.reshape(9, 3, w_up.shape[3], w_up.shape[4])
        skip_sums, *w_near = decode_skip(place, around, side, w_up)
        return decode(place, second, skip_sums, w_near, w_up, skip.shape[:3])

    space = P("gx", "gy", "gz", None)
    filters = P(None, None, None, None, "gx")
    return jax.shard_map(
        local,
        mesh=mesh,
        in_specs=(space, P(), P(), filters, filters, P()),
        out_specs=space,
        check_vma=False,
    )
```

```python
import jax
import jax.numpy as jnp
from jax import lax
from jax.experimental import pallas as pl
from jax.experimental.pallas import tpu as pltpu
from jax.sharding import PartitionSpec as P


def send(inner_block, outer_block, axis, count):
    inner = [(i, i ^ 1) for i in range(count)]
    outer = [(i, (((i + 1) ^ 1) - 1) % count) for i in range(count)]
    return lax.ppermute(inner_block, axis, inner), lax.ppermute(outer_block, axis, outer)


def swaps(low, high, axis, count):
    even = lax.axis_index(axis) % 2 == 0
    return send(jnp.where(even, high, low), jnp.where(even, low, high), axis, count)


def ordered(got_in, got_out, axis):
    even = lax.axis_index(axis) % 2 == 0
    return jnp.where(even, got_out, got_in), jnp.where(even, got_in, got_out)


def halo(field, axis, count, dim, width):
    place = lax.axis_index(axis)
    size = field.shape[dim]
    low = lax.slice_in_dim(field, 0, width, axis=dim)
    high = lax.slice_in_dim(field, size - width, size, axis=dim)
    below, above = ordered(*swaps(low, high, axis, count), axis)
    zero = jnp.zeros_like(low)
    return jnp.where(place > 0, below, zero), jnp.where(place < count - 1, above, zero)


def extend(field, axis, count, dim, width):
    below, above = halo(field, axis, count, dim, width)
    return jnp.concatenate([below, field, above], axis=dim)


def half_level(place, field, edge, weights):
    full_x, full_y, size_z, channels = field.shape
    size_x, size_y = full_x - 2, full_y - 2
    filters = weights.shape[-1]
    rows, extra = size_x * size_y * size_z, size_x * size_y

    def body(place_ref, field_ref, edge_ref, weights_ref, out_ref, coarse_ref, rows_ref, coarse_rows_ref):
        first = place_ref[2] == 0
        edge_plane = edge_ref[...].astype(jnp.float32)
        blocks = []
        for dx in range(3):
            for dy in range(3):
                main = field_ref[dx : dx + size_x, dy : dy + size_y].astype(jnp.float32).reshape(rows, channels)
                side = edge_plane[dx : dx + size_x, dy : dy + size_y].reshape(extra, channels)
                blocks.append(jnp.concatenate([main, side], axis=0).astype(jnp.bfloat16))
        block = jnp.concatenate(blocks, axis=1)
        sums = []
        for tap in range(3):
            kernel = weights_ref[:, tap].reshape(9 * channels, filters)
            sums.append(jnp.dot(block, kernel, preferred_element_type=jnp.float32))
        total = jnp.maximum(join_taps(first, sums, extra, size_z), 0.0)
        out_ref[...] = total.reshape(size_x, size_y, size_z, filters).astype(out_ref.dtype)
        total = jnp.max(total.reshape(size_x // 2, 2, size_y // 2, 2, size_z, filters), axis=(1, 3))
        count = size_y // 2
        for part in range(filters // 128):
            rows_ref[...] = total[..., 128 * part : 128 * part + 128].reshape(rows // 4, 128)
            for x in range(size_x // 2):
                for z in range(size_z // 2):
                    start = x * count * size_z + 2 * z
                    pooled = jnp.maximum(
                        rows_ref[pl.ds(start, count, stride=size_z), :], rows_ref[pl.ds(start + 1, count, stride=size_z), :]
                    )
                    coarse_rows_ref[x, count * z : count * z + count, 128 * part : 128 * part + 128] = pooled
        coarse_ref[...] = coarse_rows_ref[...].astype(coarse_ref.dtype)

    return pl.pallas_call(
        body,
        in_specs=[pl.BlockSpec(memory_space=pltpu.SMEM)] + [pl.BlockSpec(memory_space=pltpu.VMEM)] * 3,
        out_specs=[pl.BlockSpec(memory_space=pltpu.VMEM)] * 2,
        out_shape=[
            jax.ShapeDtypeStruct((size_x, size_y, size_z, filters), jnp.bfloat16),
            jax.ShapeDtypeStruct((size_x // 2, size_z * size_y // 4, filters), jnp.bfloat16),
        ],
        scratch_shapes=[
            pltpu.VMEM((rows // 4, 128), jnp.float32),
            pltpu.VMEM((size_x // 2, size_z * size_y // 4, filters), jnp.float32),
        ],
        compiler_params=pltpu.CompilerParams(vmem_limit_bytes=12 << 20),
        name="half_level",
    )(place, field, edge, weights)


def join_taps(first, sums, groups, size_z):
    rows, filters = groups * size_z, sums[0].shape[-1]
    low, mid, high = [total[:rows].reshape(groups, size_z, filters) for total in sums]
    below = jnp.where(first, 0.0, sums[0][rows : rows + groups])
    above = jnp.where(first, sums[2][rows : rows + groups], 0.0)
    index = lax.broadcasted_iota(jnp.int32, (groups, size_z, filters), 1)
    down = jnp.where(index == 0, below[:, None, :], pltpu.roll(low, 1, 1))
    up = jnp.where(index == size_z - 1, above[:, None, :], pltpu.roll(high, size_z - 1, 1))
    return down + mid + up


def assemble(place, own, x_in, x_out, y_in, y_out, weights):
    own_x, own_y, size_z, channels = own.shape
    reach = x_in.shape[0]
    full_x, full_y = own_x + 2 * reach, own_y + 2 * reach

    def body(
        place_ref, own_hbm, x_in_ref, x_out_ref, y_in_ref, y_out_ref, weights_hbm, field_ref, weights_ref, sems
    ):
        inner = field_ref.at[reach : reach + own_x, reach : reach + own_y]
        copies = [pltpu.make_async_copy(own_hbm, inner, sems.at[0])]
        for plane in range(4):
            copies.append(pltpu.make_async_copy(weights_hbm.at[plane], weights_ref.at[plane], sems.at[1 + plane]))
        for copy in copies:
            copy.start()
        even_x, even_y = place_ref[0] % 2 == 0, place_ref[1] % 2 == 0
        low_x, high_x = place_ref[0] > 0, place_ref[0] < place_ref[3]
        low_y, high_y = place_ref[1] > 0, place_ref[1] < place_ref[4]
        nil = jnp.bfloat16(0)
        inner_y = slice(reach, reach + own_y)
        below, above = jnp.where(even_x, x_out_ref[...], x_in_ref[...]), jnp.where(even_x, x_in_ref[...], x_out_ref[...])
        field_ref[:reach, inner_y] = jnp.where(low_x, below, nil)
        field_ref[reach + own_x :, inner_y] = jnp.where(high_x, above, nil)
        for x in range(full_x):
            here_low, here_high = low_y, high_y
            if x < reach:
                here_low, here_high = low_y & low_x, high_y & low_x
            if x >= reach + own_x:
                here_low, here_high = low_y & high_x, high_y & high_x
            below, above = jnp.where(even_y, y_out_ref[x], y_in_ref[x]), jnp.where(even_y, y_in_ref[x], y_out_ref[x])
            field_ref[x, :reach] = jnp.where(here_low, below, nil)
            field_ref[x, reach + own_y :] = jnp.where(here_high, above, nil)
        for copy in copies:
            copy.wait()

    return pl.pallas_call(
        body,
        in_specs=[pl.BlockSpec(memory_space=pltpu.SMEM), pl.BlockSpec(memory_space=pltpu.HBM)]
        + [pl.BlockSpec(memory_space=pltpu.VMEM)] * 4
        + [pl.BlockSpec(memory_space=pltpu.HBM)],
        out_specs=[pl.BlockSpec(memory_space=pltpu.VMEM)] * 2,
        out_shape=[
            pltpu.VMEM((full_x, full_y, size_z, channels), jnp.bfloat16),
            pltpu.VMEM(weights.shape, weights.dtype),
        ],
        scratch_shapes=[pltpu.SemaphoreType.DMA((5,))],
        compiler_params=pltpu.CompilerParams(vmem_limit_bytes=4 << 20),
        name="assemble",
    )(place, far(own), x_in, x_out, y_in, y_out, far(weights))


def encode(place, field, edge, weights):
    full_x, full_y, size_z, channels = field.shape
    reach = 3
    size_x, size_y = full_x - 2, full_y - 2
    own_x, own_y = full_x - 2 * reach, full_y - 2 * reach
    filters = weights.shape[-1] // 2
    rows, extra = size_y * size_z, size_y + (-size_y % 16)
    pool_y, pool_z = size_y // 2, size_z // 2

    def body(place_ref, field_ref, edge_ref, weights_ref, out_ref, side_ref, rows_ref):
        low_x, high_x = place_ref[0] > 0, place_ref[0] < place_ref[3]
        low_y, high_y = place_ref[1] > 0, place_ref[1] < place_ref[4]
        for x in range(full_x):
            line = lax.broadcasted_iota(jnp.int32, (full_y, channels), 0)
            inside = ((line >= reach) | low_y) & ((line < reach + own_y) | high_y)
            if x < reach:
                inside = inside & low_x
            if x >= reach + own_x:
                inside = inside & high_x
            plane = jnp.where(inside, edge_ref[x].astype(jnp.float32), 0.0)
            for dy in range(3):
                side_ref[dy, x, :size_y] = plane[dy : dy + size_y]
                side_ref[dy, x, size_y:] = jnp.zeros((extra - size_y, channels), jnp.float32)

        first = place_ref[2] == 0
        line = lax.broadcasted_iota(jnp.int32, (pool_y, pool_z, filters), 0)
        inside_y = ((line > 0) | low_y) & ((line < pool_y - 1) | high_y)
        for pair in range(size_x // 2):
            blocks = []
            for plane in range(4):
                for dy in range(3):
                    main = field_ref[2 * pair + plane, dy : dy + size_y].reshape(rows, channels)
                    side = side_ref[dy, 2 * pair + plane].astype(jnp.bfloat16)
                    blocks.append(jnp.concatenate([main, side], axis=0))
            block = jnp.concatenate(blocks, axis=1)
            sums = []
            for tap in range(3):
                kernel = weights_ref[:, :, tap].reshape(12 * channels, 2 * filters)
                sums.append(jnp.dot(block, kernel, preferred_element_type=jnp.float32))
            total = jnp.maximum(join_taps(first, sums, size_y, size_z), 0.0)
            total = jnp.maximum(total[..., :filters], total[..., filters:])
            total = jnp.max(total.reshape(pool_y, 2, size_z, filters), axis=1)
            rows_ref[...] = total.reshape(pool_y * size_z, filters)
            total = jnp.maximum(
                rows_ref[pl.ds(0, pool_y * pool_z, stride=2), :], rows_ref[pl.ds(1, pool_y * pool_z, stride=2), :]
            ).reshape(pool_y, pool_z, filters)
            inside = inside_y
            if pair == 0:
                inside = inside & low_x
            if pair == size_x // 2 - 1:
                inside = inside & high_x
            out_ref[pair] = jnp.where(inside, total, 0.0).astype(out_ref.dtype)

    return pl.pallas_call(
        body,
        in_specs=[pl.BlockSpec(memory_space=pltpu.SMEM)] + [pl.BlockSpec(memory_space=pltpu.VMEM)] * 3,
        out_specs=pl.BlockSpec(memory_space=pltpu.VMEM),
        out_shape=jax.ShapeDtypeStruct((size_x // 2, pool_y, pool_z, filters), jnp.bfloat16),
        scratch_shapes=[
            pltpu.VMEM((3, full_x, extra, channels), jnp.float32),
            pltpu.VMEM((pool_y * size_z, filters), jnp.float32),
        ],
        compiler_params=pltpu.CompilerParams(vmem_limit_bytes=14 << 20),
        name="encode",
    )(place, near(field), edge, near(weights))


def near(array):
    return pltpu.with_memory_space_constraint(array, pltpu.VMEM)


def bring(weights, after):
    def body(weights_hbm, after_ref, out_ref, sems):
        copies = [pltpu.make_async_copy(weights_hbm.at[step], out_ref.at[step], sems.at[step]) for step in range(9)]
        for copy in copies:
            copy.start()
        for copy in copies:
            copy.wait()

    return pl.pallas_call(
        body,
        in_specs=[pl.BlockSpec(memory_space=pltpu.HBM), pl.BlockSpec(memory_space=pl.ANY)],
        out_specs=pl.BlockSpec(memory_space=pltpu.VMEM),
        out_shape=pltpu.VMEM(weights.shape, weights.dtype),
        scratch_shapes=[pltpu.SemaphoreType.DMA((9,))],
        compiler_params=pltpu.CompilerParams(vmem_limit_bytes=4 << 20),
        name="bring",
    )(far(weights), after)


def far(array):
    return pltpu.with_memory_space_constraint(array, pltpu.HBM)


def prepare(w_full, w_in, w_out):
    channels, filters = w_full.shape[3:]
    depths = [w.shape[4] for w in (w_in, w_out)]

    def body(
        full_hbm, in_hbm, out_hbm, pair_hbm, to_in_hbm, to_out_hbm, full_ref, pair_ref, in_ref, out_ref, to_in_ref, to_out_ref, sems
    ):
        first = pltpu.make_async_copy(full_hbm, full_ref, sems.at[0])
        first.start()
        jobs = []
        for order, (hbm, ref) in enumerate(((in_hbm, in_ref), (out_hbm, out_ref))):
            copies = []
            for step in range(9):
                for dy in range(3):
                    to = ref.at[step, pl.ds(64 * dy, 64)]
                    sem = sems.at[1 + 27 * order + 3 * step + dy]
                    copies.append(pltpu.make_async_copy(hbm.at[step // 3, dy, step % 3], to, sem))
                    copies[-1].start()
            jobs.append(copies)
        first.wait()
        zero = jnp.zeros((3, 3, channels, filters), jnp.bfloat16)
        results = []
        for plane in range(4):
            pair_ref[plane, :, :, :, :filters] = full_ref[plane] if plane < 3 else zero
            pair_ref[plane, :, :, :, filters:] = full_ref[plane - 1] if plane > 0 else zero
            results.append(pltpu.make_async_copy(pair_ref.at[plane], pair_hbm.at[plane], sems.at[55 + plane]))
            results[-1].start()
        for order, (ref, to_ref, to_hbm) in enumerate(((in_ref, to_in_ref, to_in_hbm), (out_ref, to_out_ref, to_out_hbm))):
            for step in range(9):
                ref[step, 192:] = jnp.zeros((64, depths[order]), jnp.bfloat16)
                for copy in jobs[order][3 * step : 3 * step + 3]:
                    copy.wait()
                to_ref[step] = ref[step].T
                results.append(pltpu.make_async_copy(to_ref.at[step], to_hbm.at[step], sems.at[59 + 9 * order + step]))
                results[-1].start()
        for copy in results:
            copy.wait()

    shapes = [(4, 3, 3, channels, 2 * filters)] + [(9, depth, 256) for depth in depths]
    return pl.pallas_call(
        body,
        in_specs=[pl.BlockSpec(memory_space=pltpu.HBM)] * 3,
        out_specs=[pl.BlockSpec(memory_space=pltpu.HBM)] * 3,
        out_shape=[pltpu.HBM(shape, jnp.bfloat16) for shape in shapes],
        scratch_shapes=[pltpu.VMEM(w_full.shape, jnp.bfloat16), pltpu.VMEM(shapes[0], jnp.bfloat16)]
        + [pltpu.VMEM((9, 256, depth), jnp.bfloat16) for depth in depths]
        + [pltpu.VMEM((9, depth, 256), jnp.bfloat16) for depth in depths]
        + [pltpu.SemaphoreType.DMA((77,))],
        compiler_params=pltpu.CompilerParams(vmem_limit_bytes=20 << 20),
        name="prepare",
    )(far(w_full), far(w_in), far(w_out))


def pack_y(place, own, x_in, x_out):
    own_x, own_y, size_z, channels = own.shape
    reach = x_in.shape[0]
    full_x = own_x + 2 * reach

    def body(place_ref, own_ref, x_in_ref, x_out_ref, inner_ref, outer_ref, plane_ref, rows_ref):
        even_x, even_y, first = place_ref[0] % 2 == 0, place_ref[1] % 2 == 0, place_ref[2] == 0
        below = jnp.where(even_x, x_out_ref[...], x_in_ref[...])
        above = jnp.where(even_x, x_in_ref[...], x_out_ref[...])
        for start, block in ((0, below), (reach, own_ref[...]), (reach + own_x, above)):
            size = block.shape[0]
            low, high = block[:, :reach], block[:, own_y - reach :]
            inner_ref[start : start + size] = jnp.where(even_y, high, low)
            outer_ref[start : start + size] = jnp.where(even_y, low, high)
            block = block.astype(jnp.float32)
            edge = jnp.where(first, block[:, :, size_z - 1 :], block[:, :, :1])
            for x in range(size):
                for y in range(own_y):
                    rows_ref[start + x, y : y + 1] = edge[x, y]
        plane_ref[...] = rows_ref[...].astype(plane_ref.dtype)

    return pl.pallas_call(
        body,
        in_specs=[pl.BlockSpec(memory_space=pltpu.SMEM)] + [pl.BlockSpec(memory_space=pltpu.VMEM)] * 3,
        out_specs=[pl.BlockSpec(memory_space=pltpu.VMEM)] * 3,
        out_shape=[jax.ShapeDtypeStruct((full_x, reach, size_z, channels), jnp.bfloat16)] * 2
        + [jax.ShapeDtypeStruct((full_x, own_y, channels), jnp.bfloat16)],
        scratch_shapes=[pltpu.VMEM((full_x, own_y, channels), jnp.float32)],
        compiler_params=pltpu.CompilerParams(vmem_limit_bytes=8 << 20),
        name="pack_y",
    )(place, own, x_in, x_out)


def pack_z(place, plane, y_in, y_out):
    full_x, own_y, channels = plane.shape
    reach, size_z = y_in.shape[1:3]
    full_y = own_y + 2 * reach

    def body(place_ref, plane_ref, y_in_ref, y_out_ref, out_ref, rows_ref):
        even_y, first = place_ref[1] % 2 == 0, place_ref[2] == 0
        rows_ref[:, reach : reach + own_y] = plane_ref[...].astype(jnp.float32)
        edges = []
        for ref in (y_in_ref, y_out_ref):
            block = ref[...].astype(jnp.float32)
            edges.append(jnp.where(first, block[:, :, size_z - 1 :], block[:, :, :1]))
        below, above = jnp.where(even_y, edges[1], edges[0]), jnp.where(even_y, edges[0], edges[1])
        for x in range(full_x):
            for y in range(reach):
                rows_ref[x, y : y + 1] = below[x, y]
                rows_ref[x, reach + own_y + y : reach + own_y + y + 1] = above[x, y]
        out_ref[...] = rows_ref[...].astype(out_ref.dtype)

    return pl.pallas_call(
        body,
        in_specs=[pl.BlockSpec(memory_space=pltpu.SMEM)] + [pl.BlockSpec(memory_space=pltpu.VMEM)] * 3,
        out_specs=pl.BlockSpec(memory_space=pltpu.VMEM),
        out_shape=jax.ShapeDtypeStruct((full_x, full_y, channels), jnp.bfloat16),
        scratch_shapes=[pltpu.VMEM((full_x, full_y, channels), jnp.float32)],
        compiler_params=pltpu.CompilerParams(vmem_limit_bytes=8 << 20),
        name="pack_z",
    )(place, plane, y_in, y_out)


def halves(pair_low, pair_high):
    lane = lax.broadcasted_iota(jnp.int32, pair_low.shape, pair_low.ndim - 1)
    axis = pair_low.ndim - 1
    even = jnp.where(lane < 64, pair_low, pltpu.roll(pair_high, 64, axis))
    odd = jnp.where(lane < 64, pltpu.roll(pair_low, 64, axis), pair_high)
    return even, odd


def side_by_side(even, odd):
    lane = lax.broadcasted_iota(jnp.int32, even.shape, even.ndim - 1)
    return jnp.where(lane < 64, even, pltpu.roll(odd, 64, even.ndim - 1))


def column_product(pad_ref, weights_ref, first, start, planes, size_z):
    channels = pad_ref.shape[-1]
    rows = planes * size_z * 8
    blocks = []
    for dx in range(3):
        for dz in range(3):
            block = pad_ref[first + dx : first + dx + planes, pl.ds(start + dz, size_z)]
            blocks.append(block.reshape(rows, channels).astype(jnp.bfloat16))
    block = jnp.concatenate(blocks, axis=1)
    total = jnp.dot(block, weights_ref[...].reshape(9 * channels, 256), preferred_element_type=jnp.float32)
    low = total[:, :128].reshape(planes * size_z, 8, 128)
    mid = pltpu.roll(total[:, :128], 64, 1).reshape(planes * size_z, 8, 128)
    high = total[:, 128:].reshape(planes * size_z, 8, 128)
    total = pltpu.roll(low, 1, 1) + mid + pltpu.roll(high, 7, 1)
    return jnp.maximum(total, 0.0).reshape(planes, size_z, 8, 128)


def bottom_in(place, field, weights):
    count, own_x, lines, channels = field.shape
    devices = count // 2
    own_z = size_y = 4
    size_x, all_z, size_z = devices * own_x, 2 * own_z, own_z + 2

    def body(place_ref, field_ref, weights_ref, out_ref, pad_ref):
        zero = jnp.zeros((all_z + 2, 8, channels), jnp.float32)
        pad_ref[0] = zero
        pad_ref[size_x + 1] = zero
        for x in range(size_x):
            pad_ref[x + 1, 0] = zero[0]
            pad_ref[x + 1, all_z + 1] = zero[0]
        for i in range(devices):
            for half in range(2):
                for x in range(own_x):
                    block = field_ref[2 * i + half, x].astype(jnp.float32)
                    for z in range(own_z):
                        to = (1 + own_x * i + x, 1 + own_z * half + z)
                        pad_ref[*to, 0:1] = block[own_z * size_y + z : own_z * size_y + z + 1]
                        pad_ref[*to, 1 : size_y + 1] = block[size_y * z : size_y * z + size_y]
                        line = own_z * (size_y + 1) + z
                        pad_ref[*to, size_y + 1 : size_y + 2] = block[line : line + 1]
                        pad_ref[*to, size_y + 2 :] = zero[0, size_y + 2 :]
        start = 2 * place_ref[2]
        for first in range(0, size_x, 4):
            total = column_product(pad_ref, weights_ref, first, start, 4, size_z)
            for pair in range(2):
                both = side_by_side(total[2 * pair], total[2 * pair + 1])[:, 1 : size_y + 1].astype(out_ref.dtype)
                for i in range(devices):
                    out_ref[i, first // 2 + pair] = both

    return pl.pallas_call(
        body,
        in_specs=[pl.BlockSpec(memory_space=space) for space in (pltpu.SMEM, pltpu.VMEM, pltpu.VMEM)],
        out_specs=pl.BlockSpec(memory_space=pltpu.VMEM),
        out_shape=jax.ShapeDtypeStruct((devices, size_x // 2, size_z, size_y, 128), jnp.bfloat16),
        scratch_shapes=[
            pltpu.VMEM((size_x + 2, all_z + 2, 8, channels), jnp.float32),
        ],
        compiler_params=pltpu.CompilerParams(vmem_limit_bytes=12 << 20),
        name="bottom_in",
    )(place, field, near(weights))


def bottom_out(place, field, y_in, y_out, weights):
    devices, pairs, size_z, _, _ = field.shape
    size_x, channels = 2 * pairs, 64 * devices
    own_x = size_x // devices

    def body(place_ref, field_ref, y_in_ref, y_out_ref, weights_ref, out_ref, pad_ref, total_ref):
        even_y = place_ref[1] % 2 == 0
        low_y, high_y = place_ref[1] > 0, place_ref[1] < place_ref[4]
        zero = jnp.zeros((size_z + 2, 8, channels), jnp.float32)
        for ref in (pad_ref, total_ref):
            wide = ref.shape[-1]
            ref[0] = zero[..., :wide]
            ref[size_x + 1] = zero[..., :wide]
            for x in range(size_x):
                ref[x + 1, 0] = zero[0, :, :wide]
                ref[x + 1, size_z + 1] = zero[0, :, :wide]
        for k in range(devices // 2):
            for pair in range(pairs):
                y_first, y_last = [], []
                for i in range(2):
                    one = y_in_ref[2 * k + i, pair].astype(jnp.float32)
                    other = y_out_ref[2 * k + i, pair].astype(jnp.float32)
                    y_first.append(jnp.where(low_y, jnp.where(even_y, other, one), 0.0))
                    y_last.append(jnp.where(high_y, jnp.where(even_y, one, other), 0.0))
                own = [field_ref[2 * k + i, pair].astype(jnp.float32) for i in range(2)]
                for line, blocks in ((0, y_first), (2, own), (6, y_last)):
                    even, odd = halves(*blocks)
                    lines = slice(line, line + even.shape[1])
                    pad_ref[1 + 2 * pair, 1 : size_z + 1, lines, 128 * k : 128 * k + 128] = even
                    pad_ref[2 + 2 * pair, 1 : size_z + 1, lines, 128 * k : 128 * k + 128] = odd
        for first in range(0, size_x, 4):
            total = column_product(pad_ref, weights_ref, first, 0, 4, size_z)
            total_ref[1 + first : 5 + first, 1 : size_z + 1] = total
        start = 2 * place_ref[2]
        for i in range(size_x // 2 + 1):
            low, high = [total_ref[2 * i + n, pl.ds(start, size_z)] for n in range(2)]
            both = side_by_side(low, high).astype(out_ref.dtype)
            if i < devices:
                out_ref[i, 0] = both
            if i > 0:
                out_ref[i - 1, 1] = both

    return pl.pallas_call(
        body,
        in_specs=[pl.BlockSpec(memory_space=pltpu.SMEM)]
        + [pl.BlockSpec(memory_space=pltpu.VMEM)] * 4,
        out_specs=pl.BlockSpec(memory_space=pltpu.VMEM),
        out_shape=jax.ShapeDtypeStruct((devices, own_x, size_z, 8, 128), jnp.bfloat16),
        scratch_shapes=[
            pltpu.VMEM((size_x + 2, size_z + 2, 8, channels), jnp.float32),
            pltpu.VMEM((size_x + 2, size_z + 2, 8, 128), jnp.float32),
        ],
        compiler_params=pltpu.CompilerParams(vmem_limit_bytes=16 << 20),
        name="bottom_out",
    )(place, field, y_in, y_out, near(weights))


def decode_skip(place, skip, edge, weights):
    full_x, full_y, size_z, channels = skip.shape
    size_x, size_y = full_x - 2, full_y - 2
    filters = weights.shape[-1]
    deep = weights.shape[2] - channels
    rows, extra = size_x * size_y * size_z, size_x * size_y

    def body(skip_ref, edge_ref, weights_hbm, out_ref, *refs):
        rest_refs, (weights_ref, sems) = refs[:3], refs[3:]
        copies = [
            pltpu.make_async_copy(weights_hbm.at[step, :, pl.ds(deep, channels)], weights_ref.at[step], sems.at[step])
            for step in range(9)
        ]
        rest = [
            pltpu.make_async_copy(weights_hbm.at[step, :, pl.ds(0, deep)], rest_refs[step], sems.at[9 + step])
            for step in range(3)
        ]
        for copy in copies + rest:
            copy.start()
        edge_plane = edge_ref[...].astype(jnp.float32)
        blocks = []
        for dx in range(3):
            for dy in range(3):
                main = skip_ref[dx : dx + size_x, dy : dy + size_y].astype(jnp.float32).reshape(rows, channels)
                side = edge_plane[dx : dx + size_x, dy : dy + size_y].reshape(extra, channels)
                blocks.append(jnp.concatenate([main, side], axis=0).astype(jnp.bfloat16))
        for copy in copies:
            copy.wait()
        block = jnp.concatenate(blocks, axis=1)
        for tap in range(3):
            kernel = weights_ref[:, tap].reshape(9 * channels, filters)
            out_ref[tap] = jnp.dot(block, kernel, preferred_element_type=jnp.float32)
        for copy in rest:
            copy.wait()

    return pl.pallas_call(
        body,
        in_specs=[pl.BlockSpec(memory_space=pltpu.VMEM)] * 2 + [pl.BlockSpec(memory_space=pltpu.HBM)],
        out_specs=[pl.BlockSpec(memory_space=pltpu.VMEM)] * 4,
        out_shape=[
            pltpu.VMEM((3, rows + extra, filters), jnp.float32),
        ]
        + [pltpu.VMEM((3, deep, filters), jnp.bfloat16)] * 3,
        scratch_shapes=[pltpu.VMEM((9, 3, channels, filters), jnp.bfloat16), pltpu.SemaphoreType.DMA((12,))],
        compiler_params=pltpu.CompilerParams(vmem_limit_bytes=14 << 20),
        name="decode_skip",
    )(skip, edge, far(weights))


def decode(place, bottom, skip_sums, first_weights, weights, shape):
    devices, pairs, coarse_z, _, _ = bottom.shape
    size_x, size_y, size_z = shape
    full_x, full_y = size_x + 2, size_y + 2
    channels = 64 * devices
    filters = weights.shape[-1]
    rows, extra = size_x * size_y * size_z, size_x * size_y

    def body(place_ref, bottom_ref, skip_ref, *refs):
        near_refs, (weights_hbm, out_ref, main_ref, side_ref, sums_ref, weights_ref, sems) = refs[:3], refs[3:]
        copies = [
            pltpu.make_async_copy(weights_hbm.at[3 + step, :, pl.ds(0, channels)], weights_ref.at[step], sems.at[step])
            for step in range(6)
        ]
        for copy in copies:
            copy.start()
        first = place_ref[2] == 0
        planes = [[] for _ in range(2 * pairs)]
        for k in range(devices // 2):
            for pair in range(pairs):
                low, high = [bottom_ref[2 * k + i, pair].astype(jnp.float32) for i in range(2)]
                even, odd = halves(low, high)
                planes[2 * pair].append(even.reshape(coarse_z * 8, 128))
                planes[2 * pair + 1].append(odd.reshape(coarse_z * 8, 128))

        def choice(y, z, source):
            line = (y + 1) // 2 + 1
            inside = ((line > 1) | (place_ref[1] > 0)) & ((line < coarse_z) | (place_ref[1] < place_ref[4]))
            return jnp.where((source == z * 8 + line) & inside, 1.0, 0.0).astype(jnp.bfloat16)

        shape = (full_y * size_z, coarse_z * 8)
        row = lax.broadcasted_iota(jnp.int32, shape, 0)
        spread = choice(row // size_z, row % size_z // 2 + 1, lax.broadcasted_iota(jnp.int32, shape, 1))
        shape = (16, coarse_z * 8)
        row = lax.broadcasted_iota(jnp.int32, shape, 0)
        other = jnp.where(first, coarse_z - 1, 0)
        spread_edge = choice(row, other, lax.broadcasted_iota(jnp.int32, shape, 1))
        for plane in range(2 * pairs):
            coarse = jnp.concatenate(planes[plane], axis=1).astype(jnp.bfloat16)
            fine = jnp.dot(spread, coarse, preferred_element_type=jnp.float32)
            fine_edge = jnp.dot(spread_edge, coarse, preferred_element_type=jnp.float32)
            for x in range(full_x):
                if (x + 1) // 2 != plane:
                    continue
                for dy in range(3):
                    main_ref[dy, x] = fine[8 * dy : 8 * dy + size_y * size_z].astype(jnp.bfloat16)
                    side_ref[dy, x] = fine_edge[dy : dy + size_y]
        for dx in range(3):
            blocks = []
            for dy in range(3):
                main = main_ref[dy, dx : dx + size_x].reshape(rows, channels)
                side = side_ref[dy, dx : dx + size_x].reshape(extra, channels).astype(jnp.bfloat16)
                blocks.append(jnp.concatenate([main, side], axis=0))
                if dx:
                    copies[3 * dx + dy - 3].wait()
            block = jnp.concatenate(blocks, axis=1)
            for tap in range(3):
                if dx == 0:
                    kernel = jnp.concatenate([ref[tap] for ref in near_refs], axis=0)
                    sums_ref[tap] = skip_ref[tap] + jnp.dot(block, kernel, preferred_element_type=jnp.float32)
                else:
                    kernel = weights_ref[3 * dx - 3 : 3 * dx, tap].reshape(3 * channels, filters)
                    sums_ref[tap] += jnp.dot(block, kernel, preferred_element_type=jnp.float32)
        total = join_taps(first, [sums_ref[tap] for tap in range(3)], extra, size_z)
        out_ref[...] = total.reshape(size_x, size_y, size_z, filters).astype(out_ref.dtype)

    return pl.pallas_call(
        body,
        in_specs=[pl.BlockSpec(memory_space=pltpu.SMEM)]
        + [pl.BlockSpec(memory_space=pltpu.VMEM)] * 5
        + [pl.BlockSpec(memory_space=pltpu.HBM)],
        out_specs=pl.BlockSpec(memory_space=pltpu.VMEM),
        out_shape=jax.ShapeDtypeStruct((size_x, size_y, size_z, filters), jnp.bfloat16),
        scratch_shapes=[
            pltpu.VMEM((3, full_x, size_y * size_z, channels), jnp.bfloat16),
            pltpu.VMEM((3, full_x, size_y, channels), jnp.float32),
            pltpu.VMEM((3, rows + extra, filters), jnp.float32),
            pltpu.VMEM((6, 3, channels, filters), jnp.bfloat16),
            pltpu.SemaphoreType.DMA((6,)),
        ],
        compiler_params=pltpu.CompilerParams(vmem_limit_bytes=20 << 20),
        name="decode",
    )(place, bottom, near(skip_sums), *map(near, first_weights), far(weights))


def solution(mesh):
    gx, gy, gz = mesh.shape["gx"], mesh.shape["gy"], mesh.shape["gz"]

    def local(volume, w_full, w_half, w_bottom_in, w_bottom_out, w_up):
        place_z = lax.axis_index("gz")
        place = jnp.stack([lax.axis_index("gx"), lax.axis_index("gy"), place_z, jnp.int32(gx - 1), jnp.int32(gy - 1)])
        swap = [(0, 1), (1, 0)]

        def edge_of(plane_low, plane_high):
            return lax.ppermute(jnp.where(place_z == 0, plane_high, plane_low), "gz", swap)

        x_in, x_out = swaps(volume[:3], volume[-3:], "gx", gx)
        turned = [w.transpose(0, 1, 2, 4, 3) for w in (w_bottom_in, w_bottom_out)]
        (w_pair, w_in, w_out), x_in, x_out = lax.optimization_barrier((prepare(w_full, *turned), x_in, x_out))
        y_inner, y_outer, plane = pack_y(place, volume, x_in, x_out)
        y_in, y_out = send(y_inner, y_outer, "gy", gy)
        edge = lax.ppermute(pack_z(place, plane, y_in, y_out), "gz", swap)
        field, w_pair = assemble(place, volume, x_in, x_out, y_in, y_out, w_pair)
        pooled = encode(place, field, edge, w_pair)

        edge = edge_of(pooled[:, :, 0], pooled[:, :, -1])
        skip, coarse = half_level(place, pooled, edge, w_half.reshape(9, 3, w_half.shape[3], w_half.shape[4]))
        lines = coarse.reshape(coarse.shape[0], 4, 4, coarse.shape[2])
        below, above = halo(lines, "gy", gy, 2, 1)
        column = jnp.concatenate([coarse, below[:, :, 0], above[:, :, 0]], axis=1)
        column = jnp.broadcast_to(column[None], (gx * gz,) + column.shape)
        w_in = bring(w_in, column)
        column = lax.all_to_all(column, ("gx", "gz"), 0, 0)
        first = bottom_in(place, column, w_in)
        first = lax.all_to_all(first, "gx", 0, 0)
        w_out = bring(w_out, first)
        y_in, y_out = swaps(first[:, :, :, :2], first[:, :, :, -2:], "gy", gy)
        around = extend(skip, "gx", gx, 0, 1)
        around = extend(around, "gy", gy, 1, 1)
        side = edge_of(around[:, :, 0], around[:, :, -1])
        y_in, y_out, around, side = lax.optimization_barrier((y_in, y_out, around, side))
        second = bottom_out(place, first, y_in, y_out, w_out)
        second = lax.all_to_all(second, "gx", 0, 0)
        w_up = w_up.reshape(9, 3, w_up.shape[3], w_up.shape[4])
        skip_sums, *w_near = decode_skip(place, around, side, w_up)
        return decode(place, second, skip_sums, w_near, w_up, skip.shape[:3])

    space = P("gx", "gy", "gz", None)
    filters = P(None, None, None, None, "gx")
    return jax.shard_map(
        local,
        mesh=mesh,
        in_specs=(space, P(), P(), filters, filters, P()),
        out_specs=space,
        check_vma=False,
    )
```

```python
import jax
import jax.numpy as jnp
from jax import lax
from jax.experimental import pallas as pl
from jax.experimental.pallas import tpu as pltpu
from jax.sharding import PartitionSpec as P


def send(inner_block, outer_block, axis, count):
    inner = [(i, i ^ 1) for i in range(count)]
    outer = [(i, (((i + 1) ^ 1) - 1) % count) for i in range(count)]
    if isinstance(axis, tuple):
        inner, outer = [[(2 * i + n, 2 * j + 1 - n) for i, j in pairs for n in range(2)] for pairs in (inner, outer)]
    return lax.ppermute(inner_block, axis, inner), lax.ppermute(outer_block, axis, outer)


def swaps(low, high, axis, count):
    even = lax.axis_index(axis) % 2 == 0
    return send(jnp.where(even, high, low), jnp.where(even, low, high), axis, count)


def ordered(got_in, got_out, axis):
    even = lax.axis_index(axis) % 2 == 0
    return jnp.where(even, got_out, got_in), jnp.where(even, got_in, got_out)


def halo(field, axis, count, dim, width):
    place = lax.axis_index(axis)
    size = field.shape[dim]
    low = lax.slice_in_dim(field, 0, width, axis=dim)
    high = lax.slice_in_dim(field, size - width, size, axis=dim)
    below, above = ordered(*swaps(low, high, axis, count), axis)
    zero = jnp.zeros_like(low)
    return jnp.where(place > 0, below, zero), jnp.where(place < count - 1, above, zero)


def extend(field, axis, count, dim, width):
    below, above = halo(field, axis, count, dim, width)
    return jnp.concatenate([below, field, above], axis=dim)


def half_level(place, field, edge, weights):
    full_x, full_y, size_z, channels = field.shape
    size_x, size_y = full_x - 2, full_y - 2
    filters = weights.shape[-1]
    rows, extra = size_x * size_y * size_z, size_x * size_y

    def body(place_ref, field_ref, edge_ref, weights_ref, out_ref, coarse_ref, rows_ref, coarse_rows_ref):
        first = place_ref[2] == 0
        edge_plane = edge_ref[...].astype(jnp.float32)
        blocks = []
        for dx in range(3):
            for dy in range(3):
                main = field_ref[dx : dx + size_x, dy : dy + size_y].astype(jnp.float32).reshape(rows, channels)
                side = edge_plane[dx : dx + size_x, dy : dy + size_y].reshape(extra, channels)
                blocks.append(jnp.concatenate([main, side], axis=0).astype(jnp.bfloat16))
        block = jnp.concatenate(blocks, axis=1)
        sums = []
        for tap in range(3):
            kernel = weights_ref[:, tap].reshape(9 * channels, filters)
            sums.append(jnp.dot(block, kernel, preferred_element_type=jnp.float32))
        total = jnp.maximum(join_taps(first, sums, extra, size_z), 0.0)
        out_ref[...] = total.reshape(size_x, size_y, size_z, filters).astype(out_ref.dtype)
        total = jnp.max(total.reshape(size_x // 2, 2, size_y // 2, 2, size_z, filters), axis=(1, 3))
        count = size_y // 2
        for part in range(filters // 128):
            rows_ref[...] = total[..., 128 * part : 128 * part + 128].reshape(rows // 4, 128)
            for x in range(size_x // 2):
                for z in range(size_z // 2):
                    start = x * count * size_z + 2 * z
                    pooled = jnp.maximum(
                        rows_ref[pl.ds(start, count, stride=size_z), :], rows_ref[pl.ds(start + 1, count, stride=size_z), :]
                    )
                    coarse_rows_ref[x, count * z : count * z + count, 128 * part : 128 * part + 128] = pooled
        coarse_ref[...] = coarse_rows_ref[...].astype(coarse_ref.dtype)

    return pl.pallas_call(
        body,
        in_specs=[pl.BlockSpec(memory_space=pltpu.SMEM)] + [pl.BlockSpec(memory_space=pltpu.VMEM)] * 3,
        out_specs=[pl.BlockSpec(memory_space=pltpu.VMEM)] * 2,
        out_shape=[
            jax.ShapeDtypeStruct((size_x, size_y, size_z, filters), jnp.bfloat16),
            jax.ShapeDtypeStruct((size_x // 2, size_z * size_y // 4, filters), jnp.bfloat16),
        ],
        scratch_shapes=[
            pltpu.VMEM((rows // 4, 128), jnp.float32),
            pltpu.VMEM((size_x // 2, size_z * size_y // 4, filters), jnp.float32),
        ],
        compiler_params=pltpu.CompilerParams(vmem_limit_bytes=12 << 20),
        name="half_level",
    )(place, field, edge, weights)


def join_taps(first, sums, groups, size_z):
    rows, filters = groups * size_z, sums[0].shape[-1]
    low, mid, high = [total[:rows].reshape(groups, size_z, filters) for total in sums]
    below = jnp.where(first, 0.0, sums[0][rows : rows + groups])
    above = jnp.where(first, sums[2][rows : rows + groups], 0.0)
    index = lax.broadcasted_iota(jnp.int32, (groups, size_z, filters), 1)
    down = jnp.where(index == 0, below[:, None, :], pltpu.roll(low, 1, 1))
    up = jnp.where(index == size_z - 1, above[:, None, :], pltpu.roll(high, size_z - 1, 1))
    return down + mid + up


def encode(place, own, x_in, x_out, y_in, y_out, edge, edge_in, edge_out, weights):
    own_x, own_y, size_z, channels = own.shape
    reach = x_in.shape[0]
    full_x, full_y = own_x + 2 * reach, own_y + 2 * reach
    size_x, size_y = full_x - 2, full_y - 2
    filters = weights.shape[-1] // 2
    rows, extra = size_y * size_z, size_y + (-size_y % 16)
    pool_y, pool_z = size_y // 2, size_z // 2

    def body(
        place_ref,
        own_ref,
        x_in_ref,
        x_out_ref,
        y_in_ref,
        y_out_ref,
        edge_ref,
        edge_in_ref,
        edge_out_ref,
        weights_ref,
        out_ref,
        x_ref,
        y_ref,
        side_ref,
        rows_ref,
    ):
        even_x, even_y = place_ref[0] % 2 == 0, place_ref[1] % 2 == 0
        low_x, high_x = place_ref[0] > 0, place_ref[0] < place_ref[3]
        low_y, high_y = place_ref[1] > 0, place_ref[1] < place_ref[4]
        nil = jnp.bfloat16(0)
        x_ref[0] = jnp.where(low_x, jnp.where(even_x, x_out_ref[...], x_in_ref[...]), nil)
        x_ref[1] = jnp.where(high_x, jnp.where(even_x, x_in_ref[...], x_out_ref[...]), nil)
        for x in range(full_x):
            here_low, here_high, here = low_y, high_y, None
            if x < reach:
                here_low, here_high, here = low_y & low_x, high_y & low_x, low_x
            if x >= reach + own_x:
                here_low, here_high, here = low_y & high_x, high_y & high_x, high_x
            y_ref[0, x] = jnp.where(here_low, jnp.where(even_y, y_out_ref[x], y_in_ref[x]), nil)
            y_ref[1, x] = jnp.where(here_high, jnp.where(even_y, y_in_ref[x], y_out_ref[x]), nil)
            middle = edge_ref[x].astype(jnp.float32)
            if here is not None:
                middle = jnp.where(here, middle, 0.0)
            one, other = edge_in_ref[x].astype(jnp.float32), edge_out_ref[x].astype(jnp.float32)
            below = jnp.where(here_low, jnp.where(even_y, other, one), 0.0)
            above = jnp.where(here_high, jnp.where(even_y, one, other), 0.0)
            for dy in range(3):
                if dy < reach:
                    side_ref[dy, x, : reach - dy] = below[dy:]
                side_ref[dy, x, reach - dy : reach - dy + own_y] = middle
                side_ref[dy, x, reach - dy + own_y : size_y] = above[: dy + 1]
                side_ref[dy, x, size_y:] = jnp.zeros((extra - size_y, channels), jnp.float32)

        def lines(x, dy):
            if x < reach:
                middle = x_ref[0, x]
            elif x < reach + own_x:
                middle = own_ref[x - reach]
            else:
                middle = x_ref[1, x - reach - own_x]
            block = jnp.concatenate([y_ref[0, x, dy:], middle, y_ref[1, x, : dy + 1]], axis=0)
            return block.reshape(rows, channels)

        first = place_ref[2] == 0
        line = lax.broadcasted_iota(jnp.int32, (pool_y, pool_z, filters), 0)
        inside_y = ((line > 0) | low_y) & ((line < pool_y - 1) | high_y)
        for pair in range(size_x // 2):
            blocks = []
            for plane in range(4):
                for dy in range(3):
                    main = lines(2 * pair + plane, dy)
                    side = side_ref[dy, 2 * pair + plane].astype(jnp.bfloat16)
                    blocks.append(jnp.concatenate([main, side], axis=0))
            block = jnp.concatenate(blocks, axis=1)
            sums = []
            for tap in range(3):
                kernel = weights_ref[:, :, tap].reshape(12 * channels, 2 * filters)
                sums.append(jnp.dot(block, kernel, preferred_element_type=jnp.float32))
            total = jnp.maximum(join_taps(first, sums, size_y, size_z), 0.0)
            total = jnp.maximum(total[..., :filters], total[..., filters:])
            total = jnp.max(total.reshape(pool_y, 2, size_z, filters), axis=1)
            rows_ref[...] = total.reshape(pool_y * size_z, filters)
            total = jnp.maximum(
                rows_ref[pl.ds(0, pool_y * pool_z, stride=2), :], rows_ref[pl.ds(1, pool_y * pool_z, stride=2), :]
            ).reshape(pool_y, pool_z, filters)
            inside = inside_y
            if pair == 0:
                inside = inside & low_x
            if pair == size_x // 2 - 1:
                inside = inside & high_x
            out_ref[pair] = jnp.where(inside, total, 0.0).astype(out_ref.dtype)

    return pl.pallas_call(
        body,
        in_specs=[pl.BlockSpec(memory_space=pltpu.SMEM)] + [pl.BlockSpec(memory_space=pltpu.VMEM)] * 9,
        out_specs=pl.BlockSpec(memory_space=pltpu.VMEM),
        out_shape=jax.ShapeDtypeStruct((size_x // 2, pool_y, pool_z, filters), jnp.bfloat16),
        scratch_shapes=[
            pltpu.VMEM((2, reach, own_y, size_z, channels), jnp.bfloat16),
            pltpu.VMEM((2, full_x, reach, size_z, channels), jnp.bfloat16),
            pltpu.VMEM((3, full_x, extra, channels), jnp.float32),
            pltpu.VMEM((pool_y * size_z, filters), jnp.float32),
        ],
        compiler_params=pltpu.CompilerParams(vmem_limit_bytes=14 << 20),
        name="encode",
    )(place, near(own), x_in, x_out, y_in, y_out, edge, edge_in, edge_out, near(weights))


def near(array):
    return pltpu.with_memory_space_constraint(array, pltpu.VMEM)


def bring(arrays, after):
    pieces = [(i, n) for i, array in enumerate(arrays) for n in range(array.shape[0])]
    count = len(arrays)

    def body(*refs):
        hbms, outs, sems = refs[:count], refs[count + 1 : -1], refs[-1]
        copies = [pltpu.make_async_copy(hbms[i].at[n], outs[i].at[n], sems.at[k]) for k, (i, n) in enumerate(pieces)]
        for copy in copies:
            copy.start()
        for copy in copies:
            copy.wait()

    return pl.pallas_call(
        body,
        in_specs=[pl.BlockSpec(memory_space=pltpu.HBM)] * count + [pl.BlockSpec(memory_space=pl.ANY)],
        out_specs=[pl.BlockSpec(memory_space=pltpu.VMEM)] * count,
        out_shape=[pltpu.VMEM(array.shape, array.dtype) for array in arrays],
        scratch_shapes=[pltpu.SemaphoreType.DMA((len(pieces),))],
        compiler_params=pltpu.CompilerParams(vmem_limit_bytes=4 << 20),
        name="bring",
    )(*map(far, arrays), after)


def far(array):
    return pltpu.with_memory_space_constraint(array, pltpu.HBM)


def prepare(w_full, w_in, w_out):
    channels, filters = w_full.shape[3:]
    depths = [w.shape[4] for w in (w_in, w_out)]

    def body(
        full_hbm, in_hbm, out_hbm, pair_hbm, to_in_hbm, to_out_hbm, full_ref, pair_ref, in_ref, out_ref, to_in_ref, to_out_ref, sems
    ):
        first = pltpu.make_async_copy(full_hbm, full_ref, sems.at[0])
        first.start()
        jobs = []
        for order, (hbm, ref) in enumerate(((in_hbm, in_ref), (out_hbm, out_ref))):
            copies = []
            for step in range(9):
                for dy in range(3):
                    to = ref.at[step, pl.ds(64 * dy, 64)]
                    sem = sems.at[1 + 27 * order + 3 * step + dy]
                    copies.append(pltpu.make_async_copy(hbm.at[step // 3, dy, step % 3], to, sem))
                    copies[-1].start()
            jobs.append(copies)
        first.wait()
        zero = jnp.zeros((3, 3, channels, filters), jnp.bfloat16)
        results = []
        for plane in range(4):
            pair_ref[plane, :, :, :, :filters] = full_ref[plane] if plane < 3 else zero
            pair_ref[plane, :, :, :, filters:] = full_ref[plane - 1] if plane > 0 else zero
            results.append(pltpu.make_async_copy(pair_ref.at[plane], pair_hbm.at[plane], sems.at[55 + plane]))
            results[-1].start()
        for order, (ref, to_ref, to_hbm) in enumerate(((in_ref, to_in_ref, to_in_hbm), (out_ref, to_out_ref, to_out_hbm))):
            for step in range(9):
                ref[step, 192:] = jnp.zeros((64, depths[order]), jnp.bfloat16)
                for copy in jobs[order][3 * step : 3 * step + 3]:
                    copy.wait()
                to_ref[step] = ref[step].T
                results.append(pltpu.make_async_copy(to_ref.at[step], to_hbm.at[step], sems.at[59 + 9 * order + step]))
                results[-1].start()
        for copy in results:
            copy.wait()

    shapes = [(4, 3, 3, channels, 2 * filters)] + [(9, depth, 256) for depth in depths]
    return pl.pallas_call(
        body,
        in_specs=[pl.BlockSpec(memory_space=pltpu.HBM)] * 3,
        out_specs=[pl.BlockSpec(memory_space=pltpu.HBM)] * 3,
        out_shape=[pltpu.HBM(shape, jnp.bfloat16) for shape in shapes],
        scratch_shapes=[pltpu.VMEM(w_full.shape, jnp.bfloat16), pltpu.VMEM(shapes[0], jnp.bfloat16)]
        + [pltpu.VMEM((9, 256, depth), jnp.bfloat16) for depth in depths]
        + [pltpu.VMEM((9, depth, 256), jnp.bfloat16) for depth in depths]
        + [pltpu.SemaphoreType.DMA((77,))],
        compiler_params=pltpu.CompilerParams(vmem_limit_bytes=20 << 20),
        name="prepare",
    )(far(w_full), far(w_in), far(w_out))


def pack_y(place, own, x_in, x_out):
    own_x, own_y, size_z, channels = own.shape
    reach = x_in.shape[0]
    full_x = own_x + 2 * reach

    def body(place_ref, own_ref, x_in_ref, x_out_ref, inner_ref, outer_ref, plane_ref, inner_edge_ref, outer_edge_ref, rows_ref):
        even_x, even_y, first = place_ref[0] % 2 == 0, place_ref[1] % 2 == 0, place_ref[2] == 0
        below = jnp.where(even_x, x_out_ref[...], x_in_ref[...])
        above = jnp.where(even_x, x_in_ref[...], x_out_ref[...])
        for start, block in ((0, below), (reach, own_ref[...]), (reach + own_x, above)):
            size = block.shape[0]
            low, high = block[:, :reach], block[:, own_y - reach :]
            inner_ref[start : start + size] = jnp.where(even_y, high, low)
            outer_ref[start : start + size] = jnp.where(even_y, low, high)
            block = block.astype(jnp.float32)
            edge = jnp.where(first, block[:, :, size_z - 1 :], block[:, :, :1])
            for x in range(size):
                for y in range(own_y):
                    rows_ref[start + x, y : y + 1] = edge[x, y]
        plane_ref[...] = rows_ref[...].astype(plane_ref.dtype)
        low, high = rows_ref[:, :reach], rows_ref[:, own_y - reach :]
        inner_edge_ref[...] = jnp.where(even_y, high, low).astype(plane_ref.dtype)
        outer_edge_ref[...] = jnp.where(even_y, low, high).astype(plane_ref.dtype)

    return pl.pallas_call(
        body,
        in_specs=[pl.BlockSpec(memory_space=pltpu.SMEM)] + [pl.BlockSpec(memory_space=pltpu.VMEM)] * 3,
        out_specs=[pl.BlockSpec(memory_space=pltpu.VMEM)] * 5,
        out_shape=[jax.ShapeDtypeStruct((full_x, reach, size_z, channels), jnp.bfloat16)] * 2
        + [jax.ShapeDtypeStruct((full_x, rows, channels), jnp.bfloat16) for rows in (own_y, reach, reach)],
        scratch_shapes=[pltpu.VMEM((full_x, own_y, channels), jnp.float32)],
        compiler_params=pltpu.CompilerParams(vmem_limit_bytes=8 << 20),
        name="pack_y",
    )(place, own, x_in, x_out)


def halves(pair_low, pair_high):
    lane = lax.broadcasted_iota(jnp.int32, pair_low.shape, pair_low.ndim - 1)
    axis = pair_low.ndim - 1
    even = jnp.where(lane < 64, pair_low, pltpu.roll(pair_high, 64, axis))
    odd = jnp.where(lane < 64, pltpu.roll(pair_low, 64, axis), pair_high)
    return even, odd


def side_by_side(even, odd):
    lane = lax.broadcasted_iota(jnp.int32, even.shape, even.ndim - 1)
    return jnp.where(lane < 64, even, pltpu.roll(odd, 64, even.ndim - 1))


def column_product(pad_ref, weights_ref, first, start, planes, size_z):
    channels = pad_ref.shape[-1]
    rows = planes * size_z * 8
    blocks = []
    for dx in range(3):
        for dz in range(3):
            block = pad_ref[first + dx : first + dx + planes, pl.ds(start + dz, size_z)]
            blocks.append(block.reshape(rows, channels).astype(jnp.bfloat16))
    block = jnp.concatenate(blocks, axis=1)
    total = jnp.dot(block, weights_ref[...].reshape(9 * channels, 256), preferred_element_type=jnp.float32)
    low = total[:, :128].reshape(planes * size_z, 8, 128)
    mid = pltpu.roll(total[:, :128], 64, 1).reshape(planes * size_z, 8, 128)
    high = total[:, 128:].reshape(planes * size_z, 8, 128)
    total = pltpu.roll(low, 1, 1) + mid + pltpu.roll(high, 7, 1)
    return jnp.maximum(total, 0.0).reshape(planes, size_z, 8, 128)


def bottom_in(place, field, weights):
    count, own_x, lines, channels = field.shape
    devices = count // 2
    own_z = size_y = 4
    size_x, all_z, size_z = devices * own_x, 2 * own_z, own_z + 2

    def body(place_ref, field_ref, weights_ref, out_ref, pad_ref):
        zero = jnp.zeros((all_z + 2, 8, channels), jnp.float32)
        pad_ref[0] = zero
        pad_ref[size_x + 1] = zero
        for x in range(size_x):
            pad_ref[x + 1, 0] = zero[0]
            pad_ref[x + 1, all_z + 1] = zero[0]
        for i in range(devices):
            for half in range(2):
                for x in range(own_x):
                    block = field_ref[2 * i + half, x].astype(jnp.float32)
                    for z in range(own_z):
                        to = (1 + own_x * i + x, 1 + own_z * half + z)
                        pad_ref[*to, 0:1] = block[own_z * size_y + z : own_z * size_y + z + 1]
                        pad_ref[*to, 1 : size_y + 1] = block[size_y * z : size_y * z + size_y]
                        line = own_z * (size_y + 1) + z
                        pad_ref[*to, size_y + 1 : size_y + 2] = block[line : line + 1]
                        pad_ref[*to, size_y + 2 :] = zero[0, size_y + 2 :]
        start = 2 * place_ref[2]
        for first in range(0, size_x, 4):
            total = column_product(pad_ref, weights_ref, first, start, 4, size_z)
            for pair in range(2):
                both = side_by_side(total[2 * pair], total[2 * pair + 1])[:, 1 : size_y + 1].astype(out_ref.dtype)
                for i in range(devices):
                    out_ref[i, first // 2 + pair] = both

    return pl.pallas_call(
        body,
        in_specs=[pl.BlockSpec(memory_space=space) for space in (pltpu.SMEM, pltpu.VMEM, pltpu.VMEM)],
        out_specs=pl.BlockSpec(memory_space=pltpu.VMEM),
        out_shape=jax.ShapeDtypeStruct((devices, size_x // 2, size_z, size_y, 128), jnp.bfloat16),
        scratch_shapes=[
            pltpu.VMEM((size_x + 2, all_z + 2, 8, channels), jnp.float32),
        ],
        compiler_params=pltpu.CompilerParams(vmem_limit_bytes=12 << 20),
        name="bottom_in",
    )(place, field, near(weights))


def bottom_out(place, field, y_in, y_out, weights):
    devices, pairs, size_z, _, _ = field.shape
    size_x, channels = 2 * pairs, 64 * devices
    own_x = size_x // devices

    def body(place_ref, field_ref, y_in_ref, y_out_ref, weights_ref, out_ref, pad_ref, total_ref):
        even_y = place_ref[1] % 2 == 0
        low_y, high_y = place_ref[1] > 0, place_ref[1] < place_ref[4]
        zero = jnp.zeros((size_z + 2, 8, channels), jnp.float32)
        for ref in (pad_ref, total_ref):
            wide = ref.shape[-1]
            ref[0] = zero[..., :wide]
            ref[size_x + 1] = zero[..., :wide]
            for x in range(size_x):
                ref[x + 1, 0] = zero[0, :, :wide]
                ref[x + 1, size_z + 1] = zero[0, :, :wide]
        for k in range(devices // 2):
            for pair in range(pairs):
                y_first, y_last = [], []
                for i in range(2):
                    one = y_in_ref[2 * k + i, pair].astype(jnp.float32)
                    other = y_out_ref[2 * k + i, pair].astype(jnp.float32)
                    y_first.append(jnp.where(low_y, jnp.where(even_y, other, one), 0.0))
                    y_last.append(jnp.where(high_y, jnp.where(even_y, one, other), 0.0))
                own = [field_ref[2 * k + i, pair].astype(jnp.float32) for i in range(2)]
                for line, blocks in ((0, y_first), (2, own), (6, y_last)):
                    even, odd = halves(*blocks)
                    lines = slice(line, line + even.shape[1])
                    pad_ref[1 + 2 * pair, 1 : size_z + 1, lines, 128 * k : 128 * k + 128] = even
                    pad_ref[2 + 2 * pair, 1 : size_z + 1, lines, 128 * k : 128 * k + 128] = odd
        for first in range(0, size_x, 4):
            total = column_product(pad_ref, weights_ref, first, 0, 4, size_z)
            total_ref[1 + first : 5 + first, 1 : size_z + 1] = total
        start = 2 * place_ref[2]
        for i in range(size_x // 2 + 1):
            low, high = [total_ref[2 * i + n, pl.ds(start, size_z)] for n in range(2)]
            both = side_by_side(low, high).astype(out_ref.dtype)
            if i < devices:
                out_ref[i, 0] = both
            if i > 0:
                out_ref[i - 1, 1] = both

    return pl.pallas_call(
        body,
        in_specs=[pl.BlockSpec(memory_space=pltpu.SMEM)]
        + [pl.BlockSpec(memory_space=pltpu.VMEM)] * 4,
        out_specs=pl.BlockSpec(memory_space=pltpu.VMEM),
        out_shape=jax.ShapeDtypeStruct((devices, own_x, size_z, 8, 128), jnp.bfloat16),
        scratch_shapes=[
            pltpu.VMEM((size_x + 2, size_z + 2, 8, channels), jnp.float32),
            pltpu.VMEM((size_x + 2, size_z + 2, 8, 128), jnp.float32),
        ],
        compiler_params=pltpu.CompilerParams(vmem_limit_bytes=16 << 20),
        name="bottom_out",
    )(place, field, y_in, y_out, near(weights))


def decode_skip(place, skip, edge, weights):
    full_x, full_y, size_z, channels = skip.shape
    size_x, size_y = full_x - 2, full_y - 2
    filters = weights.shape[-1]
    deep = weights.shape[2] - channels
    rows, extra = size_x * size_y * size_z, size_x * size_y

    def body(skip_ref, edge_ref, weights_hbm, out_ref, *refs):
        rest_refs, (weights_ref, sems) = refs[:3], refs[3:]
        copies = [
            pltpu.make_async_copy(weights_hbm.at[step, :, pl.ds(deep, channels)], weights_ref.at[step], sems.at[step])
            for step in range(9)
        ]
        rest = [
            pltpu.make_async_copy(weights_hbm.at[step, :, pl.ds(0, deep)], rest_refs[step], sems.at[9 + step])
            for step in range(3)
        ]
        for copy in copies + rest:
            copy.start()
        edge_plane = edge_ref[...].astype(jnp.float32)
        blocks = []
        for dx in range(3):
            for dy in range(3):
                main = skip_ref[dx : dx + size_x, dy : dy + size_y].astype(jnp.float32).reshape(rows, channels)
                side = edge_plane[dx : dx + size_x, dy : dy + size_y].reshape(extra, channels)
                blocks.append(jnp.concatenate([main, side], axis=0).astype(jnp.bfloat16))
        for copy in copies:
            copy.wait()
        block = jnp.concatenate(blocks, axis=1)
        for tap in range(3):
            kernel = weights_ref[:, tap].reshape(9 * channels, filters)
            out_ref[tap] = jnp.dot(block, kernel, preferred_element_type=jnp.float32)
        for copy in rest:
            copy.wait()

    return pl.pallas_call(
        body,
        in_specs=[pl.BlockSpec(memory_space=pltpu.VMEM)] * 2 + [pl.BlockSpec(memory_space=pltpu.HBM)],
        out_specs=[pl.BlockSpec(memory_space=pltpu.VMEM)] * 4,
        out_shape=[
            pltpu.VMEM((3, rows + extra, filters), jnp.float32),
        ]
        + [pltpu.VMEM((3, deep, filters), jnp.bfloat16)] * 3,
        scratch_shapes=[pltpu.VMEM((9, 3, channels, filters), jnp.bfloat16), pltpu.SemaphoreType.DMA((12,))],
        compiler_params=pltpu.CompilerParams(vmem_limit_bytes=14 << 20),
        name="decode_skip",
    )(skip, edge, far(weights))


def decode(place, bottom, skip_sums, first_weights, weights, shape):
    devices, pairs, coarse_z, _, _ = bottom.shape
    size_x, size_y, size_z = shape
    full_x, full_y = size_x + 2, size_y + 2
    channels = 64 * devices
    filters = weights.shape[-1]
    rows, extra = size_x * size_y * size_z, size_x * size_y

    def body(place_ref, bottom_ref, skip_ref, *refs):
        near_refs, (weights_hbm, out_ref, main_ref, side_ref, sums_ref, weights_ref, sems) = refs[:3], refs[3:]
        copies = [
            pltpu.make_async_copy(weights_hbm.at[3 + step, :, pl.ds(0, channels)], weights_ref.at[step], sems.at[step])
            for step in range(6)
        ]
        for copy in copies:
            copy.start()
        first = place_ref[2] == 0
        planes = [[] for _ in range(2 * pairs)]
        for k in range(devices // 2):
            for pair in range(pairs):
                low, high = [bottom_ref[2 * k + i, pair].astype(jnp.float32) for i in range(2)]
                even, odd = halves(low, high)
                planes[2 * pair].append(even.reshape(coarse_z * 8, 128))
                planes[2 * pair + 1].append(odd.reshape(coarse_z * 8, 128))

        def choice(y, z, source):
            line = (y + 1) // 2 + 1
            inside = ((line > 1) | (place_ref[1] > 0)) & ((line < coarse_z) | (place_ref[1] < place_ref[4]))
            return jnp.where((source == z * 8 + line) & inside, 1.0, 0.0).astype(jnp.bfloat16)

        shape = (full_y * size_z, coarse_z * 8)
        row = lax.broadcasted_iota(jnp.int32, shape, 0)
        spread = choice(row // size_z, row % size_z // 2 + 1, lax.broadcasted_iota(jnp.int32, shape, 1))
        shape = (16, coarse_z * 8)
        row = lax.broadcasted_iota(jnp.int32, shape, 0)
        other = jnp.where(first, coarse_z - 1, 0)
        spread_edge = choice(row, other, lax.broadcasted_iota(jnp.int32, shape, 1))
        for plane in range(2 * pairs):
            coarse = jnp.concatenate(planes[plane], axis=1).astype(jnp.bfloat16)
            fine = jnp.dot(spread, coarse, preferred_element_type=jnp.float32)
            fine_edge = jnp.dot(spread_edge, coarse, preferred_element_type=jnp.float32)
            for x in range(full_x):
                if (x + 1) // 2 != plane:
                    continue
                for dy in range(3):
                    main_ref[dy, x] = fine[8 * dy : 8 * dy + size_y * size_z].astype(jnp.bfloat16)
                    side_ref[dy, x] = fine_edge[dy : dy + size_y]
        for dx in range(3):
            blocks = []
            for dy in range(3):
                main = main_ref[dy, dx : dx + size_x].reshape(rows, channels)
                side = side_ref[dy, dx : dx + size_x].reshape(extra, channels).astype(jnp.bfloat16)
                blocks.append(jnp.concatenate([main, side], axis=0))
                if dx:
                    copies[3 * dx + dy - 3].wait()
            block = jnp.concatenate(blocks, axis=1)
            for tap in range(3):
                if dx == 0:
                    kernel = jnp.concatenate([ref[tap] for ref in near_refs], axis=0)
                    sums_ref[tap] = skip_ref[tap] + jnp.dot(block, kernel, preferred_element_type=jnp.float32)
                else:
                    kernel = weights_ref[3 * dx - 3 : 3 * dx, tap].reshape(3 * channels, filters)
                    sums_ref[tap] += jnp.dot(block, kernel, preferred_element_type=jnp.float32)
        total = join_taps(first, [sums_ref[tap] for tap in range(3)], extra, size_z)
        out_ref[...] = total.reshape(size_x, size_y, size_z, filters).astype(out_ref.dtype)

    return pl.pallas_call(
        body,
        in_specs=[pl.BlockSpec(memory_space=pltpu.SMEM)]
        + [pl.BlockSpec(memory_space=pltpu.VMEM)] * 5
        + [pl.BlockSpec(memory_space=pltpu.HBM)],
        out_specs=pl.BlockSpec(memory_space=pltpu.VMEM),
        out_shape=jax.ShapeDtypeStruct((size_x, size_y, size_z, filters), jnp.bfloat16),
        scratch_shapes=[
            pltpu.VMEM((3, full_x, size_y * size_z, channels), jnp.bfloat16),
            pltpu.VMEM((3, full_x, size_y, channels), jnp.float32),
            pltpu.VMEM((3, rows + extra, filters), jnp.float32),
            pltpu.VMEM((6, 3, channels, filters), jnp.bfloat16),
            pltpu.SemaphoreType.DMA((6,)),
        ],
        compiler_params=pltpu.CompilerParams(vmem_limit_bytes=20 << 20),
        name="decode",
    )(place, bottom, near(skip_sums), *map(near, first_weights), far(weights))


def solution(mesh):
    gx, gy, gz = mesh.shape["gx"], mesh.shape["gy"], mesh.shape["gz"]

    def local(volume, w_full, w_half, w_bottom_in, w_bottom_out, w_up):
        place_z = lax.axis_index("gz")
        place = jnp.stack([lax.axis_index("gx"), lax.axis_index("gy"), place_z, jnp.int32(gx - 1), jnp.int32(gy - 1)])
        swap = [(0, 1), (1, 0)]

        def edge_of(plane_low, plane_high):
            return lax.ppermute(jnp.where(place_z == 0, plane_high, plane_low), "gz", swap)

        x_in, x_out = swaps(volume[:3], volume[-3:], "gx", gx)
        turned = [w.transpose(0, 1, 2, 4, 3) for w in (w_bottom_in, w_bottom_out)]
        (w_pair, w_in, w_out), x_in, x_out = lax.optimization_barrier((prepare(w_full, *turned), x_in, x_out))
        y_inner, y_outer, plane, edge_inner, edge_outer = pack_y(place, volume, x_in, x_out)
        y_in, y_out = send(y_inner, y_outer, "gy", gy)
        edge = lax.ppermute(plane, "gz", swap)
        edge_in, edge_out = send(edge_inner, edge_outer, ("gy", "gz"), gy)
        own, w_pair = bring([volume, w_pair], plane)
        pooled = encode(place, own, x_in, x_out, y_in, y_out, edge, edge_in, edge_out, w_pair)

        edge = edge_of(pooled[:, :, 0], pooled[:, :, -1])
        skip, coarse = half_level(place, pooled, edge, w_half.reshape(9, 3, w_half.shape[3], w_half.shape[4]))
        lines = coarse.reshape(coarse.shape[0], 4, 4, coarse.shape[2])
        below, above = halo(lines, "gy", gy, 2, 1)
        column = jnp.concatenate([coarse, below[:, :, 0], above[:, :, 0]], axis=1)
        column = jnp.broadcast_to(column[None], (gx * gz,) + column.shape)
        (w_in,) = bring([w_in], column)
        column = lax.all_to_all(column, ("gx", "gz"), 0, 0)
        first = bottom_in(place, column, w_in)
        first = lax.all_to_all(first, "gx", 0, 0)
        (w_out,) = bring([w_out], first)
        y_in, y_out = swaps(first[:, :, :, :2], first[:, :, :, -2:], "gy", gy)
        around = extend(skip, "gx", gx, 0, 1)
        around = extend(around, "gy", gy, 1, 1)
        side = edge_of(around[:, :, 0], around[:, :, -1])
        y_in, y_out, around, side = lax.optimization_barrier((y_in, y_out, around, side))
        second = bottom_out(place, first, y_in, y_out, w_out)
        second = lax.all_to_all(second, "gx", 0, 0)
        w_up = w_up.reshape(9, 3, w_up.shape[3], w_up.shape[4])
        skip_sums, *w_near = decode_skip(place, around, side, w_up)
        return decode(place, second, skip_sums, w_near, w_up, skip.shape[:3])

    space = P("gx", "gy", "gz", None)
    filters = P(None, None, None, None, "gx")
    return jax.shard_map(
        local,
        mesh=mesh,
        in_specs=(space, P(), P(), filters, filters, P()),
        out_specs=space,
        check_vma=False,
    )
```

```python
import jax
import jax.numpy as jnp
from jax import lax
from jax.experimental import pallas as pl
from jax.experimental.pallas import tpu as pltpu
from jax.sharding import PartitionSpec as P


def send(inner_block, outer_block, axis, count):
    inner = [(i, i ^ 1) for i in range(count)]
    outer = [(i, (((i + 1) ^ 1) - 1) % count) for i in range(count)]
    if isinstance(axis, tuple):
        inner, outer = [[(2 * i + n, 2 * j + 1 - n) for i, j in pairs for n in range(2)] for pairs in (inner, outer)]
    return lax.ppermute(inner_block, axis, inner), lax.ppermute(outer_block, axis, outer)


def swaps(low, high, axis, count):
    even = lax.axis_index(axis) % 2 == 0
    return send(jnp.where(even, high, low), jnp.where(even, low, high), axis, count)


def ordered(got_in, got_out, axis):
    even = lax.axis_index(axis) % 2 == 0
    return jnp.where(even, got_out, got_in), jnp.where(even, got_in, got_out)


def halo(field, axis, count, dim, width):
    place = lax.axis_index(axis)
    size = field.shape[dim]
    low = lax.slice_in_dim(field, 0, width, axis=dim)
    high = lax.slice_in_dim(field, size - width, size, axis=dim)
    below, above = ordered(*swaps(low, high, axis, count), axis)
    zero = jnp.zeros_like(low)
    return jnp.where(place > 0, below, zero), jnp.where(place < count - 1, above, zero)


def extend(field, axis, count, dim, width):
    below, above = halo(field, axis, count, dim, width)
    return jnp.concatenate([below, field, above], axis=dim)


def half_level(place, field, edge, weights):
    full_x, full_y, size_z, channels = field.shape
    size_x, size_y = full_x - 2, full_y - 2
    filters = weights.shape[-1]
    rows, extra = size_x * size_y * size_z, size_x * size_y

    def body(place_ref, field_ref, edge_ref, weights_ref, out_ref, coarse_ref, rows_ref, coarse_rows_ref):
        first = place_ref[2] == 0
        edge_plane = edge_ref[...].astype(jnp.float32)
        blocks = []
        for dx in range(3):
            for dy in range(3):
                main = field_ref[dx : dx + size_x, dy : dy + size_y].astype(jnp.float32).reshape(rows, channels)
                side = edge_plane[dx : dx + size_x, dy : dy + size_y].reshape(extra, channels)
                blocks.append(jnp.concatenate([main, side], axis=0).astype(jnp.bfloat16))
        block = jnp.concatenate(blocks, axis=1)
        sums = []
        for tap in range(3):
            kernel = weights_ref[:, tap].reshape(9 * channels, filters)
            sums.append(jnp.dot(block, kernel, preferred_element_type=jnp.float32))
        total = jnp.maximum(join_taps(first, sums, extra, size_z), 0.0)
        out_ref[...] = total.reshape(size_x, size_y, size_z, filters).astype(out_ref.dtype)
        total = jnp.max(total.reshape(size_x // 2, 2, size_y // 2, 2, size_z, filters), axis=(1, 3))
        count = size_y // 2
        for part in range(filters // 128):
            rows_ref[...] = total[..., 128 * part : 128 * part + 128].reshape(rows // 4, 128)
            for x in range(size_x // 2):
                for z in range(size_z // 2):
                    start = x * count * size_z + 2 * z
                    pooled = jnp.maximum(
                        rows_ref[pl.ds(start, count, stride=size_z), :], rows_ref[pl.ds(start + 1, count, stride=size_z), :]
                    )
                    coarse_rows_ref[x, count * z : count * z + count, 128 * part : 128 * part + 128] = pooled
        coarse_ref[...] = coarse_rows_ref[...].astype(coarse_ref.dtype)

    return pl.pallas_call(
        body,
        in_specs=[pl.BlockSpec(memory_space=pltpu.SMEM)] + [pl.BlockSpec(memory_space=pltpu.VMEM)] * 3,
        out_specs=[pl.BlockSpec(memory_space=pltpu.VMEM)] * 2,
        out_shape=[
            jax.ShapeDtypeStruct((size_x, size_y, size_z, filters), jnp.bfloat16),
            jax.ShapeDtypeStruct((size_x // 2, size_z * size_y // 4, filters), jnp.bfloat16),
        ],
        scratch_shapes=[
            pltpu.VMEM((rows // 4, 128), jnp.float32),
            pltpu.VMEM((size_x // 2, size_z * size_y // 4, filters), jnp.float32),
        ],
        compiler_params=pltpu.CompilerParams(vmem_limit_bytes=12 << 20),
        name="half_level",
    )(place, field, edge, weights)


def join_taps(first, sums, groups, size_z):
    rows, filters = groups * size_z, sums[0].shape[-1]
    low, mid, high = [total[:rows].reshape(groups, size_z, filters) for total in sums]
    below = jnp.where(first, 0.0, sums[0][rows : rows + groups])
    above = jnp.where(first, sums[2][rows : rows + groups], 0.0)
    index = lax.broadcasted_iota(jnp.int32, (groups, size_z, filters), 1)
    down = jnp.where(index == 0, below[:, None, :], pltpu.roll(low, 1, 1))
    up = jnp.where(index == size_z - 1, above[:, None, :], pltpu.roll(high, size_z - 1, 1))
    return down + mid + up


def encode(place, own, x_in, x_out, y_in, y_out, edge, edge_in, edge_out, weights):
    own_x, own_y, size_z, channels = own.shape
    reach = x_in.shape[0]
    full_x, full_y = own_x + 2 * reach, own_y + 2 * reach
    size_x, size_y = full_x - 2, full_y - 2
    filters = weights.shape[-1] // 2
    rows, extra = size_y * size_z, size_y + (-size_y % 16)
    pool_y, pool_z = size_y // 2, size_z // 2

    def body(
        place_ref,
        own_ref,
        x_in_ref,
        x_out_ref,
        y_in_ref,
        y_out_ref,
        edge_ref,
        edge_in_ref,
        edge_out_ref,
        weights_ref,
        out_ref,
        x_ref,
        y_ref,
        side_ref,
        rows_ref,
    ):
        even_x, even_y = place_ref[0] % 2 == 0, place_ref[1] % 2 == 0
        low_x, high_x = place_ref[0] > 0, place_ref[0] < place_ref[3]
        low_y, high_y = place_ref[1] > 0, place_ref[1] < place_ref[4]
        nil = jnp.bfloat16(0)
        x_ref[0] = jnp.where(low_x, jnp.where(even_x, x_out_ref[...], x_in_ref[...]), nil)
        x_ref[1] = jnp.where(high_x, jnp.where(even_x, x_in_ref[...], x_out_ref[...]), nil)
        for x in range(full_x):
            here_low, here_high, here = low_y, high_y, None
            if x < reach:
                here_low, here_high, here = low_y & low_x, high_y & low_x, low_x
            if x >= reach + own_x:
                here_low, here_high, here = low_y & high_x, high_y & high_x, high_x
            y_ref[0, x] = jnp.where(here_low, jnp.where(even_y, y_out_ref[x], y_in_ref[x]), nil)
            y_ref[1, x] = jnp.where(here_high, jnp.where(even_y, y_in_ref[x], y_out_ref[x]), nil)
            middle = edge_ref[x].astype(jnp.float32)
            if here is not None:
                middle = jnp.where(here, middle, 0.0)
            one, other = edge_in_ref[x].astype(jnp.float32), edge_out_ref[x].astype(jnp.float32)
            below = jnp.where(here_low, jnp.where(even_y, other, one), 0.0)
            above = jnp.where(here_high, jnp.where(even_y, one, other), 0.0)
            for dy in range(3):
                if dy < reach:
                    side_ref[dy, x, : reach - dy] = below[dy:]
                side_ref[dy, x, reach - dy : reach - dy + own_y] = middle
                side_ref[dy, x, reach - dy + own_y : size_y] = above[: dy + 1]
                side_ref[dy, x, size_y:] = jnp.zeros((extra - size_y, channels), jnp.float32)

        def lines(x, dy):
            if x < reach:
                middle = x_ref[0, x]
            elif x < reach + own_x:
                middle = own_ref[x - reach]
            else:
                middle = x_ref[1, x - reach - own_x]
            block = jnp.concatenate([y_ref[0, x, dy:], middle, y_ref[1, x, : dy + 1]], axis=0)
            return block.reshape(rows, channels)

        first = place_ref[2] == 0
        line = lax.broadcasted_iota(jnp.int32, (pool_y, pool_z, filters), 0)
        inside_y = ((line > 0) | low_y) & ((line < pool_y - 1) | high_y)
        for pair in range(size_x // 2):
            blocks = []
            for plane in range(4):
                for dy in range(3):
                    main = lines(2 * pair + plane, dy)
                    side = side_ref[dy, 2 * pair + plane].astype(jnp.bfloat16)
                    blocks.append(jnp.concatenate([main, side], axis=0))
            block = jnp.concatenate(blocks, axis=1)
            sums = []
            for tap in range(3):
                kernel = weights_ref[:, :, tap].reshape(12 * channels, 2 * filters)
                sums.append(jnp.dot(block, kernel, preferred_element_type=jnp.float32))
            total = jnp.maximum(join_taps(first, sums, size_y, size_z), 0.0)
            total = jnp.maximum(total[..., :filters], total[..., filters:])
            total = jnp.max(total.reshape(pool_y, 2, size_z, filters), axis=1)
            rows_ref[...] = total.reshape(pool_y * size_z, filters)
            total = jnp.maximum(
                rows_ref[pl.ds(0, pool_y * pool_z, stride=2), :], rows_ref[pl.ds(1, pool_y * pool_z, stride=2), :]
            ).reshape(pool_y, pool_z, filters)
            inside = inside_y
            if pair == 0:
                inside = inside & low_x
            if pair == size_x // 2 - 1:
                inside = inside & high_x
            out_ref[pair] = jnp.where(inside, total, 0.0).astype(out_ref.dtype)

    return pl.pallas_call(
        body,
        in_specs=[pl.BlockSpec(memory_space=pltpu.SMEM)] + [pl.BlockSpec(memory_space=pltpu.VMEM)] * 9,
        out_specs=pl.BlockSpec(memory_space=pltpu.VMEM),
        out_shape=jax.ShapeDtypeStruct((size_x // 2, pool_y, pool_z, filters), jnp.bfloat16),
        scratch_shapes=[
            pltpu.VMEM((2, reach, own_y, size_z, channels), jnp.bfloat16),
            pltpu.VMEM((2, full_x, reach, size_z, channels), jnp.bfloat16),
            pltpu.VMEM((3, full_x, extra, channels), jnp.float32),
            pltpu.VMEM((pool_y * size_z, filters), jnp.float32),
        ],
        compiler_params=pltpu.CompilerParams(vmem_limit_bytes=14 << 20),
        name="encode",
    )(place, near(own), x_in, x_out, y_in, y_out, edge, edge_in, edge_out, near(weights))


def near(array):
    return pltpu.with_memory_space_constraint(array, pltpu.VMEM)


def bring(arrays, after):
    pieces = [(i, n) for i, array in enumerate(arrays) for n in range(array.shape[0])]
    count = len(arrays)

    def body(*refs):
        hbms, outs, sems = refs[:count], refs[count + 1 : -1], refs[-1]
        copies = [pltpu.make_async_copy(hbms[i].at[n], outs[i].at[n], sems.at[k]) for k, (i, n) in enumerate(pieces)]
        for copy in copies:
            copy.start()
        for copy in copies:
            copy.wait()

    return pl.pallas_call(
        body,
        in_specs=[pl.BlockSpec(memory_space=pltpu.HBM)] * count + [pl.BlockSpec(memory_space=pl.ANY)],
        out_specs=[pl.BlockSpec(memory_space=pltpu.VMEM)] * count,
        out_shape=[pltpu.VMEM(array.shape, array.dtype) for array in arrays],
        scratch_shapes=[pltpu.SemaphoreType.DMA((len(pieces),))],
        compiler_params=pltpu.CompilerParams(vmem_limit_bytes=4 << 20),
        name="bring",
    )(*map(far, arrays), after)


def far(array):
    return pltpu.with_memory_space_constraint(array, pltpu.HBM)


def prepare(w_full, w_in, w_out):
    channels, filters = w_full.shape[3:]
    depths = [w.shape[4] for w in (w_in, w_out)]

    def body(
        full_hbm, in_hbm, out_hbm, pair_hbm, to_in_hbm, to_out_hbm, full_ref, pair_ref, in_ref, out_ref, to_in_ref, to_out_ref, sems
    ):
        first = pltpu.make_async_copy(full_hbm, full_ref, sems.at[0])
        first.start()
        jobs = []
        for order, (hbm, ref) in enumerate(((in_hbm, in_ref), (out_hbm, out_ref))):
            copies = []
            for step in range(9):
                for dy in range(3):
                    to = ref.at[step, pl.ds(64 * dy, 64)]
                    sem = sems.at[1 + 27 * order + 3 * step + dy]
                    copies.append(pltpu.make_async_copy(hbm.at[step // 3, dy, step % 3], to, sem))
                    copies[-1].start()
            jobs.append(copies)
        first.wait()
        zero = jnp.zeros((3, 3, channels, filters), jnp.bfloat16)
        results = []
        for plane in range(4):
            pair_ref[plane, :, :, :, :filters] = full_ref[plane] if plane < 3 else zero
            pair_ref[plane, :, :, :, filters:] = full_ref[plane - 1] if plane > 0 else zero
            results.append(pltpu.make_async_copy(pair_ref.at[plane], pair_hbm.at[plane], sems.at[55 + plane]))
            results[-1].start()
        for order, (ref, to_ref, to_hbm) in enumerate(((in_ref, to_in_ref, to_in_hbm), (out_ref, to_out_ref, to_out_hbm))):
            for step in range(9):
                ref[step, 192:] = jnp.zeros((64, depths[order]), jnp.bfloat16)
                for copy in jobs[order][3 * step : 3 * step + 3]:
                    copy.wait()
                to_ref[step] = ref[step].T
                results.append(pltpu.make_async_copy(to_ref.at[step], to_hbm.at[step], sems.at[59 + 9 * order + step]))
                results[-1].start()
        for copy in results:
            copy.wait()

    shapes = [(4, 3, 3, channels, 2 * filters)] + [(9, depth, 256) for depth in depths]
    return pl.pallas_call(
        body,
        in_specs=[pl.BlockSpec(memory_space=pltpu.HBM)] * 3,
        out_specs=[pl.BlockSpec(memory_space=pltpu.HBM)] * 3,
        out_shape=[pltpu.HBM(shape, jnp.bfloat16) for shape in shapes],
        scratch_shapes=[pltpu.VMEM(w_full.shape, jnp.bfloat16), pltpu.VMEM(shapes[0], jnp.bfloat16)]
        + [pltpu.VMEM((9, 256, depth), jnp.bfloat16) for depth in depths]
        + [pltpu.VMEM((9, depth, 256), jnp.bfloat16) for depth in depths]
        + [pltpu.SemaphoreType.DMA((77,))],
        compiler_params=pltpu.CompilerParams(vmem_limit_bytes=20 << 20),
        name="prepare",
    )(far(w_full), far(w_in), far(w_out))


def pack_y(place, own, x_in, x_out):
    own_x, own_y, size_z, channels = own.shape
    reach = x_in.shape[0]
    full_x = own_x + 2 * reach

    def body(place_ref, own_ref, x_in_ref, x_out_ref, inner_ref, outer_ref, plane_ref, inner_edge_ref, outer_edge_ref, rows_ref):
        even_x, even_y, first = place_ref[0] % 2 == 0, place_ref[1] % 2 == 0, place_ref[2] == 0
        below = jnp.where(even_x, x_out_ref[...], x_in_ref[...])
        above = jnp.where(even_x, x_in_ref[...], x_out_ref[...])
        for start, block in ((0, below), (reach, own_ref[...]), (reach + own_x, above)):
            size = block.shape[0]
            low, high = block[:, :reach], block[:, own_y - reach :]
            inner_ref[start : start + size] = jnp.where(even_y, high, low)
            outer_ref[start : start + size] = jnp.where(even_y, low, high)
            block = block.astype(jnp.float32)
            edge = jnp.where(first, block[:, :, size_z - 1 :], block[:, :, :1])
            for x in range(size):
                for y in range(own_y):
                    rows_ref[start + x, y : y + 1] = edge[x, y]
        plane_ref[...] = rows_ref[...].astype(plane_ref.dtype)
        low, high = rows_ref[:, :reach], rows_ref[:, own_y - reach :]
        inner_edge_ref[...] = jnp.where(even_y, high, low).astype(plane_ref.dtype)
        outer_edge_ref[...] = jnp.where(even_y, low, high).astype(plane_ref.dtype)

    return pl.pallas_call(
        body,
        in_specs=[pl.BlockSpec(memory_space=pltpu.SMEM)] + [pl.BlockSpec(memory_space=pltpu.VMEM)] * 3,
        out_specs=[pl.BlockSpec(memory_space=pltpu.VMEM)] * 5,
        out_shape=[jax.ShapeDtypeStruct((full_x, reach, size_z, channels), jnp.bfloat16)] * 2
        + [jax.ShapeDtypeStruct((full_x, rows, channels), jnp.bfloat16) for rows in (own_y, reach, reach)],
        scratch_shapes=[pltpu.VMEM((full_x, own_y, channels), jnp.float32)],
        compiler_params=pltpu.CompilerParams(vmem_limit_bytes=8 << 20),
        name="pack_y",
    )(place, own, x_in, x_out)


def halves(pair_low, pair_high):
    lane = lax.broadcasted_iota(jnp.int32, pair_low.shape, pair_low.ndim - 1)
    axis = pair_low.ndim - 1
    even = jnp.where(lane < 64, pair_low, pltpu.roll(pair_high, 64, axis))
    odd = jnp.where(lane < 64, pltpu.roll(pair_low, 64, axis), pair_high)
    return even, odd


def side_by_side(even, odd):
    lane = lax.broadcasted_iota(jnp.int32, even.shape, even.ndim - 1)
    return jnp.where(lane < 64, even, pltpu.roll(odd, 64, even.ndim - 1))


def pair_planes(pad_ref, pair_ref):
    pairs = pair_ref.shape[1]
    for odd in range(2):
        for pair in range(pairs - odd):
            planes = [pad_ref[2 * pair + odd + n] for n in range(2)]
            pair_ref[odd, pair] = jnp.concatenate(planes, axis=1).astype(pair_ref.dtype)


def column_product(pair_ref, weights_ref, first, start, pairs, size_z):
    channels = pair_ref.shape[-1]
    rows = pairs * size_z * 16
    blocks = []
    for dx in range(3):
        for dz in range(3):
            block = pair_ref[dx % 2, first + dx // 2 : first + dx // 2 + pairs, pl.ds(start + dz, size_z)]
            blocks.append(block.reshape(rows, channels))
    block = jnp.concatenate(blocks, axis=1)
    total = jnp.dot(block, weights_ref[...].reshape(9 * channels, 256), preferred_element_type=jnp.float32)
    groups = pairs * size_z * 2
    low = total[:, :128].reshape(groups, 8, 128)
    mid = pltpu.roll(total[:, :128], 64, 1).reshape(groups, 8, 128)
    high = total[:, 128:].reshape(groups, 8, 128)
    total = pltpu.roll(low, 1, 1) + mid + pltpu.roll(high, 7, 1)
    return jnp.maximum(total, 0.0).reshape(pairs, size_z, 2, 8, 128)


def bottom_in(place, field, weights):
    count, own_x, lines, channels = field.shape
    devices = count // 2
    own_z = size_y = 4
    size_x, all_z, size_z = devices * own_x, 2 * own_z, own_z + 2

    def body(place_ref, field_ref, weights_ref, out_ref, pad_ref, pair_ref):
        zero = jnp.zeros((all_z + 2, 8, channels), jnp.float32)
        pad_ref[0] = zero
        pad_ref[size_x + 1] = zero
        for x in range(size_x):
            pad_ref[x + 1, 0] = zero[0]
            pad_ref[x + 1, all_z + 1] = zero[0]
        for i in range(devices):
            for half in range(2):
                for x in range(own_x):
                    block = field_ref[2 * i + half, x].astype(jnp.float32)
                    for z in range(own_z):
                        to = (1 + own_x * i + x, 1 + own_z * half + z)
                        pad_ref[*to, 0:1] = block[own_z * size_y + z : own_z * size_y + z + 1]
                        pad_ref[*to, 1 : size_y + 1] = block[size_y * z : size_y * z + size_y]
                        line = own_z * (size_y + 1) + z
                        pad_ref[*to, size_y + 1 : size_y + 2] = block[line : line + 1]
                        pad_ref[*to, size_y + 2 :] = zero[0, size_y + 2 :]
        start = 2 * place_ref[2]
        pair_planes(pad_ref, pair_ref)
        for first in range(0, size_x // 2, 2):
            total = column_product(pair_ref, weights_ref, first, start, 2, size_z)
            for pair in range(2):
                both = side_by_side(total[pair, :, 0], total[pair, :, 1])[:, 1 : size_y + 1].astype(out_ref.dtype)
                for i in range(devices):
                    out_ref[i, first + pair] = both

    return pl.pallas_call(
        body,
        in_specs=[pl.BlockSpec(memory_space=space) for space in (pltpu.SMEM, pltpu.VMEM, pltpu.VMEM)],
        out_specs=pl.BlockSpec(memory_space=pltpu.VMEM),
        out_shape=jax.ShapeDtypeStruct((devices, size_x // 2, size_z, size_y, 128), jnp.bfloat16),
        scratch_shapes=[
            pltpu.VMEM((size_x + 2, all_z + 2, 8, channels), jnp.float32),
            pltpu.VMEM((2, size_x // 2 + 1, all_z + 2, 16, channels), jnp.bfloat16),
        ],
        compiler_params=pltpu.CompilerParams(vmem_limit_bytes=16 << 20),
        name="bottom_in",
    )(place, field, near(weights))


def bottom_out(place, field, y_in, y_out, weights):
    devices, pairs, size_z, _, _ = field.shape
    size_x, channels = 2 * pairs, 64 * devices
    own_x = size_x // devices

    def body(place_ref, field_ref, y_in_ref, y_out_ref, weights_ref, out_ref, pad_ref, pair_ref, total_ref):
        even_y = place_ref[1] % 2 == 0
        low_y, high_y = place_ref[1] > 0, place_ref[1] < place_ref[4]
        zero = jnp.zeros((size_z + 2, 8, channels), jnp.float32)
        for ref in (pad_ref, total_ref):
            wide = ref.shape[-1]
            ref[0] = zero[..., :wide]
            ref[size_x + 1] = zero[..., :wide]
            for x in range(size_x):
                ref[x + 1, 0] = zero[0, :, :wide]
                ref[x + 1, size_z + 1] = zero[0, :, :wide]
        for k in range(devices // 2):
            for pair in range(pairs):
                y_first, y_last = [], []
                for i in range(2):
                    one = y_in_ref[2 * k + i, pair].astype(jnp.float32)
                    other = y_out_ref[2 * k + i, pair].astype(jnp.float32)
                    y_first.append(jnp.where(low_y, jnp.where(even_y, other, one), 0.0))
                    y_last.append(jnp.where(high_y, jnp.where(even_y, one, other), 0.0))
                own = [field_ref[2 * k + i, pair].astype(jnp.float32) for i in range(2)]
                for line, blocks in ((0, y_first), (2, own), (6, y_last)):
                    even, odd = halves(*blocks)
                    lines = slice(line, line + even.shape[1])
                    pad_ref[1 + 2 * pair, 1 : size_z + 1, lines, 128 * k : 128 * k + 128] = even
                    pad_ref[2 + 2 * pair, 1 : size_z + 1, lines, 128 * k : 128 * k + 128] = odd
        pair_planes(pad_ref, pair_ref)
        for first in range(0, pairs, 2):
            total = column_product(pair_ref, weights_ref, first, 0, 2, size_z)
            for plane in range(4):
                total_ref[1 + 2 * first + plane, 1 : size_z + 1] = total[plane // 2, :, plane % 2]
        start = 2 * place_ref[2]
        for i in range(size_x // 2 + 1):
            low, high = [total_ref[2 * i + n, pl.ds(start, size_z)] for n in range(2)]
            both = side_by_side(low, high).astype(out_ref.dtype)
            if i < devices:
                out_ref[i, 0] = both
            if i > 0:
                out_ref[i - 1, 1] = both

    return pl.pallas_call(
        body,
        in_specs=[pl.BlockSpec(memory_space=pltpu.SMEM)]
        + [pl.BlockSpec(memory_space=pltpu.VMEM)] * 4,
        out_specs=pl.BlockSpec(memory_space=pltpu.VMEM),
        out_shape=jax.ShapeDtypeStruct((devices, own_x, size_z, 8, 128), jnp.bfloat16),
        scratch_shapes=[
            pltpu.VMEM((size_x + 2, size_z + 2, 8, channels), jnp.float32),
            pltpu.VMEM((2, pairs + 1, size_z + 2, 16, channels), jnp.bfloat16),
            pltpu.VMEM((size_x + 2, size_z + 2, 8, 128), jnp.float32),
        ],
        compiler_params=pltpu.CompilerParams(vmem_limit_bytes=20 << 20),
        name="bottom_out",
    )(place, field, y_in, y_out, near(weights))


def decode_skip(place, skip, edge, weights):
    full_x, full_y, size_z, channels = skip.shape
    size_x, size_y = full_x - 2, full_y - 2
    filters = weights.shape[-1]
    deep = weights.shape[2] - channels
    rows, extra = size_x * size_y * size_z, size_x * size_y

    def body(skip_ref, edge_ref, weights_hbm, out_ref, *refs):
        rest_refs, (weights_ref, sems) = refs[:3], refs[3:]
        copies = [
            pltpu.make_async_copy(weights_hbm.at[step, :, pl.ds(deep, channels)], weights_ref.at[step], sems.at[step])
            for step in range(9)
        ]
        rest = [
            pltpu.make_async_copy(weights_hbm.at[step, :, pl.ds(0, deep)], rest_refs[step], sems.at[9 + step])
            for step in range(3)
        ]
        for copy in copies + rest:
            copy.start()
        edge_plane = edge_ref[...].astype(jnp.float32)
        blocks = []
        for dx in range(3):
            for dy in range(3):
                main = skip_ref[dx : dx + size_x, dy : dy + size_y].astype(jnp.float32).reshape(rows, channels)
                side = edge_plane[dx : dx + size_x, dy : dy + size_y].reshape(extra, channels)
                blocks.append(jnp.concatenate([main, side], axis=0).astype(jnp.bfloat16))
        for copy in copies:
            copy.wait()
        block = jnp.concatenate(blocks, axis=1)
        for tap in range(3):
            kernel = weights_ref[:, tap].reshape(9 * channels, filters)
            out_ref[tap] = jnp.dot(block, kernel, preferred_element_type=jnp.float32)
        for copy in rest:
            copy.wait()

    return pl.pallas_call(
        body,
        in_specs=[pl.BlockSpec(memory_space=pltpu.VMEM)] * 2 + [pl.BlockSpec(memory_space=pltpu.HBM)],
        out_specs=[pl.BlockSpec(memory_space=pltpu.VMEM)] * 4,
        out_shape=[
            pltpu.VMEM((3, rows + extra, filters), jnp.float32),
        ]
        + [pltpu.VMEM((3, deep, filters), jnp.bfloat16)] * 3,
        scratch_shapes=[pltpu.VMEM((9, 3, channels, filters), jnp.bfloat16), pltpu.SemaphoreType.DMA((12,))],
        compiler_params=pltpu.CompilerParams(vmem_limit_bytes=14 << 20),
        name="decode_skip",
    )(skip, edge, far(weights))


def decode(place, bottom, skip_sums, first_weights, weights, shape):
    devices, pairs, coarse_z, _, _ = bottom.shape
    size_x, size_y, size_z = shape
    full_x, full_y = size_x + 2, size_y + 2
    channels = 64 * devices
    filters = weights.shape[-1]
    rows, extra = size_x * size_y * size_z, size_x * size_y

    def body(place_ref, bottom_ref, skip_ref, *refs):
        near_refs, (weights_hbm, out_ref, main_ref, side_ref, sums_ref, weights_ref, sems) = refs[:3], refs[3:]
        copies = [
            pltpu.make_async_copy(weights_hbm.at[3 + step, :, pl.ds(0, channels)], weights_ref.at[step], sems.at[step])
            for step in range(6)
        ]
        for copy in copies:
            copy.start()
        first = place_ref[2] == 0
        planes = [[] for _ in range(2 * pairs)]
        for k in range(devices // 2):
            for pair in range(pairs):
                low, high = [bottom_ref[2 * k + i, pair].astype(jnp.float32) for i in range(2)]
                even, odd = halves(low, high)
                planes[2 * pair].append(even.reshape(coarse_z * 8, 128))
                planes[2 * pair + 1].append(odd.reshape(coarse_z * 8, 128))

        def choice(y, z, source):
            line = (y + 1) // 2 + 1
            inside = ((line > 1) | (place_ref[1] > 0)) & ((line < coarse_z) | (place_ref[1] < place_ref[4]))
            return jnp.where((source == z * 8 + line) & inside, 1.0, 0.0).astype(jnp.bfloat16)

        shape = (full_y * size_z, coarse_z * 8)
        row = lax.broadcasted_iota(jnp.int32, shape, 0)
        spread = choice(row // size_z, row % size_z // 2 + 1, lax.broadcasted_iota(jnp.int32, shape, 1))
        shape = (16, coarse_z * 8)
        row = lax.broadcasted_iota(jnp.int32, shape, 0)
        other = jnp.where(first, coarse_z - 1, 0)
        spread_edge = choice(row, other, lax.broadcasted_iota(jnp.int32, shape, 1))
        for plane in range(2 * pairs):
            coarse = jnp.concatenate(planes[plane], axis=1).astype(jnp.bfloat16)
            fine = jnp.dot(spread, coarse, preferred_element_type=jnp.float32)
            fine_edge = jnp.dot(spread_edge, coarse, preferred_element_type=jnp.float32)
            for x in range(full_x):
                if (x + 1) // 2 != plane:
                    continue
                for dy in range(3):
                    main_ref[dy, x] = fine[8 * dy : 8 * dy + size_y * size_z].astype(jnp.bfloat16)
                    side_ref[dy, x] = fine_edge[dy : dy + size_y]
        for dx in range(3):
            blocks = []
            for dy in range(3):
                main = main_ref[dy, dx : dx + size_x].reshape(rows, channels)
                side = side_ref[dy, dx : dx + size_x].reshape(extra, channels).astype(jnp.bfloat16)
                blocks.append(jnp.concatenate([main, side], axis=0))
                if dx:
                    copies[3 * dx + dy - 3].wait()
            block = jnp.concatenate(blocks, axis=1)
            for tap in range(3):
                if dx == 0:
                    kernel = jnp.concatenate([ref[tap] for ref in near_refs], axis=0)
                    sums_ref[tap] = skip_ref[tap] + jnp.dot(block, kernel, preferred_element_type=jnp.float32)
                else:
                    kernel = weights_ref[3 * dx - 3 : 3 * dx, tap].reshape(3 * channels, filters)
                    sums_ref[tap] += jnp.dot(block, kernel, preferred_element_type=jnp.float32)
        total = join_taps(first, [sums_ref[tap] for tap in range(3)], extra, size_z)
        out_ref[...] = total.reshape(size_x, size_y, size_z, filters).astype(out_ref.dtype)

    return pl.pallas_call(
        body,
        in_specs=[pl.BlockSpec(memory_space=pltpu.SMEM)]
        + [pl.BlockSpec(memory_space=pltpu.VMEM)] * 5
        + [pl.BlockSpec(memory_space=pltpu.HBM)],
        out_specs=pl.BlockSpec(memory_space=pltpu.VMEM),
        out_shape=jax.ShapeDtypeStruct((size_x, size_y, size_z, filters), jnp.bfloat16),
        scratch_shapes=[
            pltpu.VMEM((3, full_x, size_y * size_z, channels), jnp.bfloat16),
            pltpu.VMEM((3, full_x, size_y, channels), jnp.float32),
            pltpu.VMEM((3, rows + extra, filters), jnp.float32),
            pltpu.VMEM((6, 3, channels, filters), jnp.bfloat16),
            pltpu.SemaphoreType.DMA((6,)),
        ],
        compiler_params=pltpu.CompilerParams(vmem_limit_bytes=20 << 20),
        name="decode",
    )(place, bottom, near(skip_sums), *map(near, first_weights), far(weights))


def solution(mesh):
    gx, gy, gz = mesh.shape["gx"], mesh.shape["gy"], mesh.shape["gz"]

    def local(volume, w_full, w_half, w_bottom_in, w_bottom_out, w_up):
        place_z = lax.axis_index("gz")
        place = jnp.stack([lax.axis_index("gx"), lax.axis_index("gy"), place_z, jnp.int32(gx - 1), jnp.int32(gy - 1)])
        swap = [(0, 1), (1, 0)]

        def edge_of(plane_low, plane_high):
            return lax.ppermute(jnp.where(place_z == 0, plane_high, plane_low), "gz", swap)

        x_in, x_out = swaps(volume[:3], volume[-3:], "gx", gx)
        turned = [w.transpose(0, 1, 2, 4, 3) for w in (w_bottom_in, w_bottom_out)]
        (w_pair, w_in, w_out), x_in, x_out = lax.optimization_barrier((prepare(w_full, *turned), x_in, x_out))
        y_inner, y_outer, plane, edge_inner, edge_outer = pack_y(place, volume, x_in, x_out)
        y_in, y_out = send(y_inner, y_outer, "gy", gy)
        edge = lax.ppermute(plane, "gz", swap)
        edge_in, edge_out = send(edge_inner, edge_outer, ("gy", "gz"), gy)
        own, w_pair = bring([volume, w_pair], plane)
        pooled = encode(place, own, x_in, x_out, y_in, y_out, edge, edge_in, edge_out, w_pair)

        edge = edge_of(pooled[:, :, 0], pooled[:, :, -1])
        skip, coarse = half_level(place, pooled, edge, w_half.reshape(9, 3, w_half.shape[3], w_half.shape[4]))
        lines = coarse.reshape(coarse.shape[0], 4, 4, coarse.shape[2])
        below, above = halo(lines, "gy", gy, 2, 1)
        column = jnp.concatenate([coarse, below[:, :, 0], above[:, :, 0]], axis=1)
        column = jnp.broadcast_to(column[None], (gx * gz,) + column.shape)
        (w_in,) = bring([w_in], column)
        column = lax.all_to_all(column, ("gx", "gz"), 0, 0)
        first = bottom_in(place, column, w_in)
        (w_out,) = bring([w_out], first)
        first = lax.all_to_all(first, "gx", 0, 0)
        around = extend(skip, "gx", gx, 0, 1)
        around = extend(around, "gy", gy, 1, 1)
        side = edge_of(around[:, :, 0], around[:, :, -1])
        first, around, side = lax.optimization_barrier((first, around, side))
        y_in, y_out = swaps(first[:, :, :, :2], first[:, :, :, -2:], "gy", gy)
        second = bottom_out(place, first, y_in, y_out, w_out)
        second = lax.all_to_all(second, "gx", 0, 0)
        w_up = w_up.reshape(9, 3, w_up.shape[3], w_up.shape[4])
        skip_sums, *w_near = decode_skip(place, around, side, w_up)
        return decode(place, second, skip_sums, w_near, w_up, skip.shape[:3])

    space = P("gx", "gy", "gz", None)
    filters = P(None, None, None, None, "gx")
    return jax.shard_map(
        local,
        mesh=mesh,
        in_specs=(space, P(), P(), filters, filters, P()),
        out_specs=space,
        check_vma=False,
    )
```

```python
import jax
import jax.numpy as jnp
from jax import lax
from jax.experimental import pallas as pl
from jax.experimental.pallas import tpu as pltpu
from jax.sharding import PartitionSpec as P


def send(inner_block, outer_block, axis, count):
    inner = [(i, i ^ 1) for i in range(count)]
    outer = [(i, (((i + 1) ^ 1) - 1) % count) for i in range(count)]
    if isinstance(axis, tuple):
        inner, outer = [[(2 * i + n, 2 * j + 1 - n) for i, j in pairs for n in range(2)] for pairs in (inner, outer)]
    return lax.ppermute(inner_block, axis, inner), lax.ppermute(outer_block, axis, outer)


def swaps(low, high, axis, count):
    even = lax.axis_index(axis) % 2 == 0
    return send(jnp.where(even, high, low), jnp.where(even, low, high), axis, count)


def ordered(got_in, got_out, axis):
    even = lax.axis_index(axis) % 2 == 0
    return jnp.where(even, got_out, got_in), jnp.where(even, got_in, got_out)


def halo(field, axis, count, dim, width):
    place = lax.axis_index(axis)
    size = field.shape[dim]
    low = lax.slice_in_dim(field, 0, width, axis=dim)
    high = lax.slice_in_dim(field, size - width, size, axis=dim)
    below, above = ordered(*swaps(low, high, axis, count), axis)
    zero = jnp.zeros_like(low)
    return jnp.where(place > 0, below, zero), jnp.where(place < count - 1, above, zero)


def extend(field, axis, count, dim, width):
    below, above = halo(field, axis, count, dim, width)
    return jnp.concatenate([below, field, above], axis=dim)


def half_level(place, field, edge, weights):
    full_x, full_y, size_z, channels = field.shape
    size_x, size_y = full_x - 2, full_y - 2
    filters = weights.shape[-1]
    rows, extra = size_x * size_y * size_z, size_x * size_y

    def body(place_ref, field_ref, edge_ref, weights_ref, out_ref, coarse_ref, rows_ref, coarse_rows_ref):
        first = place_ref[2] == 0
        edge_plane = edge_ref[...].astype(jnp.float32)
        blocks = []
        for dx in range(3):
            for dy in range(3):
                main = field_ref[dx : dx + size_x, dy : dy + size_y].astype(jnp.float32).reshape(rows, channels)
                side = edge_plane[dx : dx + size_x, dy : dy + size_y].reshape(extra, channels)
                blocks.append(jnp.concatenate([main, side], axis=0).astype(jnp.bfloat16))
        block = jnp.concatenate(blocks, axis=1)
        sums = []
        for tap in range(3):
            kernel = weights_ref[:, tap].reshape(9 * channels, filters)
            sums.append(jnp.dot(block, kernel, preferred_element_type=jnp.float32))
        total = jnp.maximum(join_taps(first, sums, extra, size_z), 0.0)
        out_ref[...] = total.reshape(size_x, size_y, size_z, filters).astype(out_ref.dtype)
        total = jnp.max(total.reshape(size_x // 2, 2, size_y // 2, 2, size_z, filters), axis=(1, 3))
        count = size_y // 2
        for part in range(filters // 128):
            rows_ref[...] = total[..., 128 * part : 128 * part + 128].reshape(rows // 4, 128)
            for x in range(size_x // 2):
                for z in range(size_z // 2):
                    start = x * count * size_z + 2 * z
                    pooled = jnp.maximum(
                        rows_ref[pl.ds(start, count, stride=size_z), :], rows_ref[pl.ds(start + 1, count, stride=size_z), :]
                    )
                    coarse_rows_ref[x, count * z : count * z + count, 128 * part : 128 * part + 128] = pooled
        coarse_ref[...] = coarse_rows_ref[...].astype(coarse_ref.dtype)

    return pl.pallas_call(
        body,
        in_specs=[pl.BlockSpec(memory_space=pltpu.SMEM)] + [pl.BlockSpec(memory_space=pltpu.VMEM)] * 3,
        out_specs=[pl.BlockSpec(memory_space=pltpu.VMEM)] * 2,
        out_shape=[
            jax.ShapeDtypeStruct((size_x, size_y, size_z, filters), jnp.bfloat16),
            jax.ShapeDtypeStruct((size_x // 2, size_z * size_y // 4, filters), jnp.bfloat16),
        ],
        scratch_shapes=[
            pltpu.VMEM((rows // 4, 128), jnp.float32),
            pltpu.VMEM((size_x // 2, size_z * size_y // 4, filters), jnp.float32),
        ],
        compiler_params=pltpu.CompilerParams(vmem_limit_bytes=12 << 20),
        name="half_level",
    )(place, field, edge, weights)


def join_taps(first, sums, groups, size_z):
    rows, filters = groups * size_z, sums[0].shape[-1]
    low, mid, high = [total[:rows].reshape(groups, size_z, filters) for total in sums]
    below = jnp.where(first, 0.0, sums[0][rows : rows + groups])
    above = jnp.where(first, sums[2][rows : rows + groups], 0.0)
    index = lax.broadcasted_iota(jnp.int32, (groups, size_z, filters), 1)
    down = jnp.where(index == 0, below[:, None, :], pltpu.roll(low, 1, 1))
    up = jnp.where(index == size_z - 1, above[:, None, :], pltpu.roll(high, size_z - 1, 1))
    return down + mid + up


def encode(place, own, x_in, x_out, y_in, y_out, edge, edge_in, edge_out, weights):
    own_x, own_y, size_z, channels = own.shape
    reach = x_in.shape[0]
    full_x, full_y = own_x + 2 * reach, own_y + 2 * reach
    size_x, size_y = full_x - 2, full_y - 2
    filters = weights.shape[-1] // 2
    rows, extra = size_y * size_z, size_y + (-size_y % 16)
    pool_y, pool_z = size_y // 2, size_z // 2

    def body(
        place_ref,
        own_ref,
        x_in_ref,
        x_out_ref,
        y_in_ref,
        y_out_ref,
        edge_ref,
        edge_in_ref,
        edge_out_ref,
        weights_ref,
        out_ref,
        x_ref,
        y_ref,
        side_ref,
        rows_ref,
    ):
        even_x, even_y = place_ref[0] % 2 == 0, place_ref[1] % 2 == 0
        low_x, high_x = place_ref[0] > 0, place_ref[0] < place_ref[3]
        low_y, high_y = place_ref[1] > 0, place_ref[1] < place_ref[4]
        nil = jnp.bfloat16(0)
        x_ref[0] = jnp.where(low_x, jnp.where(even_x, x_out_ref[...], x_in_ref[...]), nil)
        x_ref[1] = jnp.where(high_x, jnp.where(even_x, x_in_ref[...], x_out_ref[...]), nil)
        for x in range(full_x):
            here_low, here_high, here = low_y, high_y, None
            if x < reach:
                here_low, here_high, here = low_y & low_x, high_y & low_x, low_x
            if x >= reach + own_x:
                here_low, here_high, here = low_y & high_x, high_y & high_x, high_x
            y_ref[0, x] = jnp.where(here_low, jnp.where(even_y, y_out_ref[x], y_in_ref[x]), nil)
            y_ref[1, x] = jnp.where(here_high, jnp.where(even_y, y_in_ref[x], y_out_ref[x]), nil)
            middle = edge_ref[x].astype(jnp.float32)
            if here is not None:
                middle = jnp.where(here, middle, 0.0)
            one, other = edge_in_ref[x].astype(jnp.float32), edge_out_ref[x].astype(jnp.float32)
            below = jnp.where(here_low, jnp.where(even_y, other, one), 0.0)
            above = jnp.where(here_high, jnp.where(even_y, one, other), 0.0)
            for dy in range(3):
                if dy < reach:
                    side_ref[dy, x, : reach - dy] = below[dy:]
                side_ref[dy, x, reach - dy : reach - dy + own_y] = middle
                side_ref[dy, x, reach - dy + own_y : size_y] = above[: dy + 1]
                side_ref[dy, x, size_y:] = jnp.zeros((extra - size_y, channels), jnp.float32)

        def lines(x, dy):
            if x < reach:
                middle = x_ref[0, x]
            elif x < reach + own_x:
                middle = own_ref[x - reach]
            else:
                middle = x_ref[1, x - reach - own_x]
            block = jnp.concatenate([y_ref[0, x, dy:], middle, y_ref[1, x, : dy + 1]], axis=0)
            return block.reshape(rows, channels)

        first = place_ref[2] == 0
        line = lax.broadcasted_iota(jnp.int32, (pool_y, pool_z, filters), 0)
        inside_y = ((line > 0) | low_y) & ((line < pool_y - 1) | high_y)
        for pair in range(size_x // 2):
            blocks = []
            for plane in range(4):
                for dy in range(3):
                    main = lines(2 * pair + plane, dy)
                    side = side_ref[dy, 2 * pair + plane].astype(jnp.bfloat16)
                    blocks.append(jnp.concatenate([main, side], axis=0))
            block = jnp.concatenate(blocks, axis=1)
            sums = []
            for tap in range(3):
                kernel = weights_ref[:, :, tap].reshape(12 * channels, 2 * filters)
                sums.append(jnp.dot(block, kernel, preferred_element_type=jnp.float32))
            total = jnp.maximum(join_taps(first, sums, size_y, size_z), 0.0)
            total = jnp.maximum(total[..., :filters], total[..., filters:])
            total = jnp.max(total.reshape(pool_y, 2, size_z, filters), axis=1)
            rows_ref[...] = total.reshape(pool_y * size_z, filters)
            total = jnp.maximum(
                rows_ref[pl.ds(0, pool_y * pool_z, stride=2), :], rows_ref[pl.ds(1, pool_y * pool_z, stride=2), :]
            ).reshape(pool_y, pool_z, filters)
            inside = inside_y
            if pair == 0:
                inside = inside & low_x
            if pair == size_x // 2 - 1:
                inside = inside & high_x
            out_ref[pair] = jnp.where(inside, total, 0.0).astype(out_ref.dtype)

    return pl.pallas_call(
        body,
        in_specs=[pl.BlockSpec(memory_space=pltpu.SMEM)] + [pl.BlockSpec(memory_space=pltpu.VMEM)] * 9,
        out_specs=pl.BlockSpec(memory_space=pltpu.VMEM),
        out_shape=jax.ShapeDtypeStruct((size_x // 2, pool_y, pool_z, filters), jnp.bfloat16),
        scratch_shapes=[
            pltpu.VMEM((2, reach, own_y, size_z, channels), jnp.bfloat16),
            pltpu.VMEM((2, full_x, reach, size_z, channels), jnp.bfloat16),
            pltpu.VMEM((3, full_x, extra, channels), jnp.float32),
            pltpu.VMEM((pool_y * size_z, filters), jnp.float32),
        ],
        compiler_params=pltpu.CompilerParams(vmem_limit_bytes=14 << 20),
        name="encode",
    )(place, near(own), x_in, x_out, y_in, y_out, edge, edge_in, edge_out, near(weights))


def near(array):
    return pltpu.with_memory_space_constraint(array, pltpu.VMEM)


def bring(arrays, after):
    pieces = [(i, n) for i, array in enumerate(arrays) for n in range(array.shape[0])]
    count = len(arrays)

    def body(*refs):
        hbms, outs, sems = refs[:count], refs[count + 1 : -1], refs[-1]
        copies = [pltpu.make_async_copy(hbms[i].at[n], outs[i].at[n], sems.at[k]) for k, (i, n) in enumerate(pieces)]
        for copy in copies:
            copy.start()
        for copy in copies:
            copy.wait()

    return pl.pallas_call(
        body,
        in_specs=[pl.BlockSpec(memory_space=pltpu.HBM)] * count + [pl.BlockSpec(memory_space=pl.ANY)],
        out_specs=[pl.BlockSpec(memory_space=pltpu.VMEM)] * count,
        out_shape=[pltpu.VMEM(array.shape, array.dtype) for array in arrays],
        scratch_shapes=[pltpu.SemaphoreType.DMA((len(pieces),))],
        compiler_params=pltpu.CompilerParams(vmem_limit_bytes=4 << 20),
        name="bring",
    )(*map(far, arrays), after)


def far(array):
    return pltpu.with_memory_space_constraint(array, pltpu.HBM)


def prepare(w_full, w_in, w_out):
    channels, filters = w_full.shape[3:]
    depths = [w.shape[4] for w in (w_in, w_out)]

    def body(
        full_hbm, in_hbm, out_hbm, pair_hbm, to_in_hbm, to_out_hbm, full_ref, pair_ref, in_ref, out_ref, to_in_ref, to_out_ref, sems
    ):
        first = pltpu.make_async_copy(full_hbm, full_ref, sems.at[0])
        first.start()
        jobs = []
        for order, (hbm, ref) in enumerate(((in_hbm, in_ref), (out_hbm, out_ref))):
            copies = []
            for step in range(9):
                for dy in range(3):
                    to = ref.at[step, pl.ds(64 * dy, 64)]
                    sem = sems.at[1 + 27 * order + 3 * step + dy]
                    copies.append(pltpu.make_async_copy(hbm.at[step // 3, dy, step % 3], to, sem))
                    copies[-1].start()
            jobs.append(copies)
        first.wait()
        zero = jnp.zeros((3, 3, channels, filters), jnp.bfloat16)
        results = []
        for plane in range(4):
            pair_ref[plane, :, :, :, :filters] = full_ref[plane] if plane < 3 else zero
            pair_ref[plane, :, :, :, filters:] = full_ref[plane - 1] if plane > 0 else zero
            results.append(pltpu.make_async_copy(pair_ref.at[plane], pair_hbm.at[plane], sems.at[55 + plane]))
            results[-1].start()
        for order, (ref, to_ref, to_hbm) in enumerate(((in_ref, to_in_ref, to_in_hbm), (out_ref, to_out_ref, to_out_hbm))):
            for step in range(9):
                ref[step, 192:] = jnp.zeros((64, depths[order]), jnp.bfloat16)
                for copy in jobs[order][3 * step : 3 * step + 3]:
                    copy.wait()
                to_ref[step] = ref[step].T
                results.append(pltpu.make_async_copy(to_ref.at[step], to_hbm.at[step], sems.at[59 + 9 * order + step]))
                results[-1].start()
        for copy in results:
            copy.wait()

    shapes = [(4, 3, 3, channels, 2 * filters)] + [(9, depth, 256) for depth in depths]
    return pl.pallas_call(
        body,
        in_specs=[pl.BlockSpec(memory_space=pltpu.HBM)] * 3,
        out_specs=[pl.BlockSpec(memory_space=pltpu.HBM)] * 3,
        out_shape=[pltpu.HBM(shape, jnp.bfloat16) for shape in shapes],
        scratch_shapes=[pltpu.VMEM(w_full.shape, jnp.bfloat16), pltpu.VMEM(shapes[0], jnp.bfloat16)]
        + [pltpu.VMEM((9, 256, depth), jnp.bfloat16) for depth in depths]
        + [pltpu.VMEM((9, depth, 256), jnp.bfloat16) for depth in depths]
        + [pltpu.SemaphoreType.DMA((77,))],
        compiler_params=pltpu.CompilerParams(vmem_limit_bytes=20 << 20),
        name="prepare",
    )(far(w_full), far(w_in), far(w_out))


def pack_y(place, own, x_in, x_out):
    own_x, own_y, size_z, channels = own.shape
    reach = x_in.shape[0]
    full_x = own_x + 2 * reach

    def body(place_ref, own_ref, x_in_ref, x_out_ref, inner_ref, outer_ref, plane_ref, inner_edge_ref, outer_edge_ref, rows_ref):
        even_x, even_y, first = place_ref[0] % 2 == 0, place_ref[1] % 2 == 0, place_ref[2] == 0
        below = jnp.where(even_x, x_out_ref[...], x_in_ref[...])
        above = jnp.where(even_x, x_in_ref[...], x_out_ref[...])
        for start, block in ((0, below), (reach, own_ref[...]), (reach + own_x, above)):
            size = block.shape[0]
            low, high = block[:, :reach], block[:, own_y - reach :]
            inner_ref[start : start + size] = jnp.where(even_y, high, low)
            outer_ref[start : start + size] = jnp.where(even_y, low, high)
            block = block.astype(jnp.float32)
            edge = jnp.where(first, block[:, :, size_z - 1 :], block[:, :, :1])
            for x in range(size):
                for y in range(own_y):
                    rows_ref[start + x, y : y + 1] = edge[x, y]
        plane_ref[...] = rows_ref[...].astype(plane_ref.dtype)
        low, high = rows_ref[:, :reach], rows_ref[:, own_y - reach :]
        inner_edge_ref[...] = jnp.where(even_y, high, low).astype(plane_ref.dtype)
        outer_edge_ref[...] = jnp.where(even_y, low, high).astype(plane_ref.dtype)

    return pl.pallas_call(
        body,
        in_specs=[pl.BlockSpec(memory_space=pltpu.SMEM)] + [pl.BlockSpec(memory_space=pltpu.VMEM)] * 3,
        out_specs=[pl.BlockSpec(memory_space=pltpu.VMEM)] * 5,
        out_shape=[jax.ShapeDtypeStruct((full_x, reach, size_z, channels), jnp.bfloat16)] * 2
        + [jax.ShapeDtypeStruct((full_x, rows, channels), jnp.bfloat16) for rows in (own_y, reach, reach)],
        scratch_shapes=[pltpu.VMEM((full_x, own_y, channels), jnp.float32)],
        compiler_params=pltpu.CompilerParams(vmem_limit_bytes=8 << 20),
        name="pack_y",
    )(place, own, x_in, x_out)


def halves(pair_low, pair_high):
    lane = lax.broadcasted_iota(jnp.int32, pair_low.shape, pair_low.ndim - 1)
    axis = pair_low.ndim - 1
    even = jnp.where(lane < 64, pair_low, pltpu.roll(pair_high, 64, axis))
    odd = jnp.where(lane < 64, pltpu.roll(pair_low, 64, axis), pair_high)
    return even, odd


def side_by_side(even, odd):
    lane = lax.broadcasted_iota(jnp.int32, even.shape, even.ndim - 1)
    return jnp.where(lane < 64, even, pltpu.roll(odd, 64, even.ndim - 1))


def pair_planes(pad_ref, pair_ref):
    pairs = pair_ref.shape[1]
    for odd in range(2):
        for pair in range(pairs - odd):
            planes = [pad_ref[2 * pair + odd + n] for n in range(2)]
            pair_ref[odd, pair] = jnp.concatenate(planes, axis=1).astype(pair_ref.dtype)


def column_product(pair_ref, weights_ref, first, start, pairs, size_z):
    channels = pair_ref.shape[-1]
    rows = pairs * size_z * 16
    blocks = []
    for dx in range(3):
        for dz in range(3):
            block = pair_ref[dx % 2, first + dx // 2 : first + dx // 2 + pairs, pl.ds(start + dz, size_z)]
            blocks.append(block.reshape(rows, channels))
    block = jnp.concatenate(blocks, axis=1)
    total = jnp.dot(block, weights_ref[...].reshape(9 * channels, 256), preferred_element_type=jnp.float32)
    groups = pairs * size_z * 2
    low = total[:, :128].reshape(groups, 8, 128)
    mid = pltpu.roll(total[:, :128], 64, 1).reshape(groups, 8, 128)
    high = total[:, 128:].reshape(groups, 8, 128)
    total = pltpu.roll(low, 1, 1) + mid + pltpu.roll(high, 7, 1)
    return jnp.maximum(total, 0.0).reshape(pairs, size_z, 2, 8, 128)


def bottom_in(place, field, weights):
    count, own_x, lines, channels = field.shape
    devices = count // 2
    own_z = size_y = 4
    size_x, all_z, size_z = devices * own_x, 2 * own_z, own_z + 2

    def body(place_ref, field_ref, weights_ref, out_ref, pad_ref, pair_ref):
        zero = jnp.zeros((all_z + 2, 8, channels), jnp.float32)
        pad_ref[0] = zero
        pad_ref[size_x + 1] = zero
        for x in range(size_x):
            pad_ref[x + 1, 0] = zero[0]
            pad_ref[x + 1, all_z + 1] = zero[0]
        for i in range(devices):
            for half in range(2):
                for x in range(own_x):
                    block = field_ref[2 * i + half, x].astype(jnp.float32)
                    for z in range(own_z):
                        to = (1 + own_x * i + x, 1 + own_z * half + z)
                        pad_ref[*to, 0:1] = block[own_z * size_y + z : own_z * size_y + z + 1]
                        pad_ref[*to, 1 : size_y + 1] = block[size_y * z : size_y * z + size_y]
                        line = own_z * (size_y + 1) + z
                        pad_ref[*to, size_y + 1 : size_y + 2] = block[line : line + 1]
                        pad_ref[*to, size_y + 2 :] = zero[0, size_y + 2 :]
        start = 2 * place_ref[2]
        pair_planes(pad_ref, pair_ref)
        for first in range(0, size_x // 2, 2):
            total = column_product(pair_ref, weights_ref, first, start, 2, size_z)
            for pair in range(2):
                both = side_by_side(total[pair, :, 0], total[pair, :, 1])[:, 1 : size_y + 1].astype(out_ref.dtype)
                for i in range(devices):
                    out_ref[i, first + pair] = both

    return pl.pallas_call(
        body,
        in_specs=[pl.BlockSpec(memory_space=space) for space in (pltpu.SMEM, pltpu.VMEM, pltpu.VMEM)],
        out_specs=pl.BlockSpec(memory_space=pltpu.VMEM),
        out_shape=jax.ShapeDtypeStruct((devices, size_x // 2, size_z, size_y, 128), jnp.bfloat16),
        scratch_shapes=[
            pltpu.VMEM((size_x + 2, all_z + 2, 8, channels), jnp.float32),
            pltpu.VMEM((2, size_x // 2 + 1, all_z + 2, 16, channels), jnp.bfloat16),
        ],
        compiler_params=pltpu.CompilerParams(vmem_limit_bytes=16 << 20),
        name="bottom_in",
    )(place, field, near(weights))


def bottom_out(place, field, y_in, y_out, weights):
    devices, pairs, size_z, _, _ = field.shape
    size_x, channels = 2 * pairs, 64 * devices
    own_x = size_x // devices

    def body(place_ref, field_ref, y_in_ref, y_out_ref, weights_ref, out_ref, pad_ref, pair_ref, total_ref):
        even_y = place_ref[1] % 2 == 0
        low_y, high_y = place_ref[1] > 0, place_ref[1] < place_ref[4]
        zero = jnp.zeros((size_z + 2, 8, channels), jnp.float32)
        for ref in (pad_ref, total_ref):
            wide = ref.shape[-1]
            ref[0] = zero[..., :wide]
            ref[size_x + 1] = zero[..., :wide]
            for x in range(size_x):
                ref[x + 1, 0] = zero[0, :, :wide]
                ref[x + 1, size_z + 1] = zero[0, :, :wide]
        for k in range(devices // 2):
            for pair in range(pairs):
                y_first, y_last = [], []
                for i in range(2):
                    one = y_in_ref[2 * k + i, pair].astype(jnp.float32)
                    other = y_out_ref[2 * k + i, pair].astype(jnp.float32)
                    y_first.append(jnp.where(low_y, jnp.where(even_y, other, one), 0.0))
                    y_last.append(jnp.where(high_y, jnp.where(even_y, one, other), 0.0))
                own = [field_ref[2 * k + i, pair].astype(jnp.float32) for i in range(2)]
                for line, blocks in ((0, y_first), (2, own), (6, y_last)):
                    even, odd = halves(*blocks)
                    lines = slice(line, line + even.shape[1])
                    pad_ref[1 + 2 * pair, 1 : size_z + 1, lines, 128 * k : 128 * k + 128] = even
                    pad_ref[2 + 2 * pair, 1 : size_z + 1, lines, 128 * k : 128 * k + 128] = odd
        pair_planes(pad_ref, pair_ref)
        for first in range(0, pairs, 2):
            total = column_product(pair_ref, weights_ref, first, 0, 2, size_z)
            for plane in range(4):
                total_ref[1 + 2 * first + plane, 1 : size_z + 1] = total[plane // 2, :, plane % 2]
        start = 2 * place_ref[2]
        for i in range(size_x // 2 + 1):
            low, high = [total_ref[2 * i + n, pl.ds(start, size_z)] for n in range(2)]
            both = side_by_side(low, high).astype(out_ref.dtype)
            if i < devices:
                out_ref[i, 0] = both
            if i > 0:
                out_ref[i - 1, 1] = both

    return pl.pallas_call(
        body,
        in_specs=[pl.BlockSpec(memory_space=pltpu.SMEM)]
        + [pl.BlockSpec(memory_space=pltpu.VMEM)] * 4,
        out_specs=pl.BlockSpec(memory_space=pltpu.VMEM),
        out_shape=jax.ShapeDtypeStruct((devices, own_x, size_z, 8, 128), jnp.bfloat16),
        scratch_shapes=[
            pltpu.VMEM((size_x + 2, size_z + 2, 8, channels), jnp.float32),
            pltpu.VMEM((2, pairs + 1, size_z + 2, 16, channels), jnp.bfloat16),
            pltpu.VMEM((size_x + 2, size_z + 2, 8, 128), jnp.float32),
        ],
        compiler_params=pltpu.CompilerParams(vmem_limit_bytes=20 << 20),
        name="bottom_out",
    )(place, field, y_in, y_out, near(weights))


def decode_skip(place, skip, edge, weights):
    full_x, full_y, size_z, channels = skip.shape
    size_x, size_y = full_x - 2, full_y - 2
    filters = weights.shape[-1]
    deep = weights.shape[2] - channels
    rows, extra = size_x * size_y * size_z, size_x * size_y

    def body(place_ref, skip_ref, edge_ref, weights_hbm, out_hbm, *refs):
        rest_refs, (weights_ref, out_ref, sems) = refs[:4], refs[4:]
        copies = [
            pltpu.make_async_copy(weights_hbm.at[step, :, pl.ds(deep, channels)], weights_ref.at[step], sems.at[step])
            for step in range(9)
        ]
        rest = [
            pltpu.make_async_copy(weights_hbm.at[step, :, pl.ds(0, deep)], rest_refs[step], sems.at[9 + step])
            for step in range(4)
        ]
        for copy in copies + rest:
            copy.start()
        edge_plane = edge_ref[...].astype(jnp.float32)
        blocks = []
        for dx in range(3):
            for dy in range(3):
                main = skip_ref[dx : dx + size_x, dy : dy + size_y].astype(jnp.float32).reshape(rows, channels)
                side = edge_plane[dx : dx + size_x, dy : dy + size_y].reshape(extra, channels)
                blocks.append(jnp.concatenate([main, side], axis=0).astype(jnp.bfloat16))
        for copy in copies:
            copy.wait()
        block = jnp.concatenate(blocks, axis=1)
        sums = []
        for tap in range(3):
            kernel = weights_ref[:, tap].reshape(9 * channels, filters)
            sums.append(jnp.dot(block, kernel, preferred_element_type=jnp.float32))
        out_ref[...] = join_taps(place_ref[2] == 0, sums, extra, size_z)
        rest.append(pltpu.make_async_copy(out_ref, out_hbm, sems.at[13]))
        rest[-1].start()
        for copy in rest:
            copy.wait()

    return pl.pallas_call(
        body,
        in_specs=[pl.BlockSpec(memory_space=pltpu.SMEM)]
        + [pl.BlockSpec(memory_space=pltpu.VMEM)] * 2
        + [pl.BlockSpec(memory_space=pltpu.HBM)],
        out_specs=[pl.BlockSpec(memory_space=pltpu.HBM)] + [pl.BlockSpec(memory_space=pltpu.VMEM)] * 4,
        out_shape=[
            pltpu.HBM((extra, size_z, filters), jnp.float32),
        ]
        + [pltpu.VMEM((3, deep, filters), jnp.bfloat16)] * 4,
        scratch_shapes=[
            pltpu.VMEM((9, 3, channels, filters), jnp.bfloat16),
            pltpu.VMEM((extra, size_z, filters), jnp.float32),
            pltpu.SemaphoreType.DMA((14,)),
        ],
        compiler_params=pltpu.CompilerParams(vmem_limit_bytes=14 << 20),
        name="decode_skip",
    )(place, skip, edge, far(weights))


def decode(place, bottom, skip_part, first_weights, weights, shape):
    devices, pairs, coarse_z, _, _ = bottom.shape
    size_x, size_y, size_z = shape
    full_x, full_y = size_x + 2, size_y + 2
    channels = 64 * devices
    filters = weights.shape[-1]
    rows, extra = size_x * size_y * size_z, size_x * size_y

    def body(place_ref, bottom_ref, skip_hbm, *refs):
        near_refs, (weights_hbm, out_ref, main_ref, side_ref, sums_ref, skip_ref, weights_ref, sems) = refs[:4], refs[4:]
        copies = [
            pltpu.make_async_copy(weights_hbm.at[4 + step, :, pl.ds(0, channels)], weights_ref.at[step], sems.at[step])
            for step in range(5)
        ]
        copies.append(pltpu.make_async_copy(skip_hbm, skip_ref, sems.at[5]))
        for copy in copies:
            copy.start()
        first = place_ref[2] == 0
        planes = [[] for _ in range(2 * pairs)]
        for k in range(devices // 2):
            for pair in range(pairs):
                low, high = [bottom_ref[2 * k + i, pair].astype(jnp.float32) for i in range(2)]
                even, odd = halves(low, high)
                planes[2 * pair].append(even.reshape(coarse_z * 8, 128))
                planes[2 * pair + 1].append(odd.reshape(coarse_z * 8, 128))

        def choice(y, z, source):
            line = (y + 1) // 2 + 1
            inside = ((line > 1) | (place_ref[1] > 0)) & ((line < coarse_z) | (place_ref[1] < place_ref[4]))
            return jnp.where((source == z * 8 + line) & inside, 1.0, 0.0).astype(jnp.bfloat16)

        shape = (full_y * size_z, coarse_z * 8)
        row = lax.broadcasted_iota(jnp.int32, shape, 0)
        spread = choice(row // size_z, row % size_z // 2 + 1, lax.broadcasted_iota(jnp.int32, shape, 1))
        shape = (16, coarse_z * 8)
        row = lax.broadcasted_iota(jnp.int32, shape, 0)
        other = jnp.where(first, coarse_z - 1, 0)
        spread_edge = choice(row, other, lax.broadcasted_iota(jnp.int32, shape, 1))
        for plane in range(2 * pairs):
            coarse = jnp.concatenate(planes[plane], axis=1).astype(jnp.bfloat16)
            fine = jnp.dot(spread, coarse, preferred_element_type=jnp.float32)
            fine_edge = jnp.dot(spread_edge, coarse, preferred_element_type=jnp.float32)
            for x in range(full_x):
                if (x + 1) // 2 != plane:
                    continue
                for dy in range(3):
                    main_ref[dy, x] = fine[8 * dy : 8 * dy + size_y * size_z].astype(jnp.bfloat16)
                    side_ref[dy, x] = fine_edge[dy : dy + size_y]
        for step in range(9):
            dx, dy = step // 3, step % 3
            main = main_ref[dy, dx : dx + size_x].reshape(rows, channels)
            side = side_ref[dy, dx : dx + size_x].reshape(extra, channels).astype(jnp.bfloat16)
            block = jnp.concatenate([main, side], axis=0)
            if step >= 4:
                copies[step - 4].wait()
            for tap in range(3):
                kernel = near_refs[step][tap] if step < 4 else weights_ref[step - 4, tap]
                product = jnp.dot(block, kernel, preferred_element_type=jnp.float32)
                if step == 0:
                    sums_ref[tap] = product
                else:
                    sums_ref[tap] += product
        copies[-1].wait()
        total = join_taps(first, [sums_ref[tap] for tap in range(3)], extra, size_z) + skip_ref[...]
        out_ref[...] = total.reshape(size_x, size_y, size_z, filters).astype(out_ref.dtype)

    return pl.pallas_call(
        body,
        in_specs=[pl.BlockSpec(memory_space=pltpu.SMEM)]
        + [pl.BlockSpec(memory_space=space) for space in (pltpu.VMEM, pltpu.HBM)]
        + [pl.BlockSpec(memory_space=pltpu.VMEM)] * 4
        + [pl.BlockSpec(memory_space=pltpu.HBM)],
        out_specs=pl.BlockSpec(memory_space=pltpu.VMEM),
        out_shape=jax.ShapeDtypeStruct((size_x, size_y, size_z, filters), jnp.bfloat16),
        scratch_shapes=[
            pltpu.VMEM((3, full_x, size_y * size_z, channels), jnp.bfloat16),
            pltpu.VMEM((3, full_x, size_y, channels), jnp.float32),
            pltpu.VMEM((3, rows + extra, filters), jnp.float32),
            pltpu.VMEM((extra, size_z, filters), jnp.float32),
            pltpu.VMEM((5, 3, channels, filters), jnp.bfloat16),
            pltpu.SemaphoreType.DMA((6,)),
        ],
        compiler_params=pltpu.CompilerParams(vmem_limit_bytes=20 << 20),
        name="decode",
    )(place, bottom, far(skip_part), *map(near, first_weights), far(weights))


def solution(mesh):
    gx, gy, gz = mesh.shape["gx"], mesh.shape["gy"], mesh.shape["gz"]

    def local(volume, w_full, w_half, w_bottom_in, w_bottom_out, w_up):
        place_z = lax.axis_index("gz")
        place = jnp.stack([lax.axis_index("gx"), lax.axis_index("gy"), place_z, jnp.int32(gx - 1), jnp.int32(gy - 1)])
        swap = [(0, 1), (1, 0)]

        def edge_of(plane_low, plane_high):
            return lax.ppermute(jnp.where(place_z == 0, plane_high, plane_low), "gz", swap)

        x_in, x_out = swaps(volume[:3], volume[-3:], "gx", gx)
        turned = [w.transpose(0, 1, 2, 4, 3) for w in (w_bottom_in, w_bottom_out)]
        (w_pair, w_in, w_out), x_in, x_out = lax.optimization_barrier((prepare(w_full, *turned), x_in, x_out))
        y_inner, y_outer, plane, edge_inner, edge_outer = pack_y(place, volume, x_in, x_out)
        y_in, y_out = send(y_inner, y_outer, "gy", gy)
        edge = lax.ppermute(plane, "gz", swap)
        edge_in, edge_out = send(edge_inner, edge_outer, ("gy", "gz"), gy)
        own, w_pair = bring([volume, w_pair], plane)
        pooled = encode(place, own, x_in, x_out, y_in, y_out, edge, edge_in, edge_out, w_pair)

        edge = edge_of(pooled[:, :, 0], pooled[:, :, -1])
        skip, coarse = half_level(place, pooled, edge, w_half.reshape(9, 3, w_half.shape[3], w_half.shape[4]))
        lines = coarse.reshape(coarse.shape[0], 4, 4, coarse.shape[2])
        below, above = halo(lines, "gy", gy, 2, 1)
        column = jnp.concatenate([coarse, below[:, :, 0], above[:, :, 0]], axis=1)
        column = jnp.broadcast_to(column[None], (gx * gz,) + column.shape)
        (w_in,) = bring([w_in], column)
        column = lax.all_to_all(column, ("gx", "gz"), 0, 0)
        first = bottom_in(place, column, w_in)
        (w_out,) = bring([w_out], first)
        first = lax.all_to_all(first, "gx", 0, 0)
        around = extend(skip, "gx", gx, 0, 1)
        around = extend(around, "gy", gy, 1, 1)
        side = edge_of(around[:, :, 0], around[:, :, -1])
        first, around, side = lax.optimization_barrier((first, around, side))
        y_in, y_out = swaps(first[:, :, :, :2], first[:, :, :, -2:], "gy", gy)
        second = bottom_out(place, first, y_in, y_out, w_out)
        second = lax.all_to_all(second, "gx", 0, 0)
        w_up = w_up.reshape(9, 3, w_up.shape[3], w_up.shape[4])
        skip_part, *w_near = decode_skip(place, around, side, w_up)
        return decode(place, second, skip_part, w_near, w_up, skip.shape[:3])

    space = P("gx", "gy", "gz", None)
    filters = P(None, None, None, None, "gx")
    return jax.shard_map(
        local,
        mesh=mesh,
        in_specs=(space, P(), P(), filters, filters, P()),
        out_specs=space,
        check_vma=False,
    )
```

```python
import jax
import jax.numpy as jnp
from jax import lax
from jax.experimental import pallas as pl
from jax.experimental.pallas import tpu as pltpu
from jax.sharding import PartitionSpec as P


def send(inner_block, outer_block, axis, count):
    inner = [(i, i ^ 1) for i in range(count)]
    outer = [(i, (((i + 1) ^ 1) - 1) % count) for i in range(count)]
    if isinstance(axis, tuple):
        inner, outer = [[(2 * i + n, 2 * j + 1 - n) for i, j in pairs for n in range(2)] for pairs in (inner, outer)]
    return lax.ppermute(inner_block, axis, inner), lax.ppermute(outer_block, axis, outer)


def swaps(low, high, axis, count):
    even = lax.axis_index(axis) % 2 == 0
    return send(jnp.where(even, high, low), jnp.where(even, low, high), axis, count)


def ordered(got_in, got_out, axis):
    even = lax.axis_index(axis) % 2 == 0
    return jnp.where(even, got_out, got_in), jnp.where(even, got_in, got_out)


def halo(field, axis, count, dim, width):
    place = lax.axis_index(axis)
    size = field.shape[dim]
    low = lax.slice_in_dim(field, 0, width, axis=dim)
    high = lax.slice_in_dim(field, size - width, size, axis=dim)
    below, above = ordered(*swaps(low, high, axis, count), axis)
    zero = jnp.zeros_like(low)
    return jnp.where(place > 0, below, zero), jnp.where(place < count - 1, above, zero)


def extend(field, axis, count, dim, width):
    below, above = halo(field, axis, count, dim, width)
    return jnp.concatenate([below, field, above], axis=dim)


def half_level(place, field, edge, weights):
    full_x, full_y, size_z, channels = field.shape
    size_x, size_y = full_x - 2, full_y - 2
    filters = weights.shape[-1]
    rows, extra = size_x * size_y * size_z, size_x * size_y

    def body(place_ref, field_ref, edge_ref, weights_ref, out_ref, coarse_ref, rows_ref, coarse_rows_ref):
        first = place_ref[2] == 0
        edge_plane = edge_ref[...].astype(jnp.float32)
        blocks = []
        for dx in range(3):
            for dy in range(3):
                main = field_ref[dx : dx + size_x, dy : dy + size_y].astype(jnp.float32).reshape(rows, channels)
                side = edge_plane[dx : dx + size_x, dy : dy + size_y].reshape(extra, channels)
                blocks.append(jnp.concatenate([main, side], axis=0).astype(jnp.bfloat16))
        block = jnp.concatenate(blocks, axis=1)
        sums = []
        for tap in range(3):
            kernel = weights_ref[:, tap].reshape(9 * channels, filters)
            sums.append(jnp.dot(block, kernel, preferred_element_type=jnp.float32))
        total = jnp.maximum(join_taps(first, sums, extra, size_z), 0.0)
        out_ref[...] = total.reshape(size_x, size_y, size_z, filters).astype(out_ref.dtype)
        total = jnp.max(total.reshape(size_x // 2, 2, size_y // 2, 2, size_z, filters), axis=(1, 3))
        count = size_y // 2
        for part in range(filters // 128):
            rows_ref[...] = total[..., 128 * part : 128 * part + 128].reshape(rows // 4, 128)
            for x in range(size_x // 2):
                for z in range(size_z // 2):
                    start = x * count * size_z + 2 * z
                    pooled = jnp.maximum(
                        rows_ref[pl.ds(start, count, stride=size_z), :], rows_ref[pl.ds(start + 1, count, stride=size_z), :]
                    )
                    coarse_rows_ref[x, count * z : count * z + count, 128 * part : 128 * part + 128] = pooled
        coarse_ref[...] = coarse_rows_ref[...].astype(coarse_ref.dtype)

    return pl.pallas_call(
        body,
        in_specs=[pl.BlockSpec(memory_space=pltpu.SMEM)] + [pl.BlockSpec(memory_space=pltpu.VMEM)] * 3,
        out_specs=[pl.BlockSpec(memory_space=pltpu.VMEM)] * 2,
        out_shape=[
            jax.ShapeDtypeStruct((size_x, size_y, size_z, filters), jnp.bfloat16),
            jax.ShapeDtypeStruct((size_x // 2, size_z * size_y // 4, filters), jnp.bfloat16),
        ],
        scratch_shapes=[
            pltpu.VMEM((rows // 4, 128), jnp.float32),
            pltpu.VMEM((size_x // 2, size_z * size_y // 4, filters), jnp.float32),
        ],
        compiler_params=pltpu.CompilerParams(vmem_limit_bytes=12 << 20),
        name="half_level",
    )(place, field, edge, weights)


def join_taps(first, sums, groups, size_z):
    rows, filters = groups * size_z, sums[0].shape[-1]
    low, mid, high = [total[:rows].reshape(groups, size_z, filters) for total in sums]
    below = jnp.where(first, 0.0, sums[0][rows : rows + groups])
    above = jnp.where(first, sums[2][rows : rows + groups], 0.0)
    index = lax.broadcasted_iota(jnp.int32, (groups, size_z, filters), 1)
    down = jnp.where(index == 0, below[:, None, :], pltpu.roll(low, 1, 1))
    up = jnp.where(index == size_z - 1, above[:, None, :], pltpu.roll(high, size_z - 1, 1))
    return down + mid + up


def encode(place, own, x_in, x_out, y_in, y_out, edge, edge_in, edge_out, weights):
    own_x, own_y, size_z, channels = own.shape
    reach = x_in.shape[0]
    full_x, full_y = own_x + 2 * reach, own_y + 2 * reach
    size_x, size_y = full_x - 2, full_y - 2
    filters = weights.shape[-1] // 2
    rows, extra = size_y * size_z, size_y + (-size_y % 16)
    pool_y, pool_z = size_y // 2, size_z // 2

    def body(
        place_ref,
        own_ref,
        x_in_ref,
        x_out_ref,
        y_in_ref,
        y_out_ref,
        edge_ref,
        edge_in_ref,
        edge_out_ref,
        weights_ref,
        out_ref,
        x_ref,
        y_ref,
        side_ref,
        rows_ref,
    ):
        even_x, even_y = place_ref[0] % 2 == 0, place_ref[1] % 2 == 0
        low_x, high_x = place_ref[0] > 0, place_ref[0] < place_ref[3]
        low_y, high_y = place_ref[1] > 0, place_ref[1] < place_ref[4]
        nil = jnp.bfloat16(0)
        x_ref[0] = jnp.where(low_x, jnp.where(even_x, x_out_ref[...], x_in_ref[...]), nil)
        x_ref[1] = jnp.where(high_x, jnp.where(even_x, x_in_ref[...], x_out_ref[...]), nil)
        for x in range(full_x):
            here_low, here_high, here = low_y, high_y, None
            if x < reach:
                here_low, here_high, here = low_y & low_x, high_y & low_x, low_x
            if x >= reach + own_x:
                here_low, here_high, here = low_y & high_x, high_y & high_x, high_x
            y_ref[0, x] = jnp.where(here_low, jnp.where(even_y, y_out_ref[x], y_in_ref[x]), nil)
            y_ref[1, x] = jnp.where(here_high, jnp.where(even_y, y_in_ref[x], y_out_ref[x]), nil)
            middle = edge_ref[x].astype(jnp.float32)
            if here is not None:
                middle = jnp.where(here, middle, 0.0)
            one, other = edge_in_ref[x].astype(jnp.float32), edge_out_ref[x].astype(jnp.float32)
            below = jnp.where(here_low, jnp.where(even_y, other, one), 0.0)
            above = jnp.where(here_high, jnp.where(even_y, one, other), 0.0)
            for dy in range(3):
                if dy < reach:
                    side_ref[dy, x, : reach - dy] = below[dy:]
                side_ref[dy, x, reach - dy : reach - dy + own_y] = middle
                side_ref[dy, x, reach - dy + own_y : size_y] = above[: dy + 1]
                side_ref[dy, x, size_y:] = jnp.zeros((extra - size_y, channels), jnp.float32)

        def lines(x, dy):
            if x < reach:
                middle = x_ref[0, x]
            elif x < reach + own_x:
                middle = own_ref[x - reach]
            else:
                middle = x_ref[1, x - reach - own_x]
            block = jnp.concatenate([y_ref[0, x, dy:], middle, y_ref[1, x, : dy + 1]], axis=0)
            return block.reshape(rows, channels)

        first = place_ref[2] == 0
        line = lax.broadcasted_iota(jnp.int32, (pool_y, pool_z, filters), 0)
        inside_y = ((line > 0) | low_y) & ((line < pool_y - 1) | high_y)
        for pair in range(size_x // 2):
            blocks = []
            for plane in range(4):
                for dy in range(3):
                    main = lines(2 * pair + plane, dy)
                    side = side_ref[dy, 2 * pair + plane].astype(jnp.bfloat16)
                    blocks.append(jnp.concatenate([main, side], axis=0))
            block = jnp.concatenate(blocks, axis=1)
            sums = []
            for tap in range(3):
                kernel = weights_ref[tap].reshape(12 * channels, 2 * filters)
                sums.append(jnp.dot(block, kernel, preferred_element_type=jnp.float32))
            total = jnp.maximum(join_taps(first, sums, size_y, size_z), 0.0)
            total = jnp.maximum(total[..., :filters], total[..., filters:])
            total = jnp.max(total.reshape(pool_y, 2, size_z, filters), axis=1)
            rows_ref[...] = total.reshape(pool_y * size_z, filters)
            total = jnp.maximum(
                rows_ref[pl.ds(0, pool_y * pool_z, stride=2), :], rows_ref[pl.ds(1, pool_y * pool_z, stride=2), :]
            ).reshape(pool_y, pool_z, filters)
            inside = inside_y
            if pair == 0:
                inside = inside & low_x
            if pair == size_x // 2 - 1:
                inside = inside & high_x
            out_ref[pair] = jnp.where(inside, total, 0.0).astype(out_ref.dtype)

    return pl.pallas_call(
        body,
        in_specs=[pl.BlockSpec(memory_space=pltpu.SMEM)] + [pl.BlockSpec(memory_space=pltpu.VMEM)] * 9,
        out_specs=pl.BlockSpec(memory_space=pltpu.VMEM),
        out_shape=jax.ShapeDtypeStruct((size_x // 2, pool_y, pool_z, filters), jnp.bfloat16),
        scratch_shapes=[
            pltpu.VMEM((2, reach, own_y, size_z, channels), jnp.bfloat16),
            pltpu.VMEM((2, full_x, reach, size_z, channels), jnp.bfloat16),
            pltpu.VMEM((3, full_x, extra, channels), jnp.float32),
            pltpu.VMEM((pool_y * size_z, filters), jnp.float32),
        ],
        compiler_params=pltpu.CompilerParams(vmem_limit_bytes=14 << 20),
        name="encode",
    )(place, near(own), x_in, x_out, y_in, y_out, edge, edge_in, edge_out, near(weights))


def near(array):
    return pltpu.with_memory_space_constraint(array, pltpu.VMEM)


def bring(arrays, after):
    pieces = [(i, n) for i, array in enumerate(arrays) for n in range(array.shape[0])]
    count = len(arrays)

    def body(*refs):
        hbms, outs, sems = refs[:count], refs[count + 1 : -1], refs[-1]
        copies = [pltpu.make_async_copy(hbms[i].at[n], outs[i].at[n], sems.at[k]) for k, (i, n) in enumerate(pieces)]
        for copy in copies:
            copy.start()
        for copy in copies:
            copy.wait()

    return pl.pallas_call(
        body,
        in_specs=[pl.BlockSpec(memory_space=pltpu.HBM)] * count + [pl.BlockSpec(memory_space=pl.ANY)],
        out_specs=[pl.BlockSpec(memory_space=pltpu.VMEM)] * count,
        out_shape=[pltpu.VMEM(array.shape, array.dtype) for array in arrays],
        scratch_shapes=[pltpu.SemaphoreType.DMA((len(pieces),))],
        compiler_params=pltpu.CompilerParams(vmem_limit_bytes=4 << 20),
        name="bring",
    )(*map(far, arrays), after)


def far(array):
    return pltpu.with_memory_space_constraint(array, pltpu.HBM)


def prepare(w_full, w_in, w_out):
    channels, filters = w_full.shape[3:]
    depths = [w.shape[4] for w in (w_in, w_out)]

    def body(
        full_hbm, in_hbm, out_hbm, pair_hbm, to_in_hbm, to_out_hbm, full_ref, pair_ref, in_ref, out_ref, to_in_ref, to_out_ref, sems
    ):
        first = pltpu.make_async_copy(full_hbm, full_ref, sems.at[0])
        first.start()
        jobs = []
        for order, (hbm, ref) in enumerate(((in_hbm, in_ref), (out_hbm, out_ref))):
            copies = []
            for step in range(9):
                for dy in range(3):
                    to = ref.at[step, pl.ds(64 * dy, 64)]
                    sem = sems.at[1 + 27 * order + 3 * step + dy]
                    copies.append(pltpu.make_async_copy(hbm.at[step // 3, dy, step % 3], to, sem))
                    copies[-1].start()
            jobs.append(copies)
        first.wait()
        zero = jnp.zeros((3, channels, filters), jnp.bfloat16)
        results = []
        for tap in range(3):
            for plane in range(4):
                pair_ref[tap, plane, :, :, :filters] = full_ref[plane, :, tap] if plane < 3 else zero
                pair_ref[tap, plane, :, :, filters:] = full_ref[plane - 1, :, tap] if plane > 0 else zero
            results.append(pltpu.make_async_copy(pair_ref.at[tap], pair_hbm.at[tap], sems.at[55 + tap]))
            results[-1].start()
        for order, (ref, to_ref, to_hbm) in enumerate(((in_ref, to_in_ref, to_in_hbm), (out_ref, to_out_ref, to_out_hbm))):
            for step in range(9):
                ref[step, 192:] = jnp.zeros((64, depths[order]), jnp.bfloat16)
                for copy in jobs[order][3 * step : 3 * step + 3]:
                    copy.wait()
                to_ref[step] = ref[step].T
                results.append(pltpu.make_async_copy(to_ref.at[step], to_hbm.at[step], sems.at[59 + 9 * order + step]))
                results[-1].start()
        for copy in results:
            copy.wait()

    shapes = [(3, 4, 3, channels, 2 * filters)] + [(9, depth, 256) for depth in depths]
    return pl.pallas_call(
        body,
        in_specs=[pl.BlockSpec(memory_space=pltpu.HBM)] * 3,
        out_specs=[pl.BlockSpec(memory_space=pltpu.HBM)] * 3,
        out_shape=[pltpu.HBM(shape, jnp.bfloat16) for shape in shapes],
        scratch_shapes=[pltpu.VMEM(w_full.shape, jnp.bfloat16), pltpu.VMEM(shapes[0], jnp.bfloat16)]
        + [pltpu.VMEM((9, 256, depth), jnp.bfloat16) for depth in depths]
        + [pltpu.VMEM((9, depth, 256), jnp.bfloat16) for depth in depths]
        + [pltpu.SemaphoreType.DMA((77,))],
        compiler_params=pltpu.CompilerParams(vmem_limit_bytes=20 << 20),
        name="prepare",
    )(far(w_full), far(w_in), far(w_out))


def pack_y(place, own, x_in, x_out):
    own_x, own_y, size_z, channels = own.shape
    reach = x_in.shape[0]
    full_x = own_x + 2 * reach

    def body(place_ref, own_ref, x_in_ref, x_out_ref, inner_ref, outer_ref, plane_ref, inner_edge_ref, outer_edge_ref, rows_ref):
        even_x, even_y, first = place_ref[0] % 2 == 0, place_ref[1] % 2 == 0, place_ref[2] == 0
        below = jnp.where(even_x, x_out_ref[...], x_in_ref[...])
        above = jnp.where(even_x, x_in_ref[...], x_out_ref[...])
        for start, block in ((0, below), (reach, own_ref[...]), (reach + own_x, above)):
            size = block.shape[0]
            low, high = block[:, :reach], block[:, own_y - reach :]
            inner_ref[start : start + size] = jnp.where(even_y, high, low)
            outer_ref[start : start + size] = jnp.where(even_y, low, high)
            block = block.astype(jnp.float32)
            edge = jnp.where(first, block[:, :, size_z - 1 :], block[:, :, :1])
            for x in range(size):
                for y in range(own_y):
                    rows_ref[start + x, y : y + 1] = edge[x, y]
        plane_ref[...] = rows_ref[...].astype(plane_ref.dtype)
        low, high = rows_ref[:, :reach], rows_ref[:, own_y - reach :]
        inner_edge_ref[...] = jnp.where(even_y, high, low).astype(plane_ref.dtype)
        outer_edge_ref[...] = jnp.where(even_y, low, high).astype(plane_ref.dtype)

    return pl.pallas_call(
        body,
        in_specs=[pl.BlockSpec(memory_space=pltpu.SMEM)] + [pl.BlockSpec(memory_space=pltpu.VMEM)] * 3,
        out_specs=[pl.BlockSpec(memory_space=pltpu.VMEM)] * 5,
        out_shape=[jax.ShapeDtypeStruct((full_x, reach, size_z, channels), jnp.bfloat16)] * 2
        + [jax.ShapeDtypeStruct((full_x, rows, channels), jnp.bfloat16) for rows in (own_y, reach, reach)],
        scratch_shapes=[pltpu.VMEM((full_x, own_y, channels), jnp.float32)],
        compiler_params=pltpu.CompilerParams(vmem_limit_bytes=8 << 20),
        name="pack_y",
    )(place, own, x_in, x_out)


def halves(pair_low, pair_high):
    lane = lax.broadcasted_iota(jnp.int32, pair_low.shape, pair_low.ndim - 1)
    axis = pair_low.ndim - 1
    even = jnp.where(lane < 64, pair_low, pltpu.roll(pair_high, 64, axis))
    odd = jnp.where(lane < 64, pltpu.roll(pair_low, 64, axis), pair_high)
    return even, odd


def side_by_side(even, odd):
    lane = lax.broadcasted_iota(jnp.int32, even.shape, even.ndim - 1)
    return jnp.where(lane < 64, even, pltpu.roll(odd, 64, even.ndim - 1))


def pair_planes(pad_ref, pair_ref):
    pairs = pair_ref.shape[1]
    for odd in range(2):
        for pair in range(pairs - odd):
            planes = [pad_ref[2 * pair + odd + n] for n in range(2)]
            pair_ref[odd, pair] = jnp.concatenate(planes, axis=1).astype(pair_ref.dtype)


def column_product(pair_ref, weights_ref, first, start, pairs, size_z):
    channels = pair_ref.shape[-1]
    rows = pairs * size_z * 16
    blocks = []
    for dx in range(3):
        for dz in range(3):
            block = pair_ref[dx % 2, first + dx // 2 : first + dx // 2 + pairs, pl.ds(start + dz, size_z)]
            blocks.append(block.reshape(rows, channels))
    block = jnp.concatenate(blocks, axis=1)
    total = jnp.dot(block, weights_ref[...].reshape(9 * channels, 256), preferred_element_type=jnp.float32)
    groups = pairs * size_z * 2
    low = total[:, :128].reshape(groups, 8, 128)
    mid = pltpu.roll(total[:, :128], 64, 1).reshape(groups, 8, 128)
    high = total[:, 128:].reshape(groups, 8, 128)
    total = pltpu.roll(low, 1, 1) + mid + pltpu.roll(high, 7, 1)
    return jnp.maximum(total, 0.0).reshape(pairs, size_z, 2, 8, 128)


def bottom_in(place, field, weights):
    count, own_x, lines, channels = field.shape
    devices = count // 2
    own_z = size_y = 4
    size_x, all_z, size_z = devices * own_x, 2 * own_z, own_z + 2

    def body(place_ref, field_ref, weights_ref, out_ref, pad_ref, pair_ref):
        zero = jnp.zeros((all_z + 2, 8, channels), jnp.float32)
        pad_ref[0] = zero
        pad_ref[size_x + 1] = zero
        for x in range(size_x):
            pad_ref[x + 1, 0] = zero[0]
            pad_ref[x + 1, all_z + 1] = zero[0]
        for i in range(devices):
            for half in range(2):
                for x in range(own_x):
                    block = field_ref[2 * i + half, x].astype(jnp.float32)
                    for z in range(own_z):
                        to = (1 + own_x * i + x, 1 + own_z * half + z)
                        pad_ref[*to, 0:1] = block[own_z * size_y + z : own_z * size_y + z + 1]
                        pad_ref[*to, 1 : size_y + 1] = block[size_y * z : size_y * z + size_y]
                        line = own_z * (size_y + 1) + z
                        pad_ref[*to, size_y + 1 : size_y + 2] = block[line : line + 1]
                        pad_ref[*to, size_y + 2 :] = zero[0, size_y + 2 :]
        start = 2 * place_ref[2]
        pair_planes(pad_ref, pair_ref)
        for first in range(0, size_x // 2, 2):
            total = column_product(pair_ref, weights_ref, first, start, 2, size_z)
            for pair in range(2):
                both = side_by_side(total[pair, :, 0], total[pair, :, 1])[:, 1 : size_y + 1].astype(out_ref.dtype)
                for i in range(devices):
                    out_ref[i, first + pair] = both

    return pl.pallas_call(
        body,
        in_specs=[pl.BlockSpec(memory_space=space) for space in (pltpu.SMEM, pltpu.VMEM, pltpu.VMEM)],
        out_specs=pl.BlockSpec(memory_space=pltpu.VMEM),
        out_shape=jax.ShapeDtypeStruct((devices, size_x // 2, size_z, size_y, 128), jnp.bfloat16),
        scratch_shapes=[
            pltpu.VMEM((size_x + 2, all_z + 2, 8, channels), jnp.float32),
            pltpu.VMEM((2, size_x // 2 + 1, all_z + 2, 16, channels), jnp.bfloat16),
        ],
        compiler_params=pltpu.CompilerParams(vmem_limit_bytes=16 << 20),
        name="bottom_in",
    )(place, field, near(weights))


def bottom_out(place, field, y_in, y_out, weights):
    devices, pairs, size_z, _, _ = field.shape
    size_x, channels = 2 * pairs, 64 * devices
    own_x = size_x // devices

    def body(place_ref, field_ref, y_in_ref, y_out_ref, weights_ref, out_ref, pad_ref, pair_ref, total_ref):
        even_y = place_ref[1] % 2 == 0
        low_y, high_y = place_ref[1] > 0, place_ref[1] < place_ref[4]
        zero = jnp.zeros((size_z + 2, 8, channels), jnp.float32)
        for ref in (pad_ref, total_ref):
            wide = ref.shape[-1]
            ref[0] = zero[..., :wide]
            ref[size_x + 1] = zero[..., :wide]
            for x in range(size_x):
                ref[x + 1, 0] = zero[0, :, :wide]
                ref[x + 1, size_z + 1] = zero[0, :, :wide]
        for k in range(devices // 2):
            for pair in range(pairs):
                y_first, y_last = [], []
                for i in range(2):
                    one = y_in_ref[2 * k + i, pair].astype(jnp.float32)
                    other = y_out_ref[2 * k + i, pair].astype(jnp.float32)
                    y_first.append(jnp.where(low_y, jnp.where(even_y, other, one), 0.0))
                    y_last.append(jnp.where(high_y, jnp.where(even_y, one, other), 0.0))
                own = [field_ref[2 * k + i, pair].astype(jnp.float32) for i in range(2)]
                for line, blocks in ((0, y_first), (2, own), (6, y_last)):
                    even, odd = halves(*blocks)
                    lines = slice(line, line + even.shape[1])
                    pad_ref[1 + 2 * pair, 1 : size_z + 1, lines, 128 * k : 128 * k + 128] = even
                    pad_ref[2 + 2 * pair, 1 : size_z + 1, lines, 128 * k : 128 * k + 128] = odd
        pair_planes(pad_ref, pair_ref)
        for first in range(0, pairs, 2):
            total = column_product(pair_ref, weights_ref, first, 0, 2, size_z)
            for plane in range(4):
                total_ref[1 + 2 * first + plane, 1 : size_z + 1] = total[plane // 2, :, plane % 2]
        start = 2 * place_ref[2]
        for i in range(size_x // 2 + 1):
            low, high = [total_ref[2 * i + n, pl.ds(start, size_z)] for n in range(2)]
            both = side_by_side(low, high).astype(out_ref.dtype)
            if i < devices:
                out_ref[i, 0] = both
            if i > 0:
                out_ref[i - 1, 1] = both

    return pl.pallas_call(
        body,
        in_specs=[pl.BlockSpec(memory_space=pltpu.SMEM)]
        + [pl.BlockSpec(memory_space=pltpu.VMEM)] * 4,
        out_specs=pl.BlockSpec(memory_space=pltpu.VMEM),
        out_shape=jax.ShapeDtypeStruct((devices, own_x, size_z, 8, 128), jnp.bfloat16),
        scratch_shapes=[
            pltpu.VMEM((size_x + 2, size_z + 2, 8, channels), jnp.float32),
            pltpu.VMEM((2, pairs + 1, size_z + 2, 16, channels), jnp.bfloat16),
            pltpu.VMEM((size_x + 2, size_z + 2, 8, 128), jnp.float32),
        ],
        compiler_params=pltpu.CompilerParams(vmem_limit_bytes=20 << 20),
        name="bottom_out",
    )(place, field, y_in, y_out, near(weights))


def decode_skip(place, skip, edge, weights):
    full_x, full_y, size_z, channels = skip.shape
    size_x, size_y = full_x - 2, full_y - 2
    filters = weights.shape[-1]
    deep = weights.shape[2] - channels
    rows, extra = size_x * size_y * size_z, size_x * size_y

    def body(place_ref, skip_ref, edge_ref, weights_hbm, out_hbm, *refs):
        rest_refs, (weights_ref, out_ref, sems) = refs[:4], refs[4:]
        copies = [
            pltpu.make_async_copy(weights_hbm.at[step, :, pl.ds(deep, channels)], weights_ref.at[step], sems.at[step])
            for step in range(9)
        ]
        rest = [
            pltpu.make_async_copy(weights_hbm.at[step, :, pl.ds(0, deep)], rest_refs[step], sems.at[9 + step])
            for step in range(4)
        ]
        for copy in copies + rest:
            copy.start()
        edge_plane = edge_ref[...].astype(jnp.float32)
        blocks = []
        for dx in range(3):
            for dy in range(3):
                main = skip_ref[dx : dx + size_x, dy : dy + size_y].astype(jnp.float32).reshape(rows, channels)
                side = edge_plane[dx : dx + size_x, dy : dy + size_y].reshape(extra, channels)
                blocks.append(jnp.concatenate([main, side], axis=0).astype(jnp.bfloat16))
        for copy in copies:
            copy.wait()
        block = jnp.concatenate(blocks, axis=1)
        sums = []
        for tap in range(3):
            kernel = weights_ref[:, tap].reshape(9 * channels, filters)
            sums.append(jnp.dot(block, kernel, preferred_element_type=jnp.float32))
        out_ref[...] = join_taps(place_ref[2] == 0, sums, extra, size_z)
        rest.append(pltpu.make_async_copy(out_ref, out_hbm, sems.at[13]))
        rest[-1].start()
        for copy in rest:
            copy.wait()

    return pl.pallas_call(
        body,
        in_specs=[pl.BlockSpec(memory_space=pltpu.SMEM)]
        + [pl.BlockSpec(memory_space=pltpu.VMEM)] * 2
        + [pl.BlockSpec(memory_space=pltpu.HBM)],
        out_specs=[pl.BlockSpec(memory_space=pltpu.HBM)] + [pl.BlockSpec(memory_space=pltpu.VMEM)] * 4,
        out_shape=[
            pltpu.HBM((extra, size_z, filters), jnp.float32),
        ]
        + [pltpu.VMEM((3, deep, filters), jnp.bfloat16)] * 4,
        scratch_shapes=[
            pltpu.VMEM((9, 3, channels, filters), jnp.bfloat16),
            pltpu.VMEM((extra, size_z, filters), jnp.float32),
            pltpu.SemaphoreType.DMA((14,)),
        ],
        compiler_params=pltpu.CompilerParams(vmem_limit_bytes=14 << 20),
        name="decode_skip",
    )(place, skip, edge, far(weights))


def decode(place, bottom, skip_part, first_weights, weights, shape):
    devices, pairs, coarse_z, _, _ = bottom.shape
    size_x, size_y, size_z = shape
    full_x, full_y = size_x + 2, size_y + 2
    channels = 64 * devices
    filters = weights.shape[-1]
    rows, extra = size_x * size_y * size_z, size_x * size_y

    def body(place_ref, bottom_ref, skip_hbm, *refs):
        near_refs, (weights_hbm, out_ref, main_ref, side_ref, sums_ref, skip_ref, weights_ref, sems) = refs[:4], refs[4:]
        copies = [
            pltpu.make_async_copy(weights_hbm.at[4 + step, :, pl.ds(0, channels)], weights_ref.at[step], sems.at[step])
            for step in range(5)
        ]
        copies.append(pltpu.make_async_copy(skip_hbm, skip_ref, sems.at[5]))
        for copy in copies:
            copy.start()
        first = place_ref[2] == 0
        planes = [[] for _ in range(2 * pairs)]
        for k in range(devices // 2):
            for pair in range(pairs):
                low, high = [bottom_ref[2 * k + i, pair].astype(jnp.float32) for i in range(2)]
                even, odd = halves(low, high)
                planes[2 * pair].append(even.reshape(coarse_z * 8, 128))
                planes[2 * pair + 1].append(odd.reshape(coarse_z * 8, 128))

        def choice(y, z, source):
            line = (y + 1) // 2 + 1
            inside = ((line > 1) | (place_ref[1] > 0)) & ((line < coarse_z) | (place_ref[1] < place_ref[4]))
            return jnp.where((source == z * 8 + line) & inside, 1.0, 0.0).astype(jnp.bfloat16)

        shape = (full_y * size_z, coarse_z * 8)
        row = lax.broadcasted_iota(jnp.int32, shape, 0)
        spread = choice(row // size_z, row % size_z // 2 + 1, lax.broadcasted_iota(jnp.int32, shape, 1))
        shape = (16, coarse_z * 8)
        row = lax.broadcasted_iota(jnp.int32, shape, 0)
        other = jnp.where(first, coarse_z - 1, 0)
        spread_edge = choice(row, other, lax.broadcasted_iota(jnp.int32, shape, 1))
        for plane in range(2 * pairs):
            coarse = jnp.concatenate(planes[plane], axis=1).astype(jnp.bfloat16)
            fine = jnp.dot(spread, coarse, preferred_element_type=jnp.float32)
            fine_edge = jnp.dot(spread_edge, coarse, preferred_element_type=jnp.float32)
            for x in range(full_x):
                if (x + 1) // 2 != plane:
                    continue
                for dy in range(3):
                    main_ref[dy, x] = fine[8 * dy : 8 * dy + size_y * size_z].astype(jnp.bfloat16)
                    side_ref[dy, x] = fine_edge[dy : dy + size_y]
        for step in range(9):
            dx, dy = step // 3, step % 3
            main = main_ref[dy, dx : dx + size_x].reshape(rows, channels)
            side = side_ref[dy, dx : dx + size_x].reshape(extra, channels).astype(jnp.bfloat16)
            block = jnp.concatenate([main, side], axis=0)
            if step >= 4:
                copies[step - 4].wait()
            for tap in range(3):
                kernel = near_refs[step][tap] if step < 4 else weights_ref[step - 4, tap]
                product = jnp.dot(block, kernel, preferred_element_type=jnp.float32)
                if step == 0:
                    sums_ref[tap] = product
                else:
                    sums_ref[tap] += product
        copies[-1].wait()
        total = join_taps(first, [sums_ref[tap] for tap in range(3)], extra, size_z) + skip_ref[...]
        out_ref[...] = total.reshape(size_x, size_y, size_z, filters).astype(out_ref.dtype)

    return pl.pallas_call(
        body,
        in_specs=[pl.BlockSpec(memory_space=pltpu.SMEM)]
        + [pl.BlockSpec(memory_space=space) for space in (pltpu.VMEM, pltpu.HBM)]
        + [pl.BlockSpec(memory_space=pltpu.VMEM)] * 4
        + [pl.BlockSpec(memory_space=pltpu.HBM)],
        out_specs=pl.BlockSpec(memory_space=pltpu.VMEM),
        out_shape=jax.ShapeDtypeStruct((size_x, size_y, size_z, filters), jnp.bfloat16),
        scratch_shapes=[
            pltpu.VMEM((3, full_x, size_y * size_z, channels), jnp.bfloat16),
            pltpu.VMEM((3, full_x, size_y, channels), jnp.float32),
            pltpu.VMEM((3, rows + extra, filters), jnp.float32),
            pltpu.VMEM((extra, size_z, filters), jnp.float32),
            pltpu.VMEM((5, 3, channels, filters), jnp.bfloat16),
            pltpu.SemaphoreType.DMA((6,)),
        ],
        compiler_params=pltpu.CompilerParams(vmem_limit_bytes=20 << 20),
        name="decode",
    )(place, bottom, far(skip_part), *map(near, first_weights), far(weights))


def solution(mesh):
    gx, gy, gz = mesh.shape["gx"], mesh.shape["gy"], mesh.shape["gz"]

    def local(volume, w_full, w_half, w_bottom_in, w_bottom_out, w_up):
        place_z = lax.axis_index("gz")
        place = jnp.stack([lax.axis_index("gx"), lax.axis_index("gy"), place_z, jnp.int32(gx - 1), jnp.int32(gy - 1)])
        swap = [(0, 1), (1, 0)]

        def edge_of(plane_low, plane_high):
            return lax.ppermute(jnp.where(place_z == 0, plane_high, plane_low), "gz", swap)

        x_in, x_out = swaps(volume[:3], volume[-3:], "gx", gx)
        turned = [w.transpose(0, 1, 2, 4, 3) for w in (w_bottom_in, w_bottom_out)]
        (w_pair, w_in, w_out), x_in, x_out = lax.optimization_barrier((prepare(w_full, *turned), x_in, x_out))
        y_inner, y_outer, plane, edge_inner, edge_outer = pack_y(place, volume, x_in, x_out)
        y_in, y_out = send(y_inner, y_outer, "gy", gy)
        edge = lax.ppermute(plane, "gz", swap)
        edge_in, edge_out = send(edge_inner, edge_outer, ("gy", "gz"), gy)
        own, w_pair = bring([volume, w_pair], plane)
        pooled = encode(place, own, x_in, x_out, y_in, y_out, edge, edge_in, edge_out, w_pair)

        edge = edge_of(pooled[:, :, 0], pooled[:, :, -1])
        skip, coarse = half_level(place, pooled, edge, w_half.reshape(9, 3, w_half.shape[3], w_half.shape[4]))
        lines = coarse.reshape(coarse.shape[0], 4, 4, coarse.shape[2])
        below, above = halo(lines, "gy", gy, 2, 1)
        column = jnp.concatenate([coarse, below[:, :, 0], above[:, :, 0]], axis=1)
        column = jnp.broadcast_to(column[None], (gx * gz,) + column.shape)
        (w_in,) = bring([w_in], column)
        column = lax.all_to_all(column, ("gx", "gz"), 0, 0)
        first = bottom_in(place, column, w_in)
        (w_out,) = bring([w_out], first)
        first = lax.all_to_all(first, "gx", 0, 0)
        around = extend(skip, "gx", gx, 0, 1)
        around = extend(around, "gy", gy, 1, 1)
        side = edge_of(around[:, :, 0], around[:, :, -1])
        first, around, side = lax.optimization_barrier((first, around, side))
        y_in, y_out = swaps(first[:, :, :, :2], first[:, :, :, -2:], "gy", gy)
        second = bottom_out(place, first, y_in, y_out, w_out)
        second = lax.all_to_all(second, "gx", 0, 0)
        w_up = w_up.reshape(9, 3, w_up.shape[3], w_up.shape[4])
        skip_part, *w_near = decode_skip(place, around, side, w_up)
        return decode(place, second, skip_part, w_near, w_up, skip.shape[:3])

    space = P("gx", "gy", "gz", None)
    filters = P(None, None, None, None, "gx")
    return jax.shard_map(
        local,
        mesh=mesh,
        in_specs=(space, P(), P(), filters, filters, P()),
        out_specs=space,
        check_vma=False,
    )
```

```python
import jax
import jax.numpy as jnp
from jax import lax
from jax.experimental import pallas as pl
from jax.experimental.pallas import tpu as pltpu
from jax.sharding import PartitionSpec as P


def send(inner_block, outer_block, axis, count):
    inner = [(i, i ^ 1) for i in range(count)]
    outer = [(i, (((i + 1) ^ 1) - 1) % count) for i in range(count)]
    if isinstance(axis, tuple):
        inner, outer = [[(2 * i + n, 2 * j + 1 - n) for i, j in pairs for n in range(2)] for pairs in (inner, outer)]
    return lax.ppermute(inner_block, axis, inner), lax.ppermute(outer_block, axis, outer)


def swaps(low, high, axis, count):
    even = lax.axis_index(axis) % 2 == 0
    return send(jnp.where(even, high, low), jnp.where(even, low, high), axis, count)


def ordered(got_in, got_out, axis):
    even = lax.axis_index(axis) % 2 == 0
    return jnp.where(even, got_out, got_in), jnp.where(even, got_in, got_out)


def halo(field, axis, count, dim, width):
    place = lax.axis_index(axis)
    size = field.shape[dim]
    low = lax.slice_in_dim(field, 0, width, axis=dim)
    high = lax.slice_in_dim(field, size - width, size, axis=dim)
    below, above = ordered(*swaps(low, high, axis, count), axis)
    zero = jnp.zeros_like(low)
    return jnp.where(place > 0, below, zero), jnp.where(place < count - 1, above, zero)


def extend(field, axis, count, dim, width):
    below, above = halo(field, axis, count, dim, width)
    return jnp.concatenate([below, field, above], axis=dim)


def half_level(place, field, edge, weights):
    full_x, full_y, size_z, channels = field.shape
    size_x, size_y = full_x - 2, full_y - 2
    filters = weights.shape[-1]
    rows, extra = size_x * size_y * size_z, size_x * size_y

    def body(place_ref, field_ref, edge_ref, weights_ref, out_ref, coarse_ref, rows_ref, coarse_rows_ref):
        first = place_ref[2] == 0
        edge_plane = edge_ref[...].astype(jnp.float32)
        blocks = []
        for dx in range(3):
            for dy in range(3):
                main = field_ref[dx : dx + size_x, dy : dy + size_y].astype(jnp.float32).reshape(rows, channels)
                side = edge_plane[dx : dx + size_x, dy : dy + size_y].reshape(extra, channels)
                blocks.append(jnp.concatenate([main, side], axis=0).astype(jnp.bfloat16))
        block = jnp.concatenate(blocks, axis=1)
        sums = []
        for tap in range(3):
            kernel = weights_ref[:, tap].reshape(9 * channels, filters)
            sums.append(jnp.dot(block, kernel, preferred_element_type=jnp.float32))
        total = jnp.maximum(join_taps(first, sums, extra, size_z), 0.0)
        out_ref[...] = total.reshape(size_x, size_y, size_z, filters).astype(out_ref.dtype)
        total = jnp.max(total.reshape(size_x // 2, 2, size_y // 2, 2, size_z, filters), axis=(1, 3))
        count = size_y // 2
        for part in range(filters // 128):
            rows_ref[: rows // 4] = total[..., 128 * part : 128 * part + 128].reshape(rows // 4, 128)
            for x in range(size_x // 2):
                for z in range(size_z // 2):
                    start = x * count * size_z + 2 * z
                    pooled = jnp.maximum(
                        rows_ref[pl.ds(start, count, stride=size_z), :], rows_ref[pl.ds(start + 1, count, stride=size_z), :]
                    )
                    coarse_rows_ref[x, count * z : count * z + count, 128 * part : 128 * part + 128] = pooled
        coarse_ref[...] = coarse_rows_ref[...].astype(coarse_ref.dtype)

    return pl.pallas_call(
        body,
        in_specs=[pl.BlockSpec(memory_space=pltpu.SMEM)] + [pl.BlockSpec(memory_space=pltpu.VMEM)] * 3,
        out_specs=[pl.BlockSpec(memory_space=pltpu.VMEM)] * 2,
        out_shape=[
            jax.ShapeDtypeStruct((size_x, size_y, size_z, filters), jnp.bfloat16),
            jax.ShapeDtypeStruct((size_x // 2, size_z * size_y // 4, filters), jnp.bfloat16),
        ],
        scratch_shapes=[
            pltpu.VMEM((rows // 4 + 16, 128), jnp.float32),
            pltpu.VMEM((size_x // 2, size_z * size_y // 4, filters), jnp.float32),
        ],
        compiler_params=pltpu.CompilerParams(vmem_limit_bytes=12 << 20),
        name="half_level",
    )(place, field, edge, weights)


def join_taps(first, sums, groups, size_z):
    rows, filters = groups * size_z, sums[0].shape[-1]
    low, mid, high = [total[:rows].reshape(groups, size_z, filters) for total in sums]
    below = jnp.where(first, 0.0, sums[0][rows : rows + groups])
    above = jnp.where(first, sums[2][rows : rows + groups], 0.0)
    index = lax.broadcasted_iota(jnp.int32, (groups, size_z, filters), 1)
    down = jnp.where(index == 0, below[:, None, :], pltpu.roll(low, 1, 1))
    up = jnp.where(index == size_z - 1, above[:, None, :], pltpu.roll(high, size_z - 1, 1))
    return down + mid + up


def encode(place, own, x_in, x_out, y_in, y_out, edge, edge_in, edge_out, weights):
    own_x, own_y, size_z, channels = own.shape
    reach = x_in.shape[0]
    full_x, full_y = own_x + 2 * reach, own_y + 2 * reach
    size_x, size_y = full_x - 2, full_y - 2
    filters = weights.shape[-1] // 2
    rows, extra = size_y * size_z, size_y + (-size_y % 16)
    pool_y, pool_z = size_y // 2, size_z // 2

    def body(
        place_ref,
        own_ref,
        x_in_ref,
        x_out_ref,
        y_in_ref,
        y_out_ref,
        edge_ref,
        edge_in_ref,
        edge_out_ref,
        weights_ref,
        out_ref,
        x_ref,
        y_ref,
        side_ref,
        rows_ref,
    ):
        even_x, even_y = place_ref[0] % 2 == 0, place_ref[1] % 2 == 0
        low_x, high_x = place_ref[0] > 0, place_ref[0] < place_ref[3]
        low_y, high_y = place_ref[1] > 0, place_ref[1] < place_ref[4]
        nil = jnp.bfloat16(0)
        x_ref[0] = jnp.where(low_x, jnp.where(even_x, x_out_ref[...], x_in_ref[...]), nil)
        x_ref[1] = jnp.where(high_x, jnp.where(even_x, x_in_ref[...], x_out_ref[...]), nil)
        for x in range(full_x):
            here_low, here_high, here = low_y, high_y, None
            if x < reach:
                here_low, here_high, here = low_y & low_x, high_y & low_x, low_x
            if x >= reach + own_x:
                here_low, here_high, here = low_y & high_x, high_y & high_x, high_x
            y_ref[0, x] = jnp.where(here_low, jnp.where(even_y, y_out_ref[x], y_in_ref[x]), nil)
            y_ref[1, x] = jnp.where(here_high, jnp.where(even_y, y_in_ref[x], y_out_ref[x]), nil)
            middle = edge_ref[x].astype(jnp.float32)
            if here is not None:
                middle = jnp.where(here, middle, 0.0)
            one, other = edge_in_ref[x].astype(jnp.float32), edge_out_ref[x].astype(jnp.float32)
            below = jnp.where(here_low, jnp.where(even_y, other, one), 0.0)
            above = jnp.where(here_high, jnp.where(even_y, one, other), 0.0)
            for dy in range(3):
                if dy < reach:
                    side_ref[dy, x, : reach - dy] = below[dy:]
                side_ref[dy, x, reach - dy : reach - dy + own_y] = middle
                side_ref[dy, x, reach - dy + own_y : size_y] = above[: dy + 1]
                side_ref[dy, x, size_y:] = jnp.zeros((extra - size_y, channels), jnp.float32)

        def lines(x, dy):
            if x < reach:
                middle = x_ref[0, x]
            elif x < reach + own_x:
                middle = own_ref[x - reach]
            else:
                middle = x_ref[1, x - reach - own_x]
            block = jnp.concatenate([y_ref[0, x, dy:], middle, y_ref[1, x, : dy + 1]], axis=0)
            return block.reshape(rows, channels)

        first = place_ref[2] == 0
        line = lax.broadcasted_iota(jnp.int32, (pool_y, pool_z, filters), 0)
        inside_y = ((line > 0) | low_y) & ((line < pool_y - 1) | high_y)
        for pair in range(size_x // 2):
            blocks = []
            for plane in range(4):
                for dy in range(3):
                    main = lines(2 * pair + plane, dy)
                    side = side_ref[dy, 2 * pair + plane].astype(jnp.bfloat16)
                    blocks.append(jnp.concatenate([main, side], axis=0))
            block = jnp.concatenate(blocks, axis=1)
            sums = []
            for tap in range(3):
                kernel = weights_ref[tap].reshape(12 * channels, 2 * filters)
                sums.append(jnp.dot(block, kernel, preferred_element_type=jnp.float32))
            total = jnp.maximum(join_taps(first, sums, size_y, size_z), 0.0)
            total = jnp.maximum(total[..., :filters], total[..., filters:])
            total = jnp.max(total.reshape(pool_y, 2, size_z, filters), axis=1)
            rows_ref[: pool_y * size_z] = total.reshape(pool_y * size_z, filters)
            total = jnp.maximum(
                rows_ref[pl.ds(0, pool_y * pool_z, stride=2), :], rows_ref[pl.ds(1, pool_y * pool_z, stride=2), :]
            ).reshape(pool_y, pool_z, filters)
            inside = inside_y
            if pair == 0:
                inside = inside & low_x
            if pair == size_x // 2 - 1:
                inside = inside & high_x
            out_ref[pair] = jnp.where(inside, total, 0.0).astype(out_ref.dtype)

    return pl.pallas_call(
        body,
        in_specs=[pl.BlockSpec(memory_space=pltpu.SMEM)] + [pl.BlockSpec(memory_space=pltpu.VMEM)] * 9,
        out_specs=pl.BlockSpec(memory_space=pltpu.VMEM),
        out_shape=jax.ShapeDtypeStruct((size_x // 2, pool_y, pool_z, filters), jnp.bfloat16),
        scratch_shapes=[
            pltpu.VMEM((2, reach, own_y, size_z, channels), jnp.bfloat16),
            pltpu.VMEM((2, full_x, reach, size_z, channels), jnp.bfloat16),
            pltpu.VMEM((3, full_x, extra, channels), jnp.float32),
            pltpu.VMEM((pool_y * size_z + 16, filters), jnp.float32),
        ],
        compiler_params=pltpu.CompilerParams(vmem_limit_bytes=14 << 20),
        name="encode",
    )(place, near(own), x_in, x_out, y_in, y_out, edge, edge_in, edge_out, near(weights))


def near(array):
    return pltpu.with_memory_space_constraint(array, pltpu.VMEM)


def bring(arrays, after):
    pieces = [(i, n) for i, array in enumerate(arrays) for n in range(array.shape[0])]
    count = len(arrays)

    def body(*refs):
        hbms, outs, sems = refs[:count], refs[count + 1 : -1], refs[-1]
        copies = [pltpu.make_async_copy(hbms[i].at[n], outs[i].at[n], sems.at[k]) for k, (i, n) in enumerate(pieces)]
        for copy in copies:
            copy.start()
        for copy in copies:
            copy.wait()

    return pl.pallas_call(
        body,
        in_specs=[pl.BlockSpec(memory_space=pltpu.HBM)] * count + [pl.BlockSpec(memory_space=pl.ANY)],
        out_specs=[pl.BlockSpec(memory_space=pltpu.VMEM)] * count,
        out_shape=[pltpu.VMEM(array.shape, array.dtype) for array in arrays],
        scratch_shapes=[pltpu.SemaphoreType.DMA((len(pieces),))],
        compiler_params=pltpu.CompilerParams(vmem_limit_bytes=4 << 20),
        name="bring",
    )(*map(far, arrays), after)


def far(array):
    return pltpu.with_memory_space_constraint(array, pltpu.HBM)


def prepare(w_full, w_in, w_out):
    channels, filters = w_full.shape[3:]
    depths = [w.shape[4] for w in (w_in, w_out)]

    def body(
        full_hbm, in_hbm, out_hbm, pair_hbm, to_in_hbm, to_out_hbm, full_ref, pair_ref, in_ref, out_ref, to_in_ref, to_out_ref, sems
    ):
        first = pltpu.make_async_copy(full_hbm, full_ref, sems.at[0])
        first.start()
        jobs = []
        for order, (hbm, ref) in enumerate(((in_hbm, in_ref), (out_hbm, out_ref))):
            copies = []
            for step in range(9):
                for dy in range(3):
                    to = ref.at[step, pl.ds(64 * dy, 64)]
                    sem = sems.at[1 + 27 * order + 3 * step + dy]
                    copies.append(pltpu.make_async_copy(hbm.at[step // 3, dy, step % 3], to, sem))
                    copies[-1].start()
            jobs.append(copies)
        first.wait()
        zero = jnp.zeros((3, channels, filters), jnp.bfloat16)
        results = []
        for tap in range(3):
            for plane in range(4):
                pair_ref[tap, plane, :, :, :filters] = full_ref[plane, :, tap] if plane < 3 else zero
                pair_ref[tap, plane, :, :, filters:] = full_ref[plane - 1, :, tap] if plane > 0 else zero
            results.append(pltpu.make_async_copy(pair_ref.at[tap], pair_hbm.at[tap], sems.at[55 + tap]))
            results[-1].start()
        for order, (ref, to_ref, to_hbm) in enumerate(((in_ref, to_in_ref, to_in_hbm), (out_ref, to_out_ref, to_out_hbm))):
            for step in range(9):
                ref[step, 192:] = jnp.zeros((64, depths[order]), jnp.bfloat16)
                for copy in jobs[order][3 * step : 3 * step + 3]:
                    copy.wait()
                to_ref[step] = ref[step].T
                results.append(pltpu.make_async_copy(to_ref.at[step], to_hbm.at[step], sems.at[59 + 9 * order + step]))
                results[-1].start()
        for copy in results:
            copy.wait()

    shapes = [(3, 4, 3, channels, 2 * filters)] + [(9, depth, 256) for depth in depths]
    return pl.pallas_call(
        body,
        in_specs=[pl.BlockSpec(memory_space=pltpu.HBM)] * 3,
        out_specs=[pl.BlockSpec(memory_space=pltpu.HBM)] * 3,
        out_shape=[pltpu.HBM(shape, jnp.bfloat16) for shape in shapes],
        scratch_shapes=[pltpu.VMEM(w_full.shape, jnp.bfloat16), pltpu.VMEM(shapes[0], jnp.bfloat16)]
        + [pltpu.VMEM((9, 256, depth), jnp.bfloat16) for depth in depths]
        + [pltpu.VMEM((9, depth, 256), jnp.bfloat16) for depth in depths]
        + [pltpu.SemaphoreType.DMA((77,))],
        compiler_params=pltpu.CompilerParams(vmem_limit_bytes=20 << 20),
        name="prepare",
    )(far(w_full), far(w_in), far(w_out))


def pack_y(place, own, x_in, x_out):
    own_x, own_y, size_z, channels = own.shape
    reach = x_in.shape[0]
    full_x = own_x + 2 * reach

    def body(place_ref, own_ref, x_in_ref, x_out_ref, inner_ref, outer_ref, plane_ref, inner_edge_ref, outer_edge_ref, rows_ref):
        even_x, even_y, first = place_ref[0] % 2 == 0, place_ref[1] % 2 == 0, place_ref[2] == 0
        below = jnp.where(even_x, x_out_ref[...], x_in_ref[...])
        above = jnp.where(even_x, x_in_ref[...], x_out_ref[...])
        for start, block in ((0, below), (reach, own_ref[...]), (reach + own_x, above)):
            size = block.shape[0]
            low, high = block[:, :reach], block[:, own_y - reach :]
            inner_ref[start : start + size] = jnp.where(even_y, high, low)
            outer_ref[start : start + size] = jnp.where(even_y, low, high)
            block = block.astype(jnp.float32)
            edge = jnp.where(first, block[:, :, size_z - 1 :], block[:, :, :1])
            for x in range(size):
                for y in range(own_y):
                    rows_ref[start + x, y : y + 1] = edge[x, y]
        plane_ref[...] = rows_ref[...].astype(plane_ref.dtype)
        low, high = rows_ref[:, :reach], rows_ref[:, own_y - reach :]
        inner_edge_ref[...] = jnp.where(even_y, high, low).astype(plane_ref.dtype)
        outer_edge_ref[...] = jnp.where(even_y, low, high).astype(plane_ref.dtype)

    return pl.pallas_call(
        body,
        in_specs=[pl.BlockSpec(memory_space=pltpu.SMEM)] + [pl.BlockSpec(memory_space=pltpu.VMEM)] * 3,
        out_specs=[pl.BlockSpec(memory_space=pltpu.VMEM)] * 5,
        out_shape=[jax.ShapeDtypeStruct((full_x, reach, size_z, channels), jnp.bfloat16)] * 2
        + [jax.ShapeDtypeStruct((full_x, rows, channels), jnp.bfloat16) for rows in (own_y, reach, reach)],
        scratch_shapes=[pltpu.VMEM((full_x, own_y, channels), jnp.float32)],
        compiler_params=pltpu.CompilerParams(vmem_limit_bytes=8 << 20),
        name="pack_y",
    )(place, own, x_in, x_out)


def halves(pair_low, pair_high):
    lane = lax.broadcasted_iota(jnp.int32, pair_low.shape, pair_low.ndim - 1)
    axis = pair_low.ndim - 1
    even = jnp.where(lane < 64, pair_low, pltpu.roll(pair_high, 64, axis))
    odd = jnp.where(lane < 64, pltpu.roll(pair_low, 64, axis), pair_high)
    return even, odd


def side_by_side(even, odd):
    lane = lax.broadcasted_iota(jnp.int32, even.shape, even.ndim - 1)
    return jnp.where(lane < 64, even, pltpu.roll(odd, 64, even.ndim - 1))


def pair_planes(pad_ref, pair_ref):
    pairs = pair_ref.shape[1]
    for odd in range(2):
        for pair in range(pairs - odd):
            planes = [pad_ref[2 * pair + odd + n] for n in range(2)]
            pair_ref[odd, pair] = jnp.concatenate(planes, axis=1).astype(pair_ref.dtype)


def column_product(pair_ref, weights_ref, first, start, pairs, size_z):
    channels = pair_ref.shape[-1]
    rows = pairs * size_z * 16
    blocks = []
    for dx in range(3):
        for dz in range(3):
            block = pair_ref[dx % 2, first + dx // 2 : first + dx // 2 + pairs, pl.ds(start + dz, size_z)]
            blocks.append(block.reshape(rows, channels))
    block = jnp.concatenate(blocks, axis=1)
    total = jnp.dot(block, weights_ref[...].reshape(9 * channels, 256), preferred_element_type=jnp.float32)
    groups = pairs * size_z * 2
    low = total[:, :128].reshape(groups, 8, 128)
    mid = pltpu.roll(total[:, :128], 64, 1).reshape(groups, 8, 128)
    high = total[:, 128:].reshape(groups, 8, 128)
    total = pltpu.roll(low, 1, 1) + mid + pltpu.roll(high, 7, 1)
    return jnp.maximum(total, 0.0).reshape(pairs, size_z, 2, 8, 128)


def bottom_in(place, field, weights):
    count, own_x, lines, channels = field.shape
    devices = count // 2
    own_z = size_y = 4
    size_x, all_z, size_z = devices * own_x, 2 * own_z, own_z + 2

    def body(place_ref, field_ref, weights_ref, out_ref, pad_ref, pair_ref):
        zero = jnp.zeros((all_z + 2, 8, channels), jnp.float32)
        pad_ref[0] = zero
        pad_ref[size_x + 1] = zero
        for x in range(size_x):
            pad_ref[x + 1, 0] = zero[0]
            pad_ref[x + 1, all_z + 1] = zero[0]
        for i in range(devices):
            for half in range(2):
                for x in range(own_x):
                    block = field_ref[2 * i + half, x].astype(jnp.float32)
                    for z in range(own_z):
                        to = (1 + own_x * i + x, 1 + own_z * half + z)
                        pad_ref[*to, 0:1] = block[own_z * size_y + z : own_z * size_y + z + 1]
                        pad_ref[*to, 1 : size_y + 1] = block[size_y * z : size_y * z + size_y]
                        line = own_z * (size_y + 1) + z
                        pad_ref[*to, size_y + 1 : size_y + 2] = block[line : line + 1]
                        pad_ref[*to, size_y + 2 :] = zero[0, size_y + 2 :]
        start = 2 * place_ref[2]
        pair_planes(pad_ref, pair_ref)
        for first in range(0, size_x // 2, 2):
            total = column_product(pair_ref, weights_ref, first, start, 2, size_z)
            for pair in range(2):
                both = side_by_side(total[pair, :, 0], total[pair, :, 1])[:, 1 : size_y + 1].astype(out_ref.dtype)
                for i in range(devices):
                    out_ref[i, first + pair] = both

    return pl.pallas_call(
        body,
        in_specs=[pl.BlockSpec(memory_space=space) for space in (pltpu.SMEM, pltpu.VMEM, pltpu.VMEM)],
        out_specs=pl.BlockSpec(memory_space=pltpu.VMEM),
        out_shape=jax.ShapeDtypeStruct((devices, size_x // 2, size_z, size_y, 128), jnp.bfloat16),
        scratch_shapes=[
            pltpu.VMEM((size_x + 2, all_z + 2, 8, channels), jnp.float32),
            pltpu.VMEM((2, size_x // 2 + 1, all_z + 2, 16, channels), jnp.bfloat16),
        ],
        compiler_params=pltpu.CompilerParams(vmem_limit_bytes=16 << 20),
        name="bottom_in",
    )(place, field, near(weights))


def bottom_out(place, field, y_in, y_out, weights):
    devices, pairs, size_z, _, _ = field.shape
    size_x, channels = 2 * pairs, 64 * devices
    own_x = size_x // devices

    def body(place_ref, field_ref, y_in_ref, y_out_ref, weights_ref, out_ref, pad_ref, pair_ref, total_ref):
        even_y = place_ref[1] % 2 == 0
        low_y, high_y = place_ref[1] > 0, place_ref[1] < place_ref[4]
        zero = jnp.zeros((size_z + 2, 8, channels), jnp.float32)
        for ref in (pad_ref, total_ref):
            wide = ref.shape[-1]
            ref[0] = zero[..., :wide]
            ref[size_x + 1] = zero[..., :wide]
            for x in range(size_x):
                ref[x + 1, 0] = zero[0, :, :wide]
                ref[x + 1, size_z + 1] = zero[0, :, :wide]
        for k in range(devices // 2):
            for pair in range(pairs):
                y_first, y_last = [], []
                for i in range(2):
                    one = y_in_ref[2 * k + i, pair].astype(jnp.float32)
                    other = y_out_ref[2 * k + i, pair].astype(jnp.float32)
                    y_first.append(jnp.where(low_y, jnp.where(even_y, other, one), 0.0))
                    y_last.append(jnp.where(high_y, jnp.where(even_y, one, other), 0.0))
                own = [field_ref[2 * k + i, pair].astype(jnp.float32) for i in range(2)]
                for line, blocks in ((0, y_first), (2, own), (6, y_last)):
                    even, odd = halves(*blocks)
                    lines = slice(line, line + even.shape[1])
                    pad_ref[1 + 2 * pair, 1 : size_z + 1, lines, 128 * k : 128 * k + 128] = even
                    pad_ref[2 + 2 * pair, 1 : size_z + 1, lines, 128 * k : 128 * k + 128] = odd
        pair_planes(pad_ref, pair_ref)
        for first in range(0, pairs, 2):
            total = column_product(pair_ref, weights_ref, first, 0, 2, size_z)
            for plane in range(4):
                total_ref[1 + 2 * first + plane, 1 : size_z + 1] = total[plane // 2, :, plane % 2]
        start = 2 * place_ref[2]
        for i in range(size_x // 2 + 1):
            low, high = [total_ref[2 * i + n, pl.ds(start, size_z)] for n in range(2)]
            both = side_by_side(low, high).astype(out_ref.dtype)
            if i < devices:
                out_ref[i, 0] = both
            if i > 0:
                out_ref[i - 1, 1] = both

    return pl.pallas_call(
        body,
        in_specs=[pl.BlockSpec(memory_space=pltpu.SMEM)]
        + [pl.BlockSpec(memory_space=pltpu.VMEM)] * 4,
        out_specs=pl.BlockSpec(memory_space=pltpu.VMEM),
        out_shape=jax.ShapeDtypeStruct((devices, own_x, size_z, 8, 128), jnp.bfloat16),
        scratch_shapes=[
            pltpu.VMEM((size_x + 2, size_z + 2, 8, channels), jnp.float32),
            pltpu.VMEM((2, pairs + 1, size_z + 2, 16, channels), jnp.bfloat16),
            pltpu.VMEM((size_x + 2, size_z + 2, 8, 128), jnp.float32),
        ],
        compiler_params=pltpu.CompilerParams(vmem_limit_bytes=20 << 20),
        name="bottom_out",
    )(place, field, y_in, y_out, near(weights))


def decode_skip(place, skip, edge, weights):
    full_x, full_y, size_z, channels = skip.shape
    size_x, size_y = full_x - 2, full_y - 2
    filters = weights.shape[-1]
    deep = weights.shape[2] - channels
    rows, extra = size_x * size_y * size_z, size_x * size_y

    def body(place_ref, skip_ref, edge_ref, weights_hbm, out_hbm, *refs):
        rest_refs, (weights_ref, out_ref, sems) = refs[:4], refs[4:]
        copies = [
            pltpu.make_async_copy(weights_hbm.at[step, :, pl.ds(deep, channels)], weights_ref.at[step], sems.at[step])
            for step in range(9)
        ]
        rest = [
            pltpu.make_async_copy(weights_hbm.at[step, :, pl.ds(0, deep)], rest_refs[step], sems.at[9 + step])
            for step in range(4)
        ]
        for copy in copies + rest:
            copy.start()
        edge_plane = edge_ref[...].astype(jnp.float32)
        blocks = []
        for dx in range(3):
            for dy in range(3):
                main = skip_ref[dx : dx + size_x, dy : dy + size_y].astype(jnp.float32).reshape(rows, channels)
                side = edge_plane[dx : dx + size_x, dy : dy + size_y].reshape(extra, channels)
                blocks.append(jnp.concatenate([main, side], axis=0).astype(jnp.bfloat16))
        for copy in copies:
            copy.wait()
        block = jnp.concatenate(blocks, axis=1)
        sums = []
        for tap in range(3):
            kernel = weights_ref[:, tap].reshape(9 * channels, filters)
            sums.append(jnp.dot(block, kernel, preferred_element_type=jnp.float32))
        out_ref[...] = join_taps(place_ref[2] == 0, sums, extra, size_z)
        rest.append(pltpu.make_async_copy(out_ref, out_hbm, sems.at[13]))
        rest[-1].start()
        for copy in rest:
            copy.wait()

    return pl.pallas_call(
        body,
        in_specs=[pl.BlockSpec(memory_space=pltpu.SMEM)]
        + [pl.BlockSpec(memory_space=pltpu.VMEM)] * 2
        + [pl.BlockSpec(memory_space=pltpu.HBM)],
        out_specs=[pl.BlockSpec(memory_space=pltpu.HBM)] + [pl.BlockSpec(memory_space=pltpu.VMEM)] * 4,
        out_shape=[
            pltpu.HBM((extra, size_z, filters), jnp.float32),
        ]
        + [pltpu.VMEM((3, deep, filters), jnp.bfloat16)] * 4,
        scratch_shapes=[
            pltpu.VMEM((9, 3, channels, filters), jnp.bfloat16),
            pltpu.VMEM((extra, size_z, filters), jnp.float32),
            pltpu.SemaphoreType.DMA((14,)),
        ],
        compiler_params=pltpu.CompilerParams(vmem_limit_bytes=14 << 20),
        name="decode_skip",
    )(place, skip, edge, far(weights))


def decode(place, bottom, skip_part, first_weights, weights, shape):
    devices, pairs, coarse_z, _, _ = bottom.shape
    size_x, size_y, size_z = shape
    full_x, full_y = size_x + 2, size_y + 2
    channels = 64 * devices
    filters = weights.shape[-1]
    rows, extra = size_x * size_y * size_z, size_x * size_y

    def body(place_ref, bottom_ref, skip_hbm, *refs):
        near_refs, (weights_hbm, out_ref, main_ref, side_ref, sums_ref, skip_ref, weights_ref, sems) = refs[:4], refs[4:]
        copies = [
            pltpu.make_async_copy(weights_hbm.at[4 + step, :, pl.ds(0, channels)], weights_ref.at[step], sems.at[step])
            for step in range(5)
        ]
        copies.append(pltpu.make_async_copy(skip_hbm, skip_ref, sems.at[5]))
        for copy in copies:
            copy.start()
        first = place_ref[2] == 0
        planes = [[] for _ in range(2 * pairs)]
        for k in range(devices // 2):
            for pair in range(pairs):
                low, high = [bottom_ref[2 * k + i, pair].astype(jnp.float32) for i in range(2)]
                even, odd = halves(low, high)
                planes[2 * pair].append(even.reshape(coarse_z * 8, 128))
                planes[2 * pair + 1].append(odd.reshape(coarse_z * 8, 128))

        def choice(y, z, source):
            line = (y + 1) // 2 + 1
            inside = ((line > 1) | (place_ref[1] > 0)) & ((line < coarse_z) | (place_ref[1] < place_ref[4]))
            return jnp.where((source == z * 8 + line) & inside, 1.0, 0.0).astype(jnp.bfloat16)

        shape = (full_y * size_z, coarse_z * 8)
        row = lax.broadcasted_iota(jnp.int32, shape, 0)
        spread = choice(row // size_z, row % size_z // 2 + 1, lax.broadcasted_iota(jnp.int32, shape, 1))
        shape = (16, coarse_z * 8)
        row = lax.broadcasted_iota(jnp.int32, shape, 0)
        other = jnp.where(first, coarse_z - 1, 0)
        spread_edge = choice(row, other, lax.broadcasted_iota(jnp.int32, shape, 1))
        for plane in range(2 * pairs):
            coarse = jnp.concatenate(planes[plane], axis=1).astype(jnp.bfloat16)
            fine = jnp.dot(spread, coarse, preferred_element_type=jnp.float32)
            fine_edge = jnp.dot(spread_edge, coarse, preferred_element_type=jnp.float32)
            for x in range(full_x):
                if (x + 1) // 2 != plane:
                    continue
                for dy in range(3):
                    main_ref[dy, x] = fine[8 * dy : 8 * dy + size_y * size_z].astype(jnp.bfloat16)
                    side_ref[dy, x] = fine_edge[dy : dy + size_y]
        for step in range(9):
            dx, dy = step // 3, step % 3
            main = main_ref[dy, dx : dx + size_x].reshape(rows, channels)
            side = side_ref[dy, dx : dx + size_x].reshape(extra, channels).astype(jnp.bfloat16)
            block = jnp.concatenate([main, side], axis=0)
            if step >= 4:
                copies[step - 4].wait()
            for tap in range(3):
                kernel = near_refs[step][tap] if step < 4 else weights_ref[step - 4, tap]
                product = jnp.dot(block, kernel, preferred_element_type=jnp.float32)
                if step == 0:
                    sums_ref[tap] = product
                else:
                    sums_ref[tap] += product
        copies[-1].wait()
        total = join_taps(first, [sums_ref[tap] for tap in range(3)], extra, size_z) + skip_ref[...]
        out_ref[...] = total.reshape(size_x, size_y, size_z, filters).astype(out_ref.dtype)

    return pl.pallas_call(
        body,
        in_specs=[pl.BlockSpec(memory_space=pltpu.SMEM)]
        + [pl.BlockSpec(memory_space=space) for space in (pltpu.VMEM, pltpu.HBM)]
        + [pl.BlockSpec(memory_space=pltpu.VMEM)] * 4
        + [pl.BlockSpec(memory_space=pltpu.HBM)],
        out_specs=pl.BlockSpec(memory_space=pltpu.VMEM),
        out_shape=jax.ShapeDtypeStruct((size_x, size_y, size_z, filters), jnp.bfloat16),
        scratch_shapes=[
            pltpu.VMEM((3, full_x, size_y * size_z, channels), jnp.bfloat16),
            pltpu.VMEM((3, full_x, size_y, channels), jnp.float32),
            pltpu.VMEM((3, rows + extra, filters), jnp.float32),
            pltpu.VMEM((extra, size_z, filters), jnp.float32),
            pltpu.VMEM((5, 3, channels, filters), jnp.bfloat16),
            pltpu.SemaphoreType.DMA((6,)),
        ],
        compiler_params=pltpu.CompilerParams(vmem_limit_bytes=20 << 20),
        name="decode",
    )(place, bottom, far(skip_part), *map(near, first_weights), far(weights))


def solution(mesh):
    gx, gy, gz = mesh.shape["gx"], mesh.shape["gy"], mesh.shape["gz"]

    def local(volume, w_full, w_half, w_bottom_in, w_bottom_out, w_up):
        place_z = lax.axis_index("gz")
        place = jnp.stack([lax.axis_index("gx"), lax.axis_index("gy"), place_z, jnp.int32(gx - 1), jnp.int32(gy - 1)])
        swap = [(0, 1), (1, 0)]

        def edge_of(plane_low, plane_high):
            return lax.ppermute(jnp.where(place_z == 0, plane_high, plane_low), "gz", swap)

        x_in, x_out = swaps(volume[:3], volume[-3:], "gx", gx)
        turned = [w.transpose(0, 1, 2, 4, 3) for w in (w_bottom_in, w_bottom_out)]
        (w_pair, w_in, w_out), x_in, x_out = lax.optimization_barrier((prepare(w_full, *turned), x_in, x_out))
        y_inner, y_outer, plane, edge_inner, edge_outer = pack_y(place, volume, x_in, x_out)
        y_in, y_out = send(y_inner, y_outer, "gy", gy)
        edge = lax.ppermute(plane, "gz", swap)
        edge_in, edge_out = send(edge_inner, edge_outer, ("gy", "gz"), gy)
        own, w_pair = bring([volume, w_pair], plane)
        pooled = encode(place, own, x_in, x_out, y_in, y_out, edge, edge_in, edge_out, w_pair)

        edge = edge_of(pooled[:, :, 0], pooled[:, :, -1])
        skip, coarse = half_level(place, pooled, edge, w_half.reshape(9, 3, w_half.shape[3], w_half.shape[4]))
        lines = coarse.reshape(coarse.shape[0], 4, 4, coarse.shape[2])
        below, above = halo(lines, "gy", gy, 2, 1)
        column = jnp.concatenate([coarse, below[:, :, 0], above[:, :, 0]], axis=1)
        column = jnp.broadcast_to(column[None], (gx * gz,) + column.shape)
        (w_in,) = bring([w_in], column)
        column = lax.all_to_all(column, ("gx", "gz"), 0, 0)
        first = bottom_in(place, column, w_in)
        (w_out,) = bring([w_out], first)
        first = lax.all_to_all(first, "gx", 0, 0)
        around = extend(skip, "gx", gx, 0, 1)
        around = extend(around, "gy", gy, 1, 1)
        side = edge_of(around[:, :, 0], around[:, :, -1])
        first, around, side = lax.optimization_barrier((first, around, side))
        y_in, y_out = swaps(first[:, :, :, :2], first[:, :, :, -2:], "gy", gy)
        second = bottom_out(place, first, y_in, y_out, w_out)
        second = lax.all_to_all(second, "gx", 0, 0)
        w_up = w_up.reshape(9, 3, w_up.shape[3], w_up.shape[4])
        skip_part, *w_near = decode_skip(place, around, side, w_up)
        return decode(place, second, skip_part, w_near, w_up, skip.shape[:3])

    space = P("gx", "gy", "gz", None)
    filters = P(None, None, None, None, "gx")
    return jax.shard_map(
        local,
        mesh=mesh,
        in_specs=(space, P(), P(), filters, filters, P()),
        out_specs=space,
        check_vma=False,
    )
```
